128 devices in a mesh: gx: 32 (over z, x, y_hi), gy: 4 (over y_lo, core).
Axes of the slice: x: 4, y: 4 (y_hi: 2, y_lo: 2; y = y_hi * 2 + y_lo), z: 4, core: 2. Of those that a mesh axis runs over, the one named last changes fastest.
Arguments:
- rhs_field: float32 [2, 8, 256, 1024], P(None, None, 'gx', 'gy'), may hold values from -6 to 6
- permittivity: float32 [8, 256, 1024], P(None, 'gx', 'gy'), may hold values from 1 to 4
- surf_dist: float32 [16384, 128], P(('gx', 'gy')), may hold values from 0.2 to 1
- surf_normal: float32 [3, 16384, 128], P(None, ('gx', 'gy')), may hold values from -4 to 4
- surf_inc: float32 [2, 16384, 128], P(None, ('gx', 'gy')), may hold values from -6 to 6
- surf_cell: int32 [16384, 128], P(('gx', 'gy')), may hold values from 0 to 16383
- surf_mask: int32 [16384, 128], P(('gx', 'gy')), may hold values 0 or 1
- surf_owner: int32 [16384, 1], P(('gx', 'gy')), may hold values from 0 to 127; in each aligned block of 128 rows (0 to 127, 128 to 255, ...) at most 2 rows name the same one
Outputs:
- solution: float32 [2, 8, 256, 1024], P(None, None, 'gx', 'gy')
- residual: float32 [2, 8, 256, 1024], P(None, None, 'gx', 'gy')
The draws below stay inside these ranges and needn't reach their ends.
Inputs may be any that keep to these rules, and one draw needn't show every extreme that they name: `surf_owner`: within the 128 rows of one device no owner is named more than 2 times, a bound that some block reaches.
All inputs are finite; a program needn't handle non-finite values. No bound on the sum of `surf_mask` on one device may be relied on, other than what follows from the above.
Results may differ from the reference program's by a relative error of at most 0.00002.
Values sent between devices are 32-bit elements; how exact they have to be, the bound alone decides.
No kernel may reach another device: no remote copies, remote signals or barrier semaphores. Data moves between devices by JAX's collectives and lax.ppermute only.
A program may use at most 128 MiB of HBM per device.

```python
import math
import jax
import jax.numpy as jnp
import numpy as np

NZ = 8
CX = 8
CY = 256
PTS = 128
CAP = 2
ITERS = 2
SWEEPS = 2
SB = 128
NB = 16384
NX = 256
NY = 1024
N_GX = 32
N_GY = 4


def with_ends(drawn, own_key, low, top_value):
    longest = drawn.shape.index(max(drawn.shape))
    spots = []
    for shift in (0, 1):
        where = [jax.random.randint(jax.random.fold_in(own_key, axis), (), 0, length) for axis, length in enumerate(drawn.shape)]
        where[longest] = (where[longest] + shift) % drawn.shape[longest]
        spots.append(tuple(where))
    return drawn.at[spots[0]].set(low).at[spots[1]].set(top_value)


def block_scale(rng, dims, shards, low, high):
    factor_of, own = 1.0, jax.random.fold_in(rng, 6)
    for dim, parts in shards:
        heights = jnp.exp(jax.random.uniform(jax.random.fold_in(own, dim), (parts,), jnp.float32, low / len(shards), high / len(shards)))
        factor_of = factor_of * jnp.repeat(heights, dims[dim] // parts).reshape([-1 if axis == dim else 1 for axis in range(len(dims))])
    return factor_of


def assign_block(own_key, own, number, rows, number_of, top, reach, lean):
    ranking = jax.random.permutation(own_key, number_of)
    packed, ordinary = portions_of(number_of, rows * top, reach, lean, True), portions_of(number_of, rows * top, reach, lean, False)
    places = jnp.arange(number_of)

    def named(sizes, turn):
        used = int((sizes > 0).sum())
        fixed = max(1, used // 4)
        moved = fixed + (places - fixed + turn * (used - fixed)) % max(1, number_of - fixed)
        return jnp.zeros((number_of,), jnp.int32).at[ranking[jnp.where(places < fixed, places, moved)]].set(jnp.asarray(sizes, jnp.int32))

    sizes = jnp.where(number % 4 == 0, named(packed, number // 4), named(ordinary, number - number // 4 - 1))
    mixed = jax.random.permutation(jax.random.fold_in(own, 3), number_of)
    donor, sink = mixed[0:number_of // 2 * 2:2], mixed[1:number_of // 2 * 2:2]
    slack = jnp.minimum(sizes[donor] - 1, reach - sizes[sink]) // 2
    slack = jnp.where((donor == ranking[0]) | (sink == ranking[0]) | (sizes[sink] == 0), 0, jnp.maximum(slack, 0))
    moved = jax.random.randint(jax.random.fold_in(own, 4), (number_of // 2,), 0, 1 << 20) % (slack + 1)
    sizes = sizes.at[donor].add(-moved).at[sink].add(moved)
    items = jnp.searchsorted(jnp.cumsum(sizes), jnp.arange(rows * top), side="right").astype(jnp.int32)
    listing = items.reshape(top, rows).T
    listing = listing[jax.random.permutation(jax.random.fold_in(own, 1), rows)]
    turn = jax.random.randint(jax.random.fold_in(own, 2), (rows, 1), 0, top)
    return jnp.take_along_axis(listing, (jnp.arange(top)[None, :] + turn) % top, axis=1)


def portions_of(number_of, total, limit, lean, full):
    weights = [(1 << 20) // math.isqrt(rank ** lean) + 1 for rank in range(1, number_of + 1)]
    largest = limit if full else min(limit, max(-(-total // number_of), total * weights[0] // sum(weights)))
    least = 1 if total - largest >= number_of - 1 else 0
    counts, surplus = [largest] + [least] * (number_of - 1), total - largest - least * (number_of - 1)
    while surplus > 0:
        free = [i for i in range(1, number_of) if counts[i] < largest] or [i for i in range(1, number_of) if counts[i] < limit]
        pool, remaining = sum([weights[i] for i in free]), surplus
        for i in free:
            extra = min(limit - counts[i], max(1, remaining * weights[i] // pool), surplus)
            counts[i] = counts[i] + extra
            surplus = surplus - extra
    return np.array(counts)


def scatter_about(own_key, dims, scale, reach, split=(), dtype=jnp.bfloat16):
    gain = block_scale(own_key, dims, split, -0.22, 0.18) if split else 1.0
    result = jax.random.normal(own_key, dims, jnp.float32) * scale * gain
    return jnp.minimum(jnp.maximum(result, -reach), reach).astype(dtype)


def setup_inputs(seed: int = 0) -> dict:
    streams_of = jax.random.split(jax.random.key(seed), 9)
    rhs_field = scatter_about(streams_of[0], (2, NZ, NX, NY), 1.0, 6.0, ((2, 32), (3, 4)), jnp.float32)
    permittivity = jnp.clip(jnp.exp(math.log(4.0) - 1.3862944 * jax.random.uniform(streams_of[1], (NZ, NX, NY), jnp.float32) ** block_scale(streams_of[1], (NZ, NX, NY), ((1, 32), (2, 4)), -0.2, 0.2)), 1.0, 4.0)
    surf_dist = jnp.clip(0.2 + 0.8 * jax.random.uniform(streams_of[2], (NB, PTS), jnp.float32) ** block_scale(streams_of[2], (NB, PTS), ((0, 128),), -0.2, 0.2), 0.2, 1.0)
    surf_normal = scatter_about(streams_of[3], (3, NB, PTS), 1.0, 4.0, ((1, 128),), jnp.float32)
    surf_inc = scatter_about(streams_of[4], (2, NB, PTS), 1.0, 6.0, ((1, 128),), jnp.float32)
    surf_cell = with_ends(jax.random.randint(streams_of[5], (NB, PTS), 0, NZ * CX * CY), jax.random.fold_in(streams_of[5], 1), 0, (NZ * CX * CY) - 1).astype(jnp.int32)
    surf_mask = with_ends((jax.random.randint(streams_of[6], (NB, PTS), 0, 4) < 3).astype(jnp.int32), jax.random.fold_in(streams_of[6], 1), 0, 1)
    surf_owner_keys = jax.random.split(jax.random.fold_in(streams_of[7], 1), NB // SB)
    surf_owner_turns = jax.random.permutation(jax.random.fold_in(streams_of[7], 3), NB // SB)
    surf_owner = jax.vmap(lambda own, number: assign_block(jax.random.fold_in(streams_of[7], 2), own, number, SB, N_GX * N_GY, 1, CAP, 2))(surf_owner_keys, surf_owner_turns).reshape((NB, 1))
    return dict(rhs_field=rhs_field, permittivity=permittivity, surf_dist=surf_dist, surf_normal=surf_normal, surf_inc=surf_inc, surf_cell=surf_cell, surf_mask=surf_mask, surf_owner=surf_owner)


K_SQUARED = 0.25
BETA = 0.5
OMEGA = 0.8
TAU = 1.0


def apply_helm(padded, perm):
    center = padded[:, 1:-1, 1:-1, 1:-1]
    beside = padded[:, 2:, 1:-1, 1:-1] + padded[:, :-2, 1:-1, 1:-1]
    beside = beside + padded[:, 1:-1, 2:, 1:-1] + padded[:, 1:-1, :-2, 1:-1]
    beside = beside + padded[:, 1:-1, 1:-1, 2:] + padded[:, 1:-1, 1:-1, :-2]
    return (6.0 - K_SQUARED * perm)[None] * center - beside


def pad_all(field):
    return jnp.pad(field, ((0, 0), (1, 1), (1, 1), (1, 1)))


def reference(rhs_field, permittivity, surf_dist, surf_normal, surf_inc, surf_cell, surf_mask, surf_owner):
    owner_ids = jnp.broadcast_to(surf_owner, surf_cell.shape).reshape(-1)
    cells = surf_cell.reshape(-1)
    per_plane = CX * CY
    plane_idx = cells // per_plane
    remain = cells % per_plane
    row_idx = remain // CY + (owner_ids // N_GY) * CX
    col_idx = remain % CY + (owner_ids % N_GY) * CY
    stride_x = NY + 2
    stride_z = (NX + 2) * (NY + 2)
    pad_index = ((plane_idx + 1) * (NX + 2) + row_idx + 1) * stride_x + col_idx + 1
    grid_index = (plane_idx * NX + row_idx) * NY + col_idx
    weight = TAU * surf_mask.reshape(-1).astype(jnp.float32)
    dist = surf_dist.reshape(-1)
    normal = surf_normal.reshape(3, -1)
    incident = surf_inc.reshape(2, -1)

    diag_real = 6.0 - K_SQUARED * permittivity
    diag_imag = BETA * K_SQUARED * permittivity
    denom = diag_real * diag_real + diag_imag * diag_imag
    inv_real = diag_real / denom
    inv_imag = -diag_imag / denom

    def precond(vec):
        return jnp.stack([vec[0] * inv_real - vec[1] * inv_imag, vec[0] * inv_imag + vec[1] * inv_real])

    solution = jnp.zeros_like(rhs_field)
    residual = rhs_field
    for outer_no in range(ITERS):
        padded = pad_all(solution)
        image = apply_helm(padded, permittivity)
        flat_field = padded.reshape(2, -1)
        grad_dot = normal[0] * (flat_field[:, pad_index + stride_z] - flat_field[:, pad_index - stride_z])
        grad_dot = grad_dot + normal[1] * (flat_field[:, pad_index + stride_x] - flat_field[:, pad_index - stride_x])
        grad_dot = grad_dot + normal[2] * (flat_field[:, pad_index + 1] - flat_field[:, pad_index - 1])
        penalty = weight * (flat_field[:, pad_index] + dist * grad_dot * 0.5 + incident)
        surface = jnp.zeros((2, NZ * NX * NY), jnp.float32).at[:, grid_index].add(penalty)
        residual = rhs_field - image - surface.reshape(rhs_field.shape)
        update = OMEGA * precond(residual)
        for sweep_no in range(SWEEPS - 1):
            image_z = apply_helm(pad_all(update), permittivity)
            shifted = jnp.stack([image_z[0] - diag_imag * update[1], image_z[1] + diag_imag * update[0]])
            update = update + OMEGA * precond(residual - shifted)
        solution = solution + update
    return solution, residual
```

```python
import functools

import jax
import jax.numpy as jnp
from jax import lax
from jax.experimental import pallas as pl
from jax.experimental.pallas import tpu as pltpu
from jax.sharding import PartitionSpec as P

CAP = 2
K_SQUARED = 0.25
BETA = 0.5
OMEGA = 0.8
TAU = 1.0

CHANNELS = 6
PARTS = 11
GROUP = 8

f32 = jnp.float32
bf16 = jnp.bfloat16


def pack_kernel(owner_ref, dist_ref, normal_ref, inc_ref, cell_ref, mask_ref, out_ref, count_ref, coef_ref):
    blocks = dist_ref.shape[0]
    devices = out_ref.shape[0] // (CAP * CHANNELS)
    out_ref[...] = jnp.full(out_ref.shape, -1.0, f32)
    half = 0.5 * TAU * dist_ref[...]
    for k in range(3):
        coef_ref[k] = half * normal_ref[k]
    for k in range(2):
        coef_ref[3 + k] = TAU * inc_ref[k]
    cells = jnp.where(mask_ref[...] > 0, cell_ref[...], 1 << 14)
    coef_ref[5] = cells.astype(f32)

    def clear(i, carry):
        count_ref[i] = 0
        return carry

    lax.fori_loop(0, devices, clear, 0, unroll=8)

    def place(b, carry):
        owner = owner_ref[b]
        rank = count_ref[owner]
        count_ref[owner] = rank + 1
        base = (owner * CAP + rank) * CHANNELS
        for c in range(CHANNELS):
            out_ref[pl.ds(base + c, 1), :] = coef_ref[c, pl.ds(b, 1), :]
        return carry

    lax.fori_loop(0, blocks, place, 0, unroll=4)


def shift_rows(x, amount):
    return pltpu.roll(x, amount % x.shape[1], axis=1)


def scatter_kernel(recv_ref, rhs_ref, perm_ref, r1_ref, wn_ref, up_ref, down_ref, first_ref, second_ref, a_ref, b_ref, acc_ref):
    slots = recv_ref.shape[0] // CHANNELS
    planes = rhs_ref.shape[1]
    hi_n = planes * 8
    lo_n = rhs_ref.shape[3]
    data = recv_ref[...]
    row = lax.broadcasted_iota(jnp.int32, data.shape, 0)
    is_cell = lax.rem(row, CHANNELS) == CHANNELS - 1
    cell = data.astype(jnp.int32)
    lead = data.astype(bf16).astype(f32)
    first_ref[...] = jnp.where(is_cell, (cell >> 8).astype(f32), lead)
    second_ref[...] = jnp.where(is_cell, (cell & 255).astype(f32), data - lead)
    acc_ref[...] = jnp.zeros(acc_ref.shape, f32)
    hi_iota = lax.broadcasted_iota(jnp.int32, (hi_n, 128), 0).astype(f32).astype(bf16)
    lo_iota = lax.broadcasted_iota(jnp.int32, (lo_n, 128), 0).astype(f32).astype(bf16)
    one = jnp.ones((), bf16)
    zero = jnp.zeros((), bf16)

    def spread(ref, index, n):
        tile = jnp.broadcast_to(ref[pl.ds(index, 1), :], (16, 128)).astype(bf16)
        return jnp.concatenate([tile] * (n // 16), axis=0)

    def step(g, carry):
        for j in range(GROUP):
            base = (g * GROUP + j) * CHANNELS
            lanes = pl.ds(j * 128, 128)
            hot = hi_iota == spread(first_ref, base + 5, hi_n)
            for c in range(5):
                a_ref[pl.ds(2 * c * hi_n, hi_n), lanes] = jnp.where(hot, spread(first_ref, base + c, hi_n), zero)
                a_ref[pl.ds((2 * c + 1) * hi_n, hi_n), lanes] = jnp.where(hot, spread(second_ref, base + c, hi_n), zero)
            a_ref[pl.ds(10 * hi_n, hi_n), lanes] = jnp.where(hot, one, zero)
            b_ref[:, lanes] = jnp.where(lo_iota == spread(second_ref, base + 5, lo_n), one, zero)
        acc_ref[...] += lax.dot_general(
            a_ref[...], b_ref[...], (((1,), (1,)), ((), ())), preferred_element_type=f32
        )
        return carry

    lax.fori_loop(0, slots // GROUP, step, 0)

    def channel(c):
        if c == 5:
            total = acc_ref[pl.ds(10 * hi_n, hi_n), :]
        else:
            total = acc_ref[pl.ds(2 * c * hi_n, hi_n), :] + acc_ref[pl.ds((2 * c + 1) * hi_n, hi_n), :]
        return total.reshape(planes, 8, lo_n)

    re = rhs_ref[0] - channel(3)
    im = rhs_ref[1] - channel(4)
    wn = [TAU * channel(5), channel(0), channel(1), channel(2)]
    r1_ref[0] = re
    r1_ref[1] = im
    for k in range(4):
        wn_ref[k] = wn[k]
    perm = perm_ref[...]
    sub = lax.broadcasted_iota(jnp.int32, (planes, 8, lo_n), 1)
    t = jnp.where(sub < 3, re, shift_rows(im, 3))
    t = jnp.where(sub < 6, t, jnp.where(sub == 6, shift_rows(wn[0], 6), shift_rows(wn[1], 7)))
    up_ref[:, 0:8, :] = t
    t = jnp.where(sub < 3, perm, jnp.where(sub == 3, shift_rows(wn[2], 3), shift_rows(wn[3], 4)))
    up_ref[:, 8:16, :] = t
    t = jnp.where(sub >= 5, re, shift_rows(im, -3))
    t = jnp.where(sub >= 2, t, jnp.where(sub == 1, shift_rows(wn[0], -6), shift_rows(wn[1], -7)))
    down_ref[:, 0:8, :] = t
    t = jnp.where(sub >= 5, perm, jnp.where(sub == 4, shift_rows(wn[2], -3), shift_rows(wn[3], -4)))
    down_ref[:, 8:16, :] = t


ROW_PLACE = ((0, 0, 3), (0, 3, 3), (1, 0, 3), (0, 6, 1), (0, 7, 1), (1, 3, 1), (1, 4, 1))
COL_PLACE = ((0, 3), (3, 3), (6, 3), (9, 1), (10, 1), (11, 1), (12, 1))


def halo_rows(c, above_ref, below_ref, lanes):
    tile, offset, width = ROW_PLACE[c]
    rows = pl.ds(tile * 8, 8)
    below = shift_rows(below_ref[:, rows, lanes], -offset)
    above = shift_rows(above_ref[:, rows, lanes], offset)
    sub = lax.broadcasted_iota(jnp.int32, below.shape, 1)
    return jnp.where(sub < width, below, jnp.where(sub >= 8 - width, above, 0.0))


def own_channel(c, r1_ref, perm_ref, wn_ref, lanes):
    if c < 2:
        return r1_ref[c, :, :, lanes]
    if c == 2:
        return perm_ref[:, :, lanes]
    return wn_ref[c - 3, :, :, lanes]


def strip_kernel(r1_ref, perm_ref, wn_ref, above_ref, below_ref, left_ref, right_ref):
    lo_n = perm_ref.shape[2]
    planes = perm_ref.shape[0]
    lane = lax.broadcasted_iota(jnp.int32, (planes, 16, 128), 2)
    for out_ref, start, sign in ((left_ref, 0, 1), (right_ref, lo_n - 128, -1)):
        lanes = pl.ds(start, 128)
        place = lane if sign > 0 else 127 - lane
        strip = jnp.zeros((planes, 16, 128), f32)
        for c in range(7):
            full = jnp.concatenate(
                [own_channel(c, r1_ref, perm_ref, wn_ref, lanes), halo_rows(c, above_ref, below_ref, lanes)], axis=1
            )
            offset, width = COL_PLACE[c]
            moved = pltpu.roll(full, (sign * offset) % 128, axis=2)
            strip = jnp.where((place >= offset) & (place < offset + width), moved, strip)
        out_ref[...] = strip


def final_kernel(r1_ref, perm_ref, wn_ref, above_ref, below_ref, fleft_ref, fright_ref, sol_ref, res_ref):
    lo_n = perm_ref.shape[2]
    planes = perm_ref.shape[0]
    wide = lo_n + 128
    lane = lax.broadcasted_iota(jnp.int32, (planes, 16, 128), 2)
    everything = pl.ds(0, lo_n)

    def extended(c):
        body = jnp.concatenate(
            [own_channel(c, r1_ref, perm_ref, wn_ref, everything), halo_rows(c, above_ref, below_ref, everything)], axis=1
        )
        offset, width = COL_PLACE[c]
        right = pltpu.roll(fright_ref[...], (-offset) % 128, axis=2)
        left = pltpu.roll(fleft_ref[...], offset, axis=2)
        side = jnp.where(lane < width, right, jnp.where(lane >= 128 - width, left, 0.0))
        return jnp.concatenate([body, side], axis=2)

    re, im, perm, w, nz, nx, ny = [extended(c) for c in range(7)]
    diag = 6.0 - K_SQUARED * perm
    shift = BETA * K_SQUARED * perm
    denom = diag * diag + shift * shift
    inside = perm > 0.5
    inv_re = jnp.where(inside, OMEGA * diag / denom, 0.0)
    inv_im = jnp.where(inside, -OMEGA * shift / denom, 0.0)

    def damp(a, b):
        return a * inv_re - b * inv_im, a * inv_im + b * inv_re

    def sides(v):
        nothing = jnp.zeros((1,) + v.shape[1:], f32)
        after = jnp.concatenate([v[1:], nothing], axis=0)
        before = jnp.concatenate([nothing, v[:-1]], axis=0)
        return (
            (after, before),
            (pltpu.roll(v, 15, axis=1), pltpu.roll(v, 1, axis=1)),
            (pltpu.roll(v, wide - 1, axis=2), pltpu.roll(v, 1, axis=2)),
        )

    def helm(v, pairs):
        total = pairs[0][0] + pairs[0][1]
        for a, b in pairs[1:]:
            total = total + a + b
        return diag * v - total

    def swept(a, b):
        za, zb = damp(a, b)
        ma = helm(za, sides(za)) - shift * zb
        mb = helm(zb, sides(zb)) + shift * za
        da, db = damp(a - ma, b - mb)
        return za + da, zb + db

    def surface(v, pairs):
        (a, b), (c, d), (e, f) = pairs
        return w * v + nz * (a - b) + nx * (c - d) + ny * (e - f)

    def remaining(r, v):
        pairs = sides(v)
        return r - helm(v, pairs) - surface(v, pairs)

    sa, sb = swept(re, im)
    ra, rb = remaining(re, sa), remaining(im, sb)
    ua, ub = swept(ra, rb)
    res_ref[0] = ra[:, 0:8, 0:lo_n]
    res_ref[1] = rb[:, 0:8, 0:lo_n]
    sol_ref[0] = (sa + ua)[:, 0:8, 0:lo_n]
    sol_ref[1] = (sb + ub)[:, 0:8, 0:lo_n]


def in_vmem(n):
    return [pl.BlockSpec(memory_space=pltpu.VMEM)] * n


def shape(*dims):
    return jax.ShapeDtypeStruct(dims, f32)


def per_device(rhs_field, permittivity, surf_dist, surf_normal, surf_inc, surf_cell, surf_mask, surf_owner):
    planes, rows, cols = permittivity.shape
    blocks, points = surf_cell.shape
    gx, gy = lax.axis_size("gx"), lax.axis_size("gy")
    devices = gx * gy
    slots = devices * CAP
    params = pltpu.CompilerParams(vmem_limit_bytes=48 << 20)
    send = pl.pallas_call(
        pack_kernel,
        out_shape=shape(slots * CHANNELS, points),
        in_specs=[pl.BlockSpec(memory_space=pltpu.SMEM)] + in_vmem(5),
        out_specs=pl.BlockSpec(memory_space=pltpu.VMEM),
        scratch_shapes=[pltpu.SMEM((devices,), jnp.int32), pltpu.VMEM((CHANNELS, blocks, points), f32)],
        compiler_params=params,
        name="pack",
    )(surf_owner[:, 0], surf_dist, surf_normal, surf_inc, surf_cell, surf_mask)
    recv = lax.all_to_all(send.reshape(-1), ("gx", "gy"), split_axis=0, concat_axis=0, tiled=True)
    recv = recv.reshape(slots * CHANNELS, points)
    field = shape(2, planes, rows, cols)
    r1, wn, up, down = pl.pallas_call(
        scatter_kernel,
        out_shape=(field, shape(4, planes, rows, cols), shape(planes, 16, cols), shape(planes, 16, cols)),
        in_specs=in_vmem(3),
        out_specs=tuple(in_vmem(4)),
        scratch_shapes=[
            pltpu.VMEM((slots * CHANNELS, points), f32),
            pltpu.VMEM((slots * CHANNELS, points), f32),
            pltpu.VMEM((PARTS * planes * rows, GROUP * points), bf16),
            pltpu.VMEM((cols, GROUP * points), bf16),
            pltpu.VMEM((PARTS * planes * rows, cols), f32),
        ],
        compiler_params=params,
        name="scatter",
    )(recv, rhs_field, permittivity)
    later = [(i, i + 1) for i in range(gx - 1)]
    above = lax.ppermute(down, "gx", later)
    below = lax.ppermute(up, "gx", [(j, i) for i, j in later])
    strip = shape(planes, 16, 128)
    to_left, to_right = pl.pallas_call(
        strip_kernel,
        out_shape=(strip, strip),
        in_specs=in_vmem(5),
        out_specs=tuple(in_vmem(2)),
        compiler_params=params,
        name="strips",
    )(r1, permittivity, wn, above, below)
    later = [(i, i + 1) for i in range(gy - 1)]
    from_left = lax.ppermute(to_right, "gy", later)
    from_right = lax.ppermute(to_left, "gy", [(j, i) for i, j in later])
    return pl.pallas_call(
        final_kernel,
        out_shape=(field, field),
        in_specs=in_vmem(7),
        out_specs=tuple(in_vmem(2)),
        compiler_params=params,
        name="final",
    )(r1, permittivity, wn, above, below, from_left, from_right)


def solution(mesh):
    split = ("gx", "gy")
    placed = (
        P(None, None, "gx", "gy"),
        P(None, "gx", "gy"),
        P(split, None),
        P(None, split, None),
        P(None, split, None),
        P(split, None),
        P(split, None),
        P(split, None),
    )
    return jax.shard_map(
        per_device,
        mesh=mesh,
        in_specs=placed,
        out_specs=(P(None, None, "gx", "gy"), P(None, None, "gx", "gy")),
        check_vma=False,
    )
```

```python
import functools

import jax
import jax.numpy as jnp
from jax import lax
from jax.experimental import pallas as pl
from jax.experimental.pallas import tpu as pltpu
from jax.sharding import PartitionSpec as P

CAP = 2
K_SQUARED = 0.25
BETA = 0.5
OMEGA = 0.8
TAU = 1.0

CHANNELS = 6
PARTS = 11
GROUP = 32

f32 = jnp.float32
bf16 = jnp.bfloat16


def pack_kernel(
    owner_hbm, dist_hbm, normal_hbm, inc_hbm, cell_hbm, mask_hbm, out_ref,
    owner_ref, base_ref, count_ref, dist_ref, coef_ref, cell_ref, mask_ref, sems,
):
    blocks = dist_ref.shape[0]
    devices = count_ref.shape[0]
    copies = [
        pltpu.make_async_copy(owner_hbm, owner_ref, sems.at[0]),
        pltpu.make_async_copy(dist_hbm, dist_ref, sems.at[1]),
        pltpu.make_async_copy(normal_hbm, coef_ref.at[pl.ds(0, 3)], sems.at[2]),
        pltpu.make_async_copy(inc_hbm, coef_ref.at[pl.ds(3, 2)], sems.at[3]),
        pltpu.make_async_copy(cell_hbm, cell_ref, sems.at[4]),
        pltpu.make_async_copy(mask_hbm, mask_ref, sems.at[5]),
    ]
    for copy in copies:
        copy.start()
    out_ref[...] = jnp.full(out_ref.shape, -1.0, f32)

    def clear(i, carry):
        count_ref[i] = 0
        return carry

    lax.fori_loop(0, devices, clear, 0, unroll=8)
    copies[0].wait()

    def rank(b, carry):
        owner = owner_ref[b]
        seen = count_ref[owner]
        count_ref[owner] = seen + 1
        base_ref[b] = (owner * CAP + seen) * CHANNELS
        return carry

    lax.fori_loop(0, blocks, rank, 0, unroll=8)
    for copy in copies[1:]:
        copy.wait()
    half = 0.5 * TAU * dist_ref[...]
    for k in range(3):
        coef_ref[k] = half * coef_ref[k]
    for k in range(3, 5):
        coef_ref[k] = TAU * coef_ref[k]
    coef_ref[5] = jnp.where(mask_ref[...] > 0, cell_ref[...], 1 << 14).astype(f32)

    def place(b, carry):
        base = base_ref[b]
        for c in range(CHANNELS):
            out_ref[pl.ds(base + c, 1), :] = coef_ref[c, pl.ds(b, 1), :]
        return carry

    lax.fori_loop(0, blocks, place, 0, unroll=8)


def shift_rows(x, amount):
    return pltpu.roll(x, amount % x.shape[1], axis=1)


def scatter_kernel(recv_ref, rhs_ref, perm_ref, r1_ref, wn_ref, up_ref, down_ref, first_ref, second_ref, acc_ref, list_ref):
    rows = recv_ref.shape[0]
    slots = rows // CHANNELS
    planes = rhs_ref.shape[1]
    hi_n = planes * 8
    lo_n = rhs_ref.shape[3]
    data = recv_ref[...]
    is_cell = lax.rem(lax.broadcasted_iota(jnp.int32, data.shape, 0), CHANNELS) == CHANNELS - 1
    cell = data.astype(jnp.int32)
    lead = data.astype(bf16).astype(f32)
    first_ref[0:rows] = jnp.where(is_cell, (cell >> 8).astype(f32), lead)
    second_ref[0:rows] = jnp.where(is_cell, (cell & 255).astype(f32), data - lead)
    first_ref[rows : rows + 8] = jnp.full((8, 128), -1.0, f32)
    second_ref[rows : rows + 8] = jnp.zeros((8, 128), f32)
    acc_ref[...] = jnp.zeros(acc_ref.shape, f32)

    def scan(i, count):
        for j in range(8):
            base = (i * 8 + j) * CHANNELS
            list_ref[count] = base
            mark = recv_ref[pl.ds(base + 5, 1), :][0, 0]
            count = count + jnp.where(mark >= 0.0, 1, 0).astype(jnp.int32)
        return count

    count = lax.fori_loop(0, slots // 8, scan, jnp.int32(0))
    for j in range(GROUP):
        list_ref[count + j] = rows
    hi_iota = lax.broadcasted_iota(jnp.int32, (hi_n, 128), 0).astype(f32).astype(bf16)
    lo_iota = lax.broadcasted_iota(jnp.int32, (lo_n, 128), 0).astype(f32).astype(bf16)
    one = jnp.ones((), bf16)
    zero = jnp.zeros((), bf16)

    def spread(ref, index, n):
        tile = jnp.broadcast_to(ref[pl.ds(index, 1), :], (16, 128)).astype(bf16)
        return jnp.concatenate([tile] * (n // 16), axis=0)

    def step(g, carry):
        left, right = [], []
        for j in range(GROUP):
            base = list_ref[g * GROUP + j]
            hot = hi_iota == spread(first_ref, base + 5, hi_n)
            pieces = []
            for c in range(5):
                pieces.append(jnp.where(hot, spread(first_ref, base + c, hi_n), zero))
                pieces.append(jnp.where(hot, spread(second_ref, base + c, hi_n), zero))
            pieces.append(jnp.where(hot, one, zero))
            left.append(jnp.concatenate(pieces, axis=0))
            right.append(jnp.where(lo_iota == spread(second_ref, base + 5, lo_n), one, zero))
        acc_ref[...] += lax.dot_general(
            jnp.concatenate(left, axis=1),
            jnp.concatenate(right, axis=1),
            (((1,), (1,)), ((), ())),
            preferred_element_type=f32,
        )
        return carry

    lax.fori_loop(0, (count + GROUP - 1) // GROUP, step, 0)

    def channel(c):
        if c == 5:
            total = acc_ref[pl.ds(10 * hi_n, hi_n), :]
        else:
            total = acc_ref[pl.ds(2 * c * hi_n, hi_n), :] + acc_ref[pl.ds((2 * c + 1) * hi_n, hi_n), :]
        return total.reshape(planes, 8, lo_n)

    re = rhs_ref[0] - channel(3)
    im = rhs_ref[1] - channel(4)
    wn = [TAU * channel(5), channel(0), channel(1), channel(2)]
    r1_ref[0] = re
    r1_ref[1] = im
    for k in range(4):
        wn_ref[k] = wn[k]
    perm = perm_ref[...]
    place = lax.axis_index("gx")
    last = lax.axis_size("gx") - 1
    sub = lax.broadcasted_iota(jnp.int32, (planes, 8, lo_n), 1)
    t = jnp.where(sub < 3, re, shift_rows(im, 3))
    t = jnp.where(sub < 6, t, jnp.where(sub == 6, shift_rows(wn[0], 6), shift_rows(wn[1], 7)))
    up_ref[:, 0:8, :] = t
    t = jnp.where(sub < 3, perm, jnp.where(sub == 3, shift_rows(wn[2], 3), shift_rows(wn[3], 4)))
    up_ref[:, 8:16, :] = jnp.where(place == 0, 0.0, t)
    t = jnp.where(sub >= 5, re, shift_rows(im, -3))
    t = jnp.where(sub >= 2, t, jnp.where(sub == 1, shift_rows(wn[0], -6), shift_rows(wn[1], -7)))
    down_ref[:, 0:8, :] = t
    t = jnp.where(sub >= 5, perm, jnp.where(sub == 4, shift_rows(wn[2], -3), shift_rows(wn[3], -4)))
    down_ref[:, 8:16, :] = jnp.where(place == last, 0.0, t)


ROW_PLACE = ((0, 0, 3), (0, 3, 3), (1, 0, 3), (0, 6, 1), (0, 7, 1), (1, 3, 1), (1, 4, 1))
COL_PLACE = ((0, 3), (3, 3), (6, 3), (9, 1), (10, 1), (11, 1), (12, 1))


def halo_rows(c, above_ref, below_ref, lanes):
    tile, offset, width = ROW_PLACE[c]
    rows = pl.ds(tile * 8, 8)
    below = shift_rows(below_ref[:, rows, lanes], -offset)
    above = shift_rows(above_ref[:, rows, lanes], offset)
    sub = lax.broadcasted_iota(jnp.int32, below.shape, 1)
    return jnp.where(sub < width, below, jnp.where(sub >= 8 - width, above, 0.0))


def own_channel(c, r1_ref, perm_ref, wn_ref, lanes):
    if c < 2:
        return r1_ref[c, :, :, lanes]
    if c == 2:
        return perm_ref[:, :, lanes]
    return wn_ref[c - 3, :, :, lanes]


def strip_kernel(r1_ref, perm_ref, wn_ref, above_ref, below_ref, left_ref, right_ref):
    lo_n = perm_ref.shape[2]
    planes = perm_ref.shape[0]
    lane = lax.broadcasted_iota(jnp.int32, (planes, 16, 128), 2)
    position = lax.axis_index("gy")
    last = lax.axis_size("gy") - 1
    for out_ref, start, sign, edge in ((left_ref, 0, 1, 0), (right_ref, lo_n - 128, -1, last)):
        lanes = pl.ds(start, 128)
        place = lane if sign > 0 else 127 - lane
        strip = jnp.zeros((planes, 16, 128), f32)
        for c in range(7):
            full = jnp.concatenate(
                [own_channel(c, r1_ref, perm_ref, wn_ref, lanes), halo_rows(c, above_ref, below_ref, lanes)], axis=1
            )
            offset, width = COL_PLACE[c]
            moved = pltpu.roll(full, (sign * offset) % 128, axis=2)
            strip = jnp.where((place >= offset) & (place < offset + width), moved, strip)
        out_ref[...] = jnp.where(position == edge, 0.0, strip)


def final_kernel(r1_ref, perm_ref, wn_ref, above_ref, below_ref, fleft_ref, fright_ref, sol_ref, res_ref):
    lo_n = perm_ref.shape[2]
    planes = perm_ref.shape[0]
    wide = lo_n + 128
    lane = lax.broadcasted_iota(jnp.int32, (planes, 16, 128), 2)
    everything = pl.ds(0, lo_n)

    def extended(c):
        body = jnp.concatenate(
            [own_channel(c, r1_ref, perm_ref, wn_ref, everything), halo_rows(c, above_ref, below_ref, everything)], axis=1
        )
        offset, width = COL_PLACE[c]
        right = pltpu.roll(fright_ref[...], (-offset) % 128, axis=2)
        left = pltpu.roll(fleft_ref[...], offset, axis=2)
        side = jnp.where(lane < width, right, jnp.where(lane >= 128 - width, left, 0.0))
        return jnp.concatenate([body, side], axis=2)

    re, im, perm, w, nz, nx, ny = [extended(c) for c in range(7)]
    diag = 6.0 - K_SQUARED * perm
    shift = BETA * K_SQUARED * perm
    denom = diag * diag + shift * shift
    inside = perm > 0.5
    inv_re = jnp.where(inside, OMEGA * diag / denom, 0.0)
    inv_im = jnp.where(inside, -OMEGA * shift / denom, 0.0)

    def damp(a, b):
        return a * inv_re - b * inv_im, a * inv_im + b * inv_re

    def sides(v):
        nothing = jnp.zeros((1,) + v.shape[1:], f32)
        after = jnp.concatenate([v[1:], nothing], axis=0)
        before = jnp.concatenate([nothing, v[:-1]], axis=0)
        return (
            (after, before),
            (pltpu.roll(v, 15, axis=1), pltpu.roll(v, 1, axis=1)),
            (pltpu.roll(v, wide - 1, axis=2), pltpu.roll(v, 1, axis=2)),
        )

    def helm(v, pairs):
        total = pairs[0][0] + pairs[0][1]
        for a, b in pairs[1:]:
            total = total + a + b
        return diag * v - total

    def swept(a, b):
        za, zb = damp(a, b)
        ma = helm(za, sides(za)) - shift * zb
        mb = helm(zb, sides(zb)) + shift * za
        da, db = damp(a - ma, b - mb)
        return za + da, zb + db

    def surface(v, pairs):
        (a, b), (c, d), (e, f) = pairs
        return w * v + nz * (a - b) + nx * (c - d) + ny * (e - f)

    def remaining(r, v):
        pairs = sides(v)
        return r - helm(v, pairs) - surface(v, pairs)

    sa, sb = swept(re, im)
    ra, rb = remaining(re, sa), remaining(im, sb)
    ua, ub = swept(ra, rb)
    res_ref[0] = ra[:, 0:8, 0:lo_n]
    res_ref[1] = rb[:, 0:8, 0:lo_n]
    sol_ref[0] = (sa + ua)[:, 0:8, 0:lo_n]
    sol_ref[1] = (sb + ub)[:, 0:8, 0:lo_n]


def in_vmem(n):
    return [pl.BlockSpec(memory_space=pltpu.VMEM)] * n


def shape(*dims):
    return jax.ShapeDtypeStruct(dims, f32)


def per_device(rhs_field, permittivity, surf_dist, surf_normal, surf_inc, surf_cell, surf_mask, surf_owner):
    planes, rows, cols = permittivity.shape
    blocks, points = surf_cell.shape
    gx, gy = lax.axis_size("gx"), lax.axis_size("gy")
    devices = gx * gy
    slots = devices * CAP
    params = pltpu.CompilerParams(vmem_limit_bytes=48 << 20)
    send = pl.pallas_call(
        pack_kernel,
        out_shape=shape(slots * CHANNELS, points),
        in_specs=[pl.BlockSpec(memory_space=pl.ANY)] * 6,
        out_specs=pl.BlockSpec(memory_space=pltpu.VMEM),
        scratch_shapes=[
            pltpu.SMEM((blocks,), jnp.int32),
            pltpu.SMEM((blocks,), jnp.int32),
            pltpu.SMEM((devices,), jnp.int32),
            pltpu.VMEM((blocks, points), f32),
            pltpu.VMEM((CHANNELS, blocks, points), f32),
            pltpu.VMEM((blocks, points), jnp.int32),
            pltpu.VMEM((blocks, points), jnp.int32),
            pltpu.SemaphoreType.DMA((6,)),
        ],
        compiler_params=params,
        name="pack",
    )(surf_owner[:, 0], surf_dist, surf_normal, surf_inc, surf_cell, surf_mask)
    recv = lax.all_to_all(send.reshape(-1), ("gx", "gy"), split_axis=0, concat_axis=0, tiled=True)
    recv = recv.reshape(slots * CHANNELS, points)
    field = shape(2, planes, rows, cols)
    r1, wn, up, down = pl.pallas_call(
        scatter_kernel,
        out_shape=(field, shape(4, planes, rows, cols), shape(planes, 16, cols), shape(planes, 16, cols)),
        in_specs=in_vmem(3),
        out_specs=tuple(in_vmem(4)),
        scratch_shapes=[
            pltpu.VMEM((slots * CHANNELS + 8, points), f32),
            pltpu.VMEM((slots * CHANNELS + 8, points), f32),
            pltpu.VMEM((PARTS * planes * rows, cols), f32),
            pltpu.SMEM((slots + GROUP,), jnp.int32),
        ],
        compiler_params=params,
        name="scatter",
    )(recv, rhs_field, permittivity)
    later = [(i, (i + 1) % gx) for i in range(gx)]
    above = lax.ppermute(down, "gx", later)
    below = lax.ppermute(up, "gx", [(j, i) for i, j in later])
    strip = shape(planes, 16, 128)
    to_left, to_right = pl.pallas_call(
        strip_kernel,
        out_shape=(strip, strip),
        in_specs=in_vmem(5),
        out_specs=tuple(in_vmem(2)),
        compiler_params=params,
        name="strips",
    )(r1, permittivity, wn, above, below)
    later = [(i, (i + 1) % gy) for i in range(gy)]
    from_left = lax.ppermute(to_right, "gy", later)
    from_right = lax.ppermute(to_left, "gy", [(j, i) for i, j in later])
    return pl.pallas_call(
        final_kernel,
        out_shape=(field, field),
        in_specs=in_vmem(7),
        out_specs=tuple(in_vmem(2)),
        compiler_params=params,
        name="final",
    )(r1, permittivity, wn, above, below, from_left, from_right)


def solution(mesh):
    split = ("gx", "gy")
    placed = (
        P(None, None, "gx", "gy"),
        P(None, "gx", "gy"),
        P(split, None),
        P(None, split, None),
        P(None, split, None),
        P(split, None),
        P(split, None),
        P(split, None),
    )
    return jax.shard_map(
        per_device,
        mesh=mesh,
        in_specs=placed,
        out_specs=(P(None, None, "gx", "gy"), P(None, None, "gx", "gy")),
        check_vma=False,
    )
```

```python
import functools

import jax
import jax.numpy as jnp
from jax import lax
from jax.experimental import pallas as pl
from jax.experimental.pallas import tpu as pltpu
from jax.sharding import PartitionSpec as P

CAP = 2
K_SQUARED = 0.25
BETA = 0.5
OMEGA = 0.8
TAU = 1.0

CHANNELS = 6
PARTS = 11
GROUP = 32

f32 = jnp.float32
bf16 = jnp.bfloat16


def pack_kernel(
    owner_hbm, dist_hbm, normal_hbm, inc_hbm, cell_hbm, mask_hbm, out_ref,
    owner_ref, base_ref, count_ref, dist_ref, coef_ref, cell_ref, mask_ref, sems,
):
    blocks = dist_ref.shape[0]
    devices = count_ref.shape[0]
    copies = [
        pltpu.make_async_copy(owner_hbm, owner_ref, sems.at[0]),
        pltpu.make_async_copy(dist_hbm, dist_ref, sems.at[1]),
        pltpu.make_async_copy(normal_hbm, coef_ref.at[pl.ds(0, 3)], sems.at[2]),
        pltpu.make_async_copy(inc_hbm, coef_ref.at[pl.ds(3, 2)], sems.at[3]),
        pltpu.make_async_copy(cell_hbm, cell_ref, sems.at[4]),
        pltpu.make_async_copy(mask_hbm, mask_ref, sems.at[5]),
    ]
    for copy in copies:
        copy.start()
    out_ref[...] = jnp.full(out_ref.shape, -1.0, f32)

    def clear(i, carry):
        count_ref[i] = 0
        return carry

    lax.fori_loop(0, devices, clear, 0, unroll=8)
    copies[0].wait()

    def rank(b, carry):
        owner = owner_ref[b]
        seen = count_ref[owner]
        count_ref[owner] = seen + 1
        base_ref[b] = (owner * CAP + seen) * CHANNELS
        return carry

    lax.fori_loop(0, blocks, rank, 0, unroll=8)
    for copy in copies[1:]:
        copy.wait()
    half = 0.5 * TAU * dist_ref[...]
    for k in range(3):
        coef_ref[k] = half * coef_ref[k]
    for k in range(3, 5):
        coef_ref[k] = TAU * coef_ref[k]
    coef_ref[5] = jnp.where(mask_ref[...] > 0, cell_ref[...], 1 << 14).astype(f32)

    def place(b, carry):
        base = base_ref[b]
        for c in range(CHANNELS):
            out_ref[pl.ds(base + c, 1), :] = coef_ref[c, pl.ds(b, 1), :]
        return carry

    lax.fori_loop(0, blocks, place, 0, unroll=8)


def shift_rows(x, amount):
    return pltpu.roll(x, amount % x.shape[1], axis=1)


def scatter_kernel(recv_ref, rhs_ref, perm_ref, r1_ref, wn_ref, up_ref, down_ref, first_ref, second_ref, acc_ref, list_ref):
    rows = recv_ref.shape[0]
    slots = rows // CHANNELS
    planes = rhs_ref.shape[1]
    hi_n = planes * 8
    lo_n = rhs_ref.shape[3]
    data = recv_ref[...]
    is_cell = lax.rem(lax.broadcasted_iota(jnp.int32, data.shape, 0), CHANNELS) == CHANNELS - 1
    cell = data.astype(jnp.int32)
    lead = data.astype(bf16).astype(f32)
    first_ref[0:rows] = jnp.where(is_cell, (cell >> 8).astype(f32), lead)
    second_ref[0:rows] = jnp.where(is_cell, (cell & 255).astype(f32), data - lead)
    first_ref[rows : rows + 8] = jnp.full((8, 128), -1.0, f32)
    second_ref[rows : rows + 8] = jnp.zeros((8, 128), f32)
    acc_ref[...] = jnp.zeros(acc_ref.shape, f32)

    def scan(i, count):
        for j in range(8):
            base = (i * 8 + j) * CHANNELS
            list_ref[count] = base
            mark = recv_ref[pl.ds(base + 5, 1), :][0, 0]
            count = count + jnp.where(mark >= 0.0, 1, 0).astype(jnp.int32)
        return count

    count = lax.fori_loop(0, slots // 8, scan, jnp.int32(0))
    for j in range(GROUP):
        list_ref[count + j] = rows
    hi_iota = lax.broadcasted_iota(jnp.int32, (hi_n, 128), 0).astype(f32).astype(bf16)
    lo_iota = lax.broadcasted_iota(jnp.int32, (lo_n, 128), 0).astype(f32).astype(bf16)
    one = jnp.ones((), bf16)
    zero = jnp.zeros((), bf16)

    def spread(ref, index, n):
        tile = jnp.broadcast_to(ref[pl.ds(index, 1), :], (16, 128)).astype(bf16)
        return jnp.concatenate([tile] * (n // 16), axis=0)

    def step(g, carry):
        left, right = [], []
        for j in range(GROUP):
            base = list_ref[g * GROUP + j]
            hot = hi_iota == spread(first_ref, base + 5, hi_n)
            pieces = []
            for c in range(5):
                pieces.append(jnp.where(hot, spread(first_ref, base + c, hi_n), zero))
                pieces.append(jnp.where(hot, spread(second_ref, base + c, hi_n), zero))
            pieces.append(jnp.where(hot, one, zero))
            left.append(jnp.concatenate(pieces, axis=0))
            right.append(jnp.where(lo_iota == spread(second_ref, base + 5, lo_n), one, zero))
        acc_ref[...] += lax.dot_general(
            jnp.concatenate(left, axis=1),
            jnp.concatenate(right, axis=1),
            (((1,), (1,)), ((), ())),
            preferred_element_type=f32,
        )
        return carry

    lax.fori_loop(0, (count + GROUP - 1) // GROUP, step, 0)

    def channel(c):
        if c == 5:
            total = acc_ref[pl.ds(10 * hi_n, hi_n), :]
        else:
            total = acc_ref[pl.ds(2 * c * hi_n, hi_n), :] + acc_ref[pl.ds((2 * c + 1) * hi_n, hi_n), :]
        return total.reshape(planes, 8, lo_n)

    re = rhs_ref[0] - channel(3)
    im = rhs_ref[1] - channel(4)
    wn = [TAU * channel(5), channel(0), channel(1), channel(2)]
    r1_ref[0] = re
    r1_ref[1] = im
    for k in range(4):
        wn_ref[k] = wn[k]
    perm = perm_ref[...]
    place = lax.axis_index("gx")
    last = lax.axis_size("gx") - 1
    sub = lax.broadcasted_iota(jnp.int32, (planes, 8, lo_n), 1)
    t = jnp.where(sub < 3, re, shift_rows(im, 3))
    t = jnp.where(sub < 6, t, jnp.where(sub == 6, shift_rows(wn[0], 6), shift_rows(wn[1], 7)))
    up_ref[:, 0:8, :] = t
    t = jnp.where(sub < 3, perm, jnp.where(sub == 3, shift_rows(wn[2], 3), shift_rows(wn[3], 4)))
    up_ref[:, 8:16, :] = jnp.where(place == 0, 0.0, t)
    t = jnp.where(sub >= 5, re, shift_rows(im, -3))
    t = jnp.where(sub >= 2, t, jnp.where(sub == 1, shift_rows(wn[0], -6), shift_rows(wn[1], -7)))
    down_ref[:, 0:8, :] = t
    t = jnp.where(sub >= 5, perm, jnp.where(sub == 4, shift_rows(wn[2], -3), shift_rows(wn[3], -4)))
    down_ref[:, 8:16, :] = jnp.where(place == last, 0.0, t)


ROW_PLACE = ((0, 0, 3), (0, 3, 3), (1, 0, 3), (0, 6, 1), (0, 7, 1), (1, 3, 1), (1, 4, 1))
COL_PLACE = ((0, 3), (3, 3), (6, 3), (9, 1), (10, 1), (11, 1), (12, 1))


def halo_rows(c, above_ref, below_ref, lanes):
    tile, offset, width = ROW_PLACE[c]
    rows = pl.ds(tile * 8, 8)
    below = shift_rows(below_ref[:, rows, lanes], -offset)
    above = shift_rows(above_ref[:, rows, lanes], offset)
    sub = lax.broadcasted_iota(jnp.int32, below.shape, 1)
    return jnp.where(sub < width, below, jnp.where(sub >= 8 - width, above, 0.0))


def own_channel(c, r1_ref, perm_ref, wn_ref, lanes):
    if c < 2:
        return r1_ref[c, :, :, lanes]
    if c == 2:
        return perm_ref[:, :, lanes]
    return wn_ref[c - 3, :, :, lanes]


def strip_kernel(r1_ref, perm_ref, wn_ref, above_ref, below_ref, left_ref, right_ref):
    lo_n = perm_ref.shape[2]
    planes = perm_ref.shape[0]
    lane = lax.broadcasted_iota(jnp.int32, (planes, 16, 128), 2)
    position = lax.axis_index("gy")
    last = lax.axis_size("gy") - 1
    for out_ref, start, sign, edge in ((left_ref, 0, 1, 0), (right_ref, lo_n - 128, -1, last)):
        lanes = pl.ds(start, 128)
        place = lane if sign > 0 else 127 - lane
        strip = jnp.zeros((planes, 16, 128), f32)
        for c in range(7):
            full = jnp.concatenate(
                [own_channel(c, r1_ref, perm_ref, wn_ref, lanes), halo_rows(c, above_ref, below_ref, lanes)], axis=1
            )
            offset, width = COL_PLACE[c]
            moved = pltpu.roll(full, (sign * offset) % 128, axis=2)
            strip = jnp.where((place >= offset) & (place < offset + width), moved, strip)
        out_ref[...] = jnp.where(position == edge, 0.0, strip)


def final_kernel(r1_ref, perm_ref, wn_ref, above_ref, below_ref, fleft_ref, fright_ref, sol_ref, res_ref):
    lo_n = perm_ref.shape[2]
    planes = perm_ref.shape[0]
    wide = lo_n + 128
    lane = lax.broadcasted_iota(jnp.int32, (planes, 16, 128), 2)
    everything = pl.ds(0, lo_n)

    def extended(c):
        body = jnp.concatenate(
            [own_channel(c, r1_ref, perm_ref, wn_ref, everything), halo_rows(c, above_ref, below_ref, everything)], axis=1
        )
        offset, width = COL_PLACE[c]
        right = pltpu.roll(fright_ref[...], (-offset) % 128, axis=2)
        left = pltpu.roll(fleft_ref[...], offset, axis=2)
        side = jnp.where(lane < width, right, jnp.where(lane >= 128 - width, left, 0.0))
        return jnp.concatenate([body, side], axis=2)

    re, im, perm, w, nz, nx, ny = [extended(c) for c in range(7)]
    diag = 6.0 - K_SQUARED * perm
    shift = BETA * K_SQUARED * perm
    denom = diag * diag + shift * shift
    inside = perm > 0.5
    inv_re = jnp.where(inside, OMEGA * diag / denom, 0.0)
    inv_im = jnp.where(inside, -OMEGA * shift / denom, 0.0)

    def damp(a, b):
        return a * inv_re - b * inv_im, a * inv_im + b * inv_re

    def sides(v):
        nothing = jnp.zeros((1,) + v.shape[1:], f32)
        after = jnp.concatenate([v[1:], nothing], axis=0)
        before = jnp.concatenate([nothing, v[:-1]], axis=0)
        return (
            (after, before),
            (pltpu.roll(v, 15, axis=1), pltpu.roll(v, 1, axis=1)),
            (pltpu.roll(v, wide - 1, axis=2), pltpu.roll(v, 1, axis=2)),
        )

    def helm(v, pairs):
        total = pairs[0][0] + pairs[0][1]
        for a, b in pairs[1:]:
            total = total + a + b
        return diag * v - total

    def swept(a, b):
        za, zb = damp(a, b)
        ma = helm(za, sides(za)) - shift * zb
        mb = helm(zb, sides(zb)) + shift * za
        da, db = damp(a - ma, b - mb)
        return za + da, zb + db

    def surface(v, pairs):
        (a, b), (c, d), (e, f) = pairs
        return w * v + nz * (a - b) + nx * (c - d) + ny * (e - f)

    def remaining(r, v):
        pairs = sides(v)
        return r - helm(v, pairs) - surface(v, pairs)

    sa, sb = swept(re, im)
    ra, rb = remaining(re, sa), remaining(im, sb)
    ua, ub = swept(ra, rb)
    res_ref[0] = ra[:, 0:8, 0:lo_n]
    res_ref[1] = rb[:, 0:8, 0:lo_n]
    sol_ref[0] = (sa + ua)[:, 0:8, 0:lo_n]
    sol_ref[1] = (sb + ub)[:, 0:8, 0:lo_n]


def in_vmem(n):
    return [pl.BlockSpec(memory_space=pltpu.VMEM)] * n


def shape(*dims):
    return jax.ShapeDtypeStruct(dims, f32)


def per_device(rhs_field, permittivity, surf_dist, surf_normal, surf_inc, surf_cell, surf_mask, surf_owner):
    planes, rows, cols = permittivity.shape
    blocks, points = surf_cell.shape
    gx, gy = lax.axis_size("gx"), lax.axis_size("gy")
    devices = gx * gy
    slots = devices * CAP
    params = pltpu.CompilerParams(vmem_limit_bytes=48 << 20)
    send = pl.pallas_call(
        pack_kernel,
        out_shape=shape(slots * CHANNELS, points),
        in_specs=[pl.BlockSpec(memory_space=pltpu.HBM)] * 6,
        out_specs=pl.BlockSpec(memory_space=pltpu.VMEM),
        scratch_shapes=[
            pltpu.SMEM((blocks,), jnp.int32),
            pltpu.SMEM((blocks,), jnp.int32),
            pltpu.SMEM((devices,), jnp.int32),
            pltpu.VMEM((blocks, points), f32),
            pltpu.VMEM((CHANNELS, blocks, points), f32),
            pltpu.VMEM((blocks, points), jnp.int32),
            pltpu.VMEM((blocks, points), jnp.int32),
            pltpu.SemaphoreType.DMA((6,)),
        ],
        compiler_params=params,
        name="pack",
    )(*[
        pltpu.with_memory_space_constraint(x, pltpu.HBM)
        for x in (surf_owner[:, 0], surf_dist, surf_normal, surf_inc, surf_cell, surf_mask)
    ])
    recv = lax.all_to_all(send.reshape(-1), ("gx", "gy"), split_axis=0, concat_axis=0, tiled=True)
    recv = recv.reshape(slots * CHANNELS, points)
    field = shape(2, planes, rows, cols)
    r1, wn, up, down = pl.pallas_call(
        scatter_kernel,
        out_shape=(field, shape(4, planes, rows, cols), shape(planes, 16, cols), shape(planes, 16, cols)),
        in_specs=in_vmem(3),
        out_specs=tuple(in_vmem(4)),
        scratch_shapes=[
            pltpu.VMEM((slots * CHANNELS + 8, points), f32),
            pltpu.VMEM((slots * CHANNELS + 8, points), f32),
            pltpu.VMEM((PARTS * planes * rows, cols), f32),
            pltpu.SMEM((slots + GROUP,), jnp.int32),
        ],
        compiler_params=params,
        name="scatter",
    )(recv, rhs_field, permittivity)
    later = [(i, (i + 1) % gx) for i in range(gx)]
    above = lax.ppermute(down, "gx", later)
    below = lax.ppermute(up, "gx", [(j, i) for i, j in later])
    strip = shape(planes, 16, 128)
    to_left, to_right = pl.pallas_call(
        strip_kernel,
        out_shape=(strip, strip),
        in_specs=in_vmem(5),
        out_specs=tuple(in_vmem(2)),
        compiler_params=params,
        name="strips",
    )(r1, permittivity, wn, above, below)
    later = [(i, (i + 1) % gy) for i in range(gy)]
    from_left = lax.ppermute(to_right, "gy", later)
    from_right = lax.ppermute(to_left, "gy", [(j, i) for i, j in later])
    return pl.pallas_call(
        final_kernel,
        out_shape=(field, field),
        in_specs=in_vmem(7),
        out_specs=tuple(in_vmem(2)),
        compiler_params=params,
        name="final",
    )(r1, permittivity, wn, above, below, from_left, from_right)


def solution(mesh):
    split = ("gx", "gy")
    placed = (
        P(None, None, "gx", "gy"),
        P(None, "gx", "gy"),
        P(split, None),
        P(None, split, None),
        P(None, split, None),
        P(split, None),
        P(split, None),
        P(split, None),
    )
    return jax.shard_map(
        per_device,
        mesh=mesh,
        in_specs=placed,
        out_specs=(P(None, None, "gx", "gy"), P(None, None, "gx", "gy")),
        check_vma=False,
    )
```

```python
import functools

import jax
import jax.numpy as jnp
from jax import lax
from jax.experimental import pallas as pl
from jax.experimental.pallas import tpu as pltpu
from jax.sharding import PartitionSpec as P

CAP = 2
K_SQUARED = 0.25
BETA = 0.5
OMEGA = 0.8
TAU = 1.0

CHANNELS = 6
GROUP = 128

f32 = jnp.float32
bf16 = jnp.bfloat16


def pack_kernel(
    owner_hbm, dist_hbm, normal_hbm, inc_hbm, cell_hbm, mask_hbm, out_ref,
    owner_ref, base_ref, count_ref, dist_ref, coef_ref, cell_ref, mask_ref, sems,
):
    blocks = dist_ref.shape[0]
    devices = count_ref.shape[0]
    copies = [
        pltpu.make_async_copy(owner_hbm, owner_ref, sems.at[0]),
        pltpu.make_async_copy(dist_hbm, dist_ref, sems.at[1]),
        pltpu.make_async_copy(normal_hbm, coef_ref.at[pl.ds(0, 3)], sems.at[2]),
        pltpu.make_async_copy(inc_hbm, coef_ref.at[pl.ds(3, 2)], sems.at[3]),
        pltpu.make_async_copy(cell_hbm, cell_ref, sems.at[4]),
        pltpu.make_async_copy(mask_hbm, mask_ref, sems.at[5]),
    ]
    for copy in copies:
        copy.start()
    out_ref[...] = jnp.full(out_ref.shape, -1.0, f32)

    def clear(i, carry):
        count_ref[i] = 0
        return carry

    lax.fori_loop(0, devices, clear, 0, unroll=8)
    copies[0].wait()

    def rank(b, carry):
        owner = owner_ref[b]
        seen = count_ref[owner]
        count_ref[owner] = seen + 1
        base_ref[b] = (owner * CAP + seen) * CHANNELS
        return carry

    lax.fori_loop(0, blocks, rank, 0, unroll=8)
    for copy in copies[1:]:
        copy.wait()
    half = 0.5 * TAU * dist_ref[...]
    for k in range(3):
        coef_ref[k] = half * coef_ref[k]
    for k in range(3, 5):
        coef_ref[k] = TAU * coef_ref[k]
    coef_ref[5] = jnp.where(mask_ref[...] > 0, cell_ref[...], 1 << 14).astype(f32)

    def place(b, carry):
        base = base_ref[b]
        for c in range(CHANNELS):
            out_ref[pl.ds(base + c, 1), :] = coef_ref[c, pl.ds(b, 1), :]
        return carry

    lax.fori_loop(0, blocks, place, 0, unroll=8)


def scatter_slots(recv_ref, hi_ref, lo_ref, acc_ref, channels, count):
    slots = hi_ref.shape[0]
    lo_n = acc_ref.shape[1]
    hi_n = acc_ref.shape[0] // (2 * len(channels) + count)
    group = min(GROUP, slots)
    chunk = min(64, slots)
    for i in range(0, slots, chunk):
        cell = recv_ref[pl.ds(i * CHANNELS + CHANNELS - 1, chunk, stride=CHANNELS), :].astype(jnp.int32)
        hi_ref[i : i + chunk] = (cell >> 8).astype(f32)
        lo_ref[i : i + chunk] = (cell & 255).astype(f32)
    acc_ref[...] = jnp.zeros(acc_ref.shape, f32)
    hi_iota = lax.broadcasted_iota(jnp.int32, (hi_n, 128), 0).astype(f32).astype(bf16)
    lo_iota = lax.broadcasted_iota(jnp.int32, (lo_n, 128), 0).astype(f32).astype(bf16)
    one = jnp.ones((), bf16)
    zero = jnp.zeros((), bf16)

    def row(ref, index):
        return jnp.broadcast_to(ref[pl.ds(index, 1), :], (16, 128))

    def tall(tile, n):
        return jnp.concatenate([tile] * (n // 16), axis=0)

    def step(g, carry):
        left, right = [], []
        for j in range(group):
            slot = g * group + j
            hot = hi_iota == tall(row(hi_ref, slot).astype(bf16), hi_n)
            pieces = []
            for c in channels:
                value = row(recv_ref, slot * CHANNELS + c)
                lead = value.astype(bf16)
                rest = (value - lead.astype(f32)).astype(bf16)
                pieces.append(jnp.where(hot, tall(lead, hi_n), zero))
                pieces.append(jnp.where(hot, tall(rest, hi_n), zero))
            if count:
                pieces.append(jnp.where(hot, one, zero))
            left.append(jnp.concatenate(pieces, axis=0))
            right.append(jnp.where(lo_iota == tall(row(lo_ref, slot).astype(bf16), lo_n), one, zero))
        acc_ref[...] += lax.dot_general(
            jnp.concatenate(left, axis=1),
            jnp.concatenate(right, axis=1),
            (((1,), (1,)), ((), ())),
            preferred_element_type=f32,
        )
        return carry

    lax.fori_loop(0, slots // group, step, 0)

    def channel(k):
        return acc_ref[2 * k * hi_n : (2 * k + 1) * hi_n, :] + acc_ref[(2 * k + 1) * hi_n : (2 * k + 2) * hi_n, :]

    return [channel(k) for k in range(len(channels))] + ([acc_ref[2 * len(channels) * hi_n :, :]] if count else [])


def keep_tiles(ref, k, value):
    for t in range(ref.shape[1]):
        ref[k, t] = value[:, t * 128 : (t + 1) * 128]


def pack_rows(out_ref, item, ref, k, row, gate=None):
    planes = ref.shape[2] // 8
    for t in range(ref.shape[1]):
        value = ref[k, t, pl.ds(row, planes, stride=8), :]
        if gate is not None:
            value = jnp.where(gate, 0.0, value)
        out_ref[item * planes : (item + 1) * planes, t * 128 : (t + 1) * 128] = value


def unpack_rows(ref, k, row, in_ref, item):
    planes = ref.shape[2] // 8
    for t in range(ref.shape[1]):
        value = in_ref[item * planes : (item + 1) * planes, t * 128 : (t + 1) * 128]
        ref[k, t, pl.ds(row, planes, stride=8), :] = value


def incident_kernel(recv_ref, rhs_ref, perm_ref, r1_ref, up_ref, down_ref, hi_ref, lo_ref, acc_ref, tile_ref):
    parts = scatter_slots(recv_ref, hi_ref, lo_ref, acc_ref, (3, 4), 0)
    for k in range(2):
        value = rhs_ref[k] - parts[k]
        r1_ref[k] = value
        keep_tiles(tile_ref, k, value)
    keep_tiles(tile_ref, 2, perm_ref[...])
    place = lax.axis_index("gx")
    for out_ref, start, edge in ((up_ref, 0, 0), (down_ref, 5, lax.axis_size("gx") - 1)):
        for c in range(3):
            for k in range(3):
                pack_rows(out_ref, 3 * c + k, tile_ref, c, start + k, place == edge if c == 2 else None)


def coefficient_kernel(recv_ref, wn_ref, up_ref, down_ref, hi_ref, lo_ref, acc_ref, tile_ref):
    nz, nx, ny, w = scatter_slots(recv_ref, hi_ref, lo_ref, acc_ref, (0, 1, 2), 1)
    for k, value in enumerate((TAU * w, nz, nx, ny)):
        wn_ref[k] = value
        keep_tiles(tile_ref, k, value)
        pack_rows(up_ref, k, tile_ref, k, 0)
        pack_rows(down_ref, k, tile_ref, k, 7)


COL_PLACE = ((0, 3), (3, 3), (6, 3), (9, 1), (10, 1), (11, 1), (12, 1))


def strip_kernel(r1_ref, perm_ref, wn_ref, above_ref, below_ref, left_ref, right_ref, halo_ref):
    planes = perm_ref.shape[0] // 8
    lo_n = perm_ref.shape[1]
    halo_ref[...] = jnp.zeros(halo_ref.shape, f32)
    for c in range(3):
        for k in range(3):
            unpack_rows(halo_ref, c, k, below_ref, 3 * c + k)
            unpack_rows(halo_ref, c, 5 + k, above_ref, 3 * c + k)
    lane = lax.broadcasted_iota(jnp.int32, (planes, 16, 128), 2)
    position = lax.axis_index("gy")
    last = lax.axis_size("gy") - 1
    nothing = jnp.zeros((planes, 8, 128), f32)
    for out_ref, start, sign, edge in ((left_ref, 0, 1, 0), (right_ref, lo_n - 128, -1, last)):
        lanes = pl.ds(start, 128)
        place = lane if sign > 0 else 127 - lane
        strip = jnp.zeros((planes, 16, 128), f32)
        for c in range(7):
            if c < 3:
                own = perm_ref[:, lanes] if c == 2 else r1_ref[c, :, lanes]
                other = halo_ref[c, start // 128].reshape(planes, 8, 128)
            else:
                own, other = wn_ref[c - 3, :, lanes], nothing
            full = jnp.concatenate([own.reshape(planes, 8, 128), other], axis=1)
            offset, width = COL_PLACE[c]
            moved = pltpu.roll(full, (sign * offset) % 128, axis=2)
            strip = jnp.where((place >= offset) & (place < offset + width), moved, strip)
        out_ref[...] = jnp.where(position == edge, 0.0, strip)


def final_kernel(
    r1_ref, perm_ref, wn_ref, halo_ref, above_ref, below_ref, fleft_ref, fright_ref, sol_ref, res_ref, edge_ref
):
    planes = perm_ref.shape[0] // 8
    lo_n = perm_ref.shape[1]
    wide = lo_n + 128
    lane = lax.broadcasted_iota(jnp.int32, (planes, 16, 128), 2)
    edge_ref[...] = jnp.zeros(edge_ref.shape, f32)
    for k in range(4):
        unpack_rows(edge_ref, k, 0, below_ref, k)
        unpack_rows(edge_ref, k, 7, above_ref, k)

    def extended(c):
        if c < 3:
            own = perm_ref[...] if c == 2 else r1_ref[c]
            other = [halo_ref[c, t] for t in range(lo_n // 128)]
        else:
            own = wn_ref[c - 3]
            other = [edge_ref[c - 3, t] for t in range(lo_n // 128)]
        other = jnp.concatenate([t.reshape(planes, 8, 128) for t in other], axis=2)
        body = jnp.concatenate([own.reshape(planes, 8, lo_n), other], axis=1)
        offset, width = COL_PLACE[c]
        right = pltpu.roll(fright_ref[...], (-offset) % 128, axis=2)
        left = pltpu.roll(fleft_ref[...], offset, axis=2)
        side = jnp.where(lane < width, right, jnp.where(lane >= 128 - width, left, 0.0))
        return jnp.concatenate([body, side], axis=2)

    re, im, perm, w, nz, nx, ny = [extended(c) for c in range(7)]
    diag = 6.0 - K_SQUARED * perm
    shift = BETA * K_SQUARED * perm
    denom = diag * diag + shift * shift
    inside = perm > 0.5
    inv_re = jnp.where(inside, OMEGA * diag / denom, 0.0)
    inv_im = jnp.where(inside, -OMEGA * shift / denom, 0.0)

    def damp(a, b):
        return a * inv_re - b * inv_im, a * inv_im + b * inv_re

    def sides(v):
        nothing = jnp.zeros((1,) + v.shape[1:], f32)
        after = jnp.concatenate([v[1:], nothing], axis=0)
        before = jnp.concatenate([nothing, v[:-1]], axis=0)
        return (
            (after, before),
            (pltpu.roll(v, 15, axis=1), pltpu.roll(v, 1, axis=1)),
            (pltpu.roll(v, wide - 1, axis=2), pltpu.roll(v, 1, axis=2)),
        )

    def helm(v, pairs):
        total = pairs[0][0] + pairs[0][1]
        for a, b in pairs[1:]:
            total = total + a + b
        return diag * v - total

    def swept(a, b):
        za, zb = damp(a, b)
        ma = helm(za, sides(za)) - shift * zb
        mb = helm(zb, sides(zb)) + shift * za
        da, db = damp(a - ma, b - mb)
        return za + da, zb + db

    def surface(v, pairs):
        (a, b), (c, d), (e, f) = pairs
        return w * v + nz * (a - b) + nx * (c - d) + ny * (e - f)

    def remaining(r, v):
        pairs = sides(v)
        return r - helm(v, pairs) - surface(v, pairs)

    sa, sb = swept(re, im)
    ra, rb = remaining(re, sa), remaining(im, sb)
    ua, ub = swept(ra, rb)
    res_ref[0] = ra[:, 0:8, 0:lo_n]
    res_ref[1] = rb[:, 0:8, 0:lo_n]
    sol_ref[0] = (sa + ua)[:, 0:8, 0:lo_n]
    sol_ref[1] = (sb + ub)[:, 0:8, 0:lo_n]


def in_vmem(n):
    return [pl.BlockSpec(memory_space=pltpu.VMEM)] * n


def shape(*dims):
    return jax.ShapeDtypeStruct(dims, f32)


def per_device(rhs_field, permittivity, surf_dist, surf_normal, surf_inc, surf_cell, surf_mask, surf_owner):
    planes, rows, cols = permittivity.shape
    blocks, points = surf_cell.shape
    gx, gy = lax.axis_size("gx"), lax.axis_size("gy")
    devices = gx * gy
    slots = devices * CAP
    params = pltpu.CompilerParams(vmem_limit_bytes=48 << 20)
    send = pl.pallas_call(
        pack_kernel,
        out_shape=shape(slots * CHANNELS, points),
        in_specs=[pl.BlockSpec(memory_space=pltpu.HBM)] * 6,
        out_specs=pl.BlockSpec(memory_space=pltpu.VMEM),
        scratch_shapes=[
            pltpu.SMEM((blocks,), jnp.int32),
            pltpu.SMEM((blocks,), jnp.int32),
            pltpu.SMEM((devices,), jnp.int32),
            pltpu.VMEM((blocks, points), f32),
            pltpu.VMEM((CHANNELS, blocks, points), f32),
            pltpu.VMEM((blocks, points), jnp.int32),
            pltpu.VMEM((blocks, points), jnp.int32),
            pltpu.SemaphoreType.DMA((6,)),
        ],
        compiler_params=params,
        name="pack",
    )(*[
        pltpu.with_memory_space_constraint(x, pltpu.HBM)
        for x in (surf_owner[:, 0], surf_dist, surf_normal, surf_inc, surf_cell, surf_mask)
    ])
    recv = lax.all_to_all(send.reshape(-1), ("gx", "gy"), split_axis=0, concat_axis=0, tiled=True)
    recv = recv.reshape(slots * CHANNELS, points)
    cells = planes * rows
    rhs_field = rhs_field.reshape(2, cells, cols)
    permittivity = permittivity.reshape(cells, cols)

    def scatter_scratch(parts, kept):
        return [
            pltpu.VMEM((slots, points), f32),
            pltpu.VMEM((slots, points), f32),
            pltpu.VMEM((parts * cells, cols), f32),
            pltpu.VMEM((kept, cols // 128, cells, 128), f32),
        ]

    r1, up, down = pl.pallas_call(
        incident_kernel,
        out_shape=(shape(2, cells, cols), shape(9 * planes, cols), shape(9 * planes, cols)),
        in_specs=in_vmem(3),
        out_specs=tuple(in_vmem(3)),
        scratch_shapes=scatter_scratch(4, 3),
        compiler_params=params,
        name="incident",
    )(recv, rhs_field, permittivity)
    after_x = [(i, (i + 1) % gx) for i in range(gx)]
    before_x = [(j, i) for i, j in after_x]
    after_y = [(i, (i + 1) % gy) for i in range(gy)]
    before_y = [(j, i) for i, j in after_y]
    above = lax.ppermute(down, "gx", after_x)
    below = lax.ppermute(up, "gx", before_x)
    flops = 2 * 7 * cells * cols * slots * points
    wn, up, down = pl.pallas_call(
        coefficient_kernel,
        out_shape=(shape(4, cells, cols), shape(4 * planes, cols), shape(4 * planes, cols)),
        in_specs=in_vmem(1),
        out_specs=tuple(in_vmem(3)),
        scratch_shapes=scatter_scratch(7, 4),
        compiler_params=params,
        cost_estimate=pl.CostEstimate(flops=flops, transcendentals=0, bytes_accessed=slots * CHANNELS * points * 4),
        name="coefficient",
    )(recv)
    above_wn = lax.ppermute(down, "gx", after_x)
    below_wn = lax.ppermute(up, "gx", before_x)
    to_left, to_right, halo = pl.pallas_call(
        strip_kernel,
        out_shape=(shape(planes, 16, 128), shape(planes, 16, 128), shape(3, cols // 128, cells, 128)),
        in_specs=in_vmem(5),
        out_specs=tuple(in_vmem(3)),
        compiler_params=params,
        name="strips",
    )(r1, permittivity, wn, above, below)
    from_left = lax.ppermute(to_right, "gy", after_y)
    from_right = lax.ppermute(to_left, "gy", before_y)
    field = shape(2, planes, rows, cols)
    return pl.pallas_call(
        final_kernel,
        out_shape=(field, field),
        in_specs=in_vmem(8),
        out_specs=tuple(in_vmem(2)),
        scratch_shapes=[pltpu.VMEM((4, cols // 128, cells, 128), f32)],
        compiler_params=params,
        name="final",
    )(r1, permittivity, wn, halo, above_wn, below_wn, from_left, from_right)


def solution(mesh):
    split = ("gx", "gy")
    placed = (
        P(None, None, "gx", "gy"),
        P(None, "gx", "gy"),
        P(split, None),
        P(None, split, None),
        P(None, split, None),
        P(split, None),
        P(split, None),
        P(split, None),
    )
    return jax.shard_map(
        per_device,
        mesh=mesh,
        in_specs=placed,
        out_specs=(P(None, None, "gx", "gy"), P(None, None, "gx", "gy")),
        check_vma=False,
    )
```

```python
import functools

import jax
import jax.numpy as jnp
from jax import lax
from jax.experimental import pallas as pl
from jax.experimental.pallas import tpu as pltpu
from jax.sharding import PartitionSpec as P

CAP = 2
K_SQUARED = 0.25
BETA = 0.5
OMEGA = 0.8
TAU = 1.0

CHANNELS = 6
GROUP = 128

f32 = jnp.float32
bf16 = jnp.bfloat16


def pack_kernel(
    owner_hbm, dist_hbm, normal_hbm, inc_hbm, cell_hbm, mask_hbm, out_ref,
    owner_ref, base_ref, count_ref, dist_ref, coef_ref, cell_ref, mask_ref, sems,
):
    blocks = dist_ref.shape[0]
    devices = count_ref.shape[0]
    copies = [
        pltpu.make_async_copy(owner_hbm, owner_ref, sems.at[0]),
        pltpu.make_async_copy(dist_hbm, dist_ref, sems.at[1]),
        pltpu.make_async_copy(normal_hbm, coef_ref.at[pl.ds(0, 3)], sems.at[2]),
        pltpu.make_async_copy(inc_hbm, coef_ref.at[pl.ds(3, 2)], sems.at[3]),
        pltpu.make_async_copy(cell_hbm, cell_ref, sems.at[4]),
        pltpu.make_async_copy(mask_hbm, mask_ref, sems.at[5]),
    ]
    for copy in copies:
        copy.start()
    out_ref[...] = jnp.full(out_ref.shape, -1.0, f32)

    def clear(i, carry):
        count_ref[i] = 0
        return carry

    lax.fori_loop(0, devices, clear, 0, unroll=8)
    copies[0].wait()

    def rank(b, carry):
        owner = owner_ref[b]
        seen = count_ref[owner]
        count_ref[owner] = seen + 1
        base_ref[b] = (owner * CAP + seen) * CHANNELS
        return carry

    lax.fori_loop(0, blocks, rank, 0, unroll=8)
    for copy in copies[1:]:
        copy.wait()
    half = 0.5 * TAU * dist_ref[...]
    for k in range(3):
        coef_ref[k] = half * coef_ref[k]
    for k in range(3, 5):
        coef_ref[k] = TAU * coef_ref[k]
    coef_ref[5] = jnp.where(mask_ref[...] > 0, cell_ref[...], 1 << 14).astype(f32)

    def place(b, carry):
        base = base_ref[b]
        for c in range(CHANNELS):
            out_ref[pl.ds(base + c, 1), :] = coef_ref[c, pl.ds(b, 1), :]
        return carry

    lax.fori_loop(0, blocks, place, 0, unroll=8)


def scatter_slots(recv_ref, hi_ref, lo_ref, acc_ref, groups):
    slots = hi_ref.shape[0]
    lo_n = acc_ref.shape[1]
    per_step = min(GROUP, slots)
    chunk = min(64, slots)
    for i in range(0, slots, chunk):
        cell = recv_ref[pl.ds(i * CHANNELS + CHANNELS - 1, chunk, stride=CHANNELS), :].astype(jnp.int32)
        hi_ref[i : i + chunk] = (cell >> 8).astype(f32)
        lo_ref[i : i + chunk] = (cell & 255).astype(f32)
    acc_ref[...] = jnp.zeros(acc_ref.shape, f32)
    one = jnp.ones((), bf16)
    zero = jnp.zeros((), bf16)
    targets = []
    for rows, _, _ in groups:
        place = lax.broadcasted_iota(jnp.int32, (8 * len(rows), 128), 0)
        item = place >> 3
        row = jnp.zeros_like(place)
        for k, r in enumerate(rows):
            row = jnp.where(item == k, r, row)
        targets.append(((place & 7) * 8 + row).astype(f32).astype(bf16))
    lo_iota = lax.broadcasted_iota(jnp.int32, (lo_n, 128), 0).astype(f32).astype(bf16)

    def load(ref, index):
        return jnp.broadcast_to(ref[pl.ds(index, 1), :], (16, 128))

    def tall(tile, n):
        return jnp.concatenate([tile] * (n // 16), axis=0)

    def step(g, carry):
        left, right = [], []
        for j in range(per_step):
            slot = g * per_step + j
            hi = load(hi_ref, slot).astype(bf16)
            pieces = []
            for target, (rows, channels, count) in zip(targets, groups):
                n = 8 * len(rows)
                hot = target == tall(hi, n)
                for c in channels:
                    value = load(recv_ref, slot * CHANNELS + c)
                    lead = value.astype(bf16)
                    rest = (value - lead.astype(f32)).astype(bf16)
                    pieces.append(jnp.where(hot, tall(lead, n), zero))
                    pieces.append(jnp.where(hot, tall(rest, n), zero))
                if count:
                    pieces.append(jnp.where(hot, one, zero))
            left.append(jnp.concatenate(pieces, axis=0))
            right.append(jnp.where(lo_iota == tall(load(lo_ref, slot).astype(bf16), lo_n), one, zero))
        acc_ref[...] += lax.dot_general(
            jnp.concatenate(left, axis=1),
            jnp.concatenate(right, axis=1),
            (((1,), (1,)), ((), ())),
            preferred_element_type=f32,
        )
        return carry

    lax.fori_loop(0, slots // per_step, step, 0)
    sums, start = [], 0
    for rows, channels, count in groups:
        n = 8 * len(rows)
        found = []
        for _ in channels:
            found.append(acc_ref[start : start + n, :] + acc_ref[start + n : start + 2 * n, :])
            start += 2 * n
        if count:
            found.append(acc_ref[start : start + n, :])
            start += n
        sums.append(found)
    return sums


def keep_tiles(ref, k, value):
    for t in range(ref.shape[1]):
        ref[k, t] = value[:, t * 128 : (t + 1) * 128]


def load_rows(ref, k, t, row):
    return ref[k, t, pl.ds(row, ref.shape[2] // 8, stride=8), :]


def store_rows(ref, k, row, value):
    for t in range(ref.shape[1]):
        ref[k, t, pl.ds(row, ref.shape[2] // 8, stride=8), :] = value[:, t * 128 : (t + 1) * 128]


ALL = tuple(range(8))
EDGES = (0, 7)
INNER = (1, 2, 3, 4, 5, 6)
FIELDS = ((0, 1, 2), True)


def first_kernel(
    recv_ref, rhs_ref, perm_ref, r1_ref, edge_ref, pair_ref, other_ref, hi_ref, lo_ref, acc_ref, tile_ref
):
    incident, fields = scatter_slots(recv_ref, hi_ref, lo_ref, acc_ref, ((ALL, (3, 4), False), (EDGES,) + FIELDS))
    planes = perm_ref.shape[0] // 8
    for k in range(2):
        for r in range(8):
            store_rows(tile_ref, k, r, incident[k][r * planes : (r + 1) * planes])
    for k in range(2):
        inc = jnp.concatenate([tile_ref[k, t] for t in range(tile_ref.shape[1])], axis=1)
        value = rhs_ref[k] - inc
        r1_ref[k] = value
        keep_tiles(tile_ref, k, value)
    keep_tiles(tile_ref, 2, perm_ref[...])
    fields = [TAU * fields[3]] + fields[:3]
    for k in range(4):
        edge_ref[k] = fields[k]
    place = lax.axis_index("gx")
    even = lax.rem(place, 2) == 0
    top, bottom = place == 0, place == lax.axis_size("gx") - 1
    for t in range(tile_ref.shape[1]):
        lanes = slice(t * 128, (t + 1) * 128)
        for c in range(7):
            for k in range(3 if c < 3 else 1):
                if c < 3:
                    item = 3 * c + k
                    first, last = load_rows(tile_ref, c, t, k), load_rows(tile_ref, c, t, 5 + k)
                else:
                    item = 6 + c
                    first, last = fields[c - 3][0:planes, lanes], fields[c - 3][planes : 2 * planes, lanes]
                if c == 2:
                    first, last = jnp.where(top, 0.0, first), jnp.where(bottom, 0.0, last)
                rows = slice(item * planes, (item + 1) * planes)
                pair_ref[rows, lanes] = jnp.where(even, last, first)
                other_ref[rows, lanes] = jnp.where(even, first, last)


def second_kernel(recv_ref, edge_ref, wn_ref, hi_ref, lo_ref, acc_ref):
    (fields,) = scatter_slots(recv_ref, hi_ref, lo_ref, acc_ref, ((INNER,) + FIELDS,))
    planes = edge_ref.shape[1] // 2
    for k, value in enumerate([TAU * fields[3]] + fields[:3]):
        for j, r in enumerate(EDGES):
            store_rows(wn_ref, k, r, edge_ref[k, j * planes : (j + 1) * planes])
        for j, r in enumerate(INNER):
            store_rows(wn_ref, k, r, value[j * planes : (j + 1) * planes])


COL_PLACE = ((0, 3), (3, 3), (6, 3), (9, 1), (10, 1), (11, 1), (12, 1))


def strip_kernel(r1_ref, perm_ref, wn_ref, pair_ref, other_ref, out_pair_ref, out_other_ref, halo_ref):
    planes = perm_ref.shape[0] // 8
    lo_n = perm_ref.shape[1]
    even = lax.rem(lax.axis_index("gx"), 2) == 0
    halo_ref[...] = jnp.zeros(halo_ref.shape, f32)
    for c in range(7):
        width = 3 if c < 3 else 1
        for k in range(width):
            item = 3 * c + k if c < 3 else 6 + c
            rows = slice(item * planes, (item + 1) * planes)
            pair, other = pair_ref[rows, :], other_ref[rows, :]
            store_rows(halo_ref, c, k, jnp.where(even, pair, other))
            store_rows(halo_ref, c, 8 - width + k, jnp.where(even, other, pair))
    lane = lax.broadcasted_iota(jnp.int32, (planes, 16, 128), 2)
    position = lax.axis_index("gy")
    even = lax.rem(position, 2) == 0
    last = lax.axis_size("gy") - 1
    nothing = jnp.zeros((planes, 8, 128), f32)
    strips = []
    for start, sign, edge in ((0, 1, 0), (lo_n - 128, -1, last)):
        place = lane if sign > 0 else 127 - lane
        strip = jnp.zeros((planes, 16, 128), f32)
        for c in range(7):
            if c < 3:
                own = perm_ref[:, pl.ds(start, 128)] if c == 2 else r1_ref[c, :, pl.ds(start, 128)]
                other = halo_ref[c, start // 128].reshape(planes, 8, 128)
            else:
                own, other = wn_ref[c - 3, start // 128], nothing
            full = jnp.concatenate([own.reshape(planes, 8, 128), other], axis=1)
            offset, width = COL_PLACE[c]
            moved = pltpu.roll(full, (sign * offset) % 128, axis=2)
            strip = jnp.where((place >= offset) & (place < offset + width), moved, strip)
        strips.append(jnp.where(position == edge, 0.0, strip))
    out_pair_ref[...] = jnp.where(even, strips[1], strips[0])
    out_other_ref[...] = jnp.where(even, strips[0], strips[1])


def final_kernel(r1_ref, perm_ref, wn_ref, halo_ref, pair_ref, other_ref, sol_ref, res_ref):
    planes = perm_ref.shape[0] // 8
    lo_n = perm_ref.shape[1]
    wide = lo_n + 128
    lane = lax.broadcasted_iota(jnp.int32, (planes, 16, 128), 2)
    even = lax.rem(lax.axis_index("gy"), 2) == 0
    pair, other_pair = pair_ref[...], other_ref[...]
    from_right = jnp.where(even, pair, other_pair)
    from_left = jnp.where(even, other_pair, pair)

    def joined(ref, k):
        tiles = [ref[k, t].reshape(planes, 8, 128) for t in range(lo_n // 128)]
        return jnp.concatenate(tiles, axis=2)

    def extended(c):
        if c < 3:
            own = (perm_ref[...] if c == 2 else r1_ref[c]).reshape(planes, 8, lo_n)
        else:
            own = joined(wn_ref, c - 3)
        body = jnp.concatenate([own, joined(halo_ref, c)], axis=1)
        offset, width = COL_PLACE[c]
        right = pltpu.roll(from_right, (-offset) % 128, axis=2)
        left = pltpu.roll(from_left, offset, axis=2)
        side = jnp.where(lane < width, right, jnp.where(lane >= 128 - width, left, 0.0))
        return jnp.concatenate([body, side], axis=2)

    re, im, perm, w, nz, nx, ny = [extended(c) for c in range(7)]
    diag = 6.0 - K_SQUARED * perm
    shift = BETA * K_SQUARED * perm
    denom = diag * diag + shift * shift
    inside = perm > 0.5
    inv_re = jnp.where(inside, OMEGA * diag / denom, 0.0)
    inv_im = jnp.where(inside, -OMEGA * shift / denom, 0.0)

    def damp(a, b):
        return a * inv_re - b * inv_im, a * inv_im + b * inv_re

    def sides(v):
        nothing = jnp.zeros((1,) + v.shape[1:], f32)
        after = jnp.concatenate([v[1:], nothing], axis=0)
        before = jnp.concatenate([nothing, v[:-1]], axis=0)
        return (
            (after, before),
            (pltpu.roll(v, 15, axis=1), pltpu.roll(v, 1, axis=1)),
            (pltpu.roll(v, wide - 1, axis=2), pltpu.roll(v, 1, axis=2)),
        )

    def helm(v, pairs):
        total = pairs[0][0] + pairs[0][1]
        for a, b in pairs[1:]:
            total = total + a + b
        return diag * v - total

    def swept(a, b):
        za, zb = damp(a, b)
        ma = helm(za, sides(za)) - shift * zb
        mb = helm(zb, sides(zb)) + shift * za
        da, db = damp(a - ma, b - mb)
        return za + da, zb + db

    def surface(v, pairs):
        (a, b), (c, d), (e, f) = pairs
        return w * v + nz * (a - b) + nx * (c - d) + ny * (e - f)

    def remaining(r, v):
        pairs = sides(v)
        return r - helm(v, pairs) - surface(v, pairs)

    sa, sb = swept(re, im)
    ra, rb = remaining(re, sa), remaining(im, sb)
    ua, ub = swept(ra, rb)
    res_ref[0] = ra[:, 0:8, 0:lo_n]
    res_ref[1] = rb[:, 0:8, 0:lo_n]
    sol_ref[0] = (sa + ua)[:, 0:8, 0:lo_n]
    sol_ref[1] = (sb + ub)[:, 0:8, 0:lo_n]


def in_vmem(n):
    return [pl.BlockSpec(memory_space=pltpu.VMEM)] * n


def shape(*dims):
    return jax.ShapeDtypeStruct(dims, f32)


def per_device(rhs_field, permittivity, surf_dist, surf_normal, surf_inc, surf_cell, surf_mask, surf_owner):
    planes, rows, cols = permittivity.shape
    blocks, points = surf_cell.shape
    gx, gy = lax.axis_size("gx"), lax.axis_size("gy")
    devices = gx * gy
    slots = devices * CAP
    params = pltpu.CompilerParams(vmem_limit_bytes=48 << 20)
    send = pl.pallas_call(
        pack_kernel,
        out_shape=shape(slots * CHANNELS, points),
        in_specs=[pl.BlockSpec(memory_space=pltpu.HBM)] * 6,
        out_specs=pl.BlockSpec(memory_space=pltpu.VMEM),
        scratch_shapes=[
            pltpu.SMEM((blocks,), jnp.int32),
            pltpu.SMEM((blocks,), jnp.int32),
            pltpu.SMEM((devices,), jnp.int32),
            pltpu.VMEM((blocks, points), f32),
            pltpu.VMEM((CHANNELS, blocks, points), f32),
            pltpu.VMEM((blocks, points), jnp.int32),
            pltpu.VMEM((blocks, points), jnp.int32),
            pltpu.SemaphoreType.DMA((6,)),
        ],
        compiler_params=params,
        name="pack",
    )(*[
        pltpu.with_memory_space_constraint(x, pltpu.HBM)
        for x in (surf_owner[:, 0], surf_dist, surf_normal, surf_inc, surf_cell, surf_mask)
    ])
    recv = lax.all_to_all(send.reshape(-1), ("gx", "gy"), split_axis=0, concat_axis=0, tiled=True)
    recv = recv.reshape(slots * CHANNELS, points)
    cells = planes * rows
    rhs_field = rhs_field.reshape(2, cells, cols)
    permittivity = permittivity.reshape(cells, cols)

    tiles = cols // 128

    def scatter_scratch(parts):
        return [
            pltpu.VMEM((slots, points), f32),
            pltpu.VMEM((slots, points), f32),
            pltpu.VMEM((parts, cols), f32),
        ]

    def cost(parts):
        flops = 2 * parts * cols * slots * points
        return pl.CostEstimate(flops=flops, transcendentals=0, bytes_accessed=slots * CHANNELS * points * 4)

    strip = shape(13 * planes, cols)
    parts = 4 * cells + 14 * planes
    r1, edges, pair, other = pl.pallas_call(
        first_kernel,
        out_shape=(shape(2, cells, cols), shape(4, 2 * planes, cols), strip, strip),
        in_specs=in_vmem(3),
        out_specs=tuple(in_vmem(4)),
        scratch_shapes=scatter_scratch(parts) + [pltpu.VMEM((3, tiles, cells, 128), f32)],
        compiler_params=params,
        cost_estimate=cost(parts),
        name="first",
    )(recv, rhs_field, permittivity)
    from_pair = lax.ppermute(pair, "gx", [(i, i ^ 1) for i in range(gx)])
    from_other = lax.ppermute(other, "gx", [(i, (((i + 1) ^ 1) - 1) % gx) for i in range(gx)])
    parts = 7 * 6 * planes
    wn = pl.pallas_call(
        second_kernel,
        out_shape=shape(4, tiles, cells, 128),
        in_specs=in_vmem(2),
        out_specs=in_vmem(1)[0],
        scratch_shapes=scatter_scratch(parts),
        compiler_params=params,
        cost_estimate=cost(parts),
        name="second",
    )(recv, edges)
    pair, other, halo = pl.pallas_call(
        strip_kernel,
        out_shape=(shape(planes, 16, 128), shape(planes, 16, 128), shape(7, tiles, cells, 128)),
        in_specs=in_vmem(5),
        out_specs=tuple(in_vmem(3)),
        compiler_params=params,
        name="strips",
    )(r1, permittivity, wn, from_pair, from_other)
    from_pair = lax.ppermute(pair, "gy", [(i, i ^ 1) for i in range(gy)])
    from_other = lax.ppermute(other, "gy", [(i, (((i + 1) ^ 1) - 1) % gy) for i in range(gy)])
    field = shape(2, planes, rows, cols)
    return pl.pallas_call(
        final_kernel,
        out_shape=(field, field),
        in_specs=in_vmem(6),
        out_specs=tuple(in_vmem(2)),
        compiler_params=params,
        name="final",
    )(r1, permittivity, wn, halo, from_pair, from_other)


def solution(mesh):
    split = ("gx", "gy")
    placed = (
        P(None, None, "gx", "gy"),
        P(None, "gx", "gy"),
        P(split, None),
        P(None, split, None),
        P(None, split, None),
        P(split, None),
        P(split, None),
        P(split, None),
    )
    return jax.shard_map(
        per_device,
        mesh=mesh,
        in_specs=placed,
        out_specs=(P(None, None, "gx", "gy"), P(None, None, "gx", "gy")),
        check_vma=False,
    )
```

```python
import functools

import jax
import jax.numpy as jnp
from jax import lax
from jax.experimental import pallas as pl
from jax.experimental.pallas import tpu as pltpu
from jax.sharding import PartitionSpec as P

CAP = 2
K_SQUARED = 0.25
BETA = 0.5
OMEGA = 0.8
TAU = 1.0

CHANNELS = 6
GROUP = 128

f32 = jnp.float32
bf16 = jnp.bfloat16


def pack_kernel(
    owner_hbm, dist_hbm, normal_hbm, inc_hbm, cell_hbm, mask_hbm, out_ref,
    owner_ref, base_ref, count_ref, dist_ref, coef_ref, cell_ref, mask_ref, sems,
):
    blocks = dist_ref.shape[0]
    devices = count_ref.shape[0]
    copies = [
        pltpu.make_async_copy(owner_hbm, owner_ref, sems.at[0]),
        pltpu.make_async_copy(dist_hbm, dist_ref, sems.at[1]),
        pltpu.make_async_copy(normal_hbm, coef_ref.at[pl.ds(0, 3)], sems.at[2]),
        pltpu.make_async_copy(inc_hbm, coef_ref.at[pl.ds(3, 2)], sems.at[3]),
        pltpu.make_async_copy(cell_hbm, cell_ref, sems.at[4]),
        pltpu.make_async_copy(mask_hbm, mask_ref, sems.at[5]),
    ]
    for copy in copies:
        copy.start()
    out_ref[...] = jnp.full(out_ref.shape, -1.0, f32)

    def clear(i, carry):
        count_ref[i] = 0
        return carry

    lax.fori_loop(0, devices, clear, 0, unroll=8)
    copies[0].wait()

    def rank(b, carry):
        owner = owner_ref[b]
        seen = count_ref[owner]
        count_ref[owner] = seen + 1
        base_ref[b] = (owner * CAP + seen) * CHANNELS
        return carry

    lax.fori_loop(0, blocks, rank, 0, unroll=8)
    for copy in copies[1:]:
        copy.wait()
    half = 0.5 * TAU * dist_ref[...]
    for k in range(3):
        coef_ref[k] = half * coef_ref[k]
    for k in range(3, 5):
        coef_ref[k] = TAU * coef_ref[k]
    coef_ref[5] = jnp.where(mask_ref[...] > 0, cell_ref[...], 1 << 14).astype(f32)

    def place(b, carry):
        base = base_ref[b]
        for c in range(CHANNELS):
            out_ref[pl.ds(base + c, 1), :] = coef_ref[c, pl.ds(b, 1), :]
        return carry

    lax.fori_loop(0, blocks, place, 0, unroll=8)


def split_cells(recv_ref, hi_ref, lo_ref):
    slots = hi_ref.shape[0]
    chunk = min(64, slots)
    for i in range(0, slots, chunk):
        cell = recv_ref[pl.ds(i * CHANNELS + CHANNELS - 1, chunk, stride=CHANNELS), :].astype(jnp.int32)
        hi_ref[i : i + chunk] = (cell >> 8).astype(f32)
        lo_ref[i : i + chunk] = (cell & 255).astype(f32)


def scatter_slots(recv_ref, hi_ref, lo_ref, acc_ref, groups):
    slots = hi_ref.shape[0]
    lo_n = acc_ref.shape[1]
    per_step = min(GROUP, slots)
    one = jnp.ones((), bf16)
    zero = jnp.zeros((), bf16)
    targets = []
    for rows, _, _ in groups:
        place = lax.broadcasted_iota(jnp.int32, (8 * len(rows), 128), 0)
        item = place >> 3
        row = jnp.zeros_like(place)
        for k, r in enumerate(rows):
            row = jnp.where(item == k, r, row)
        targets.append(((place & 7) * 8 + row).astype(f32).astype(bf16))
    lo_iota = lax.broadcasted_iota(jnp.int32, (lo_n, 128), 0).astype(f32).astype(bf16)

    def load(ref, index):
        return jnp.broadcast_to(ref[pl.ds(index, 1), :], (16, 128))

    def tall(tile, n):
        return jnp.concatenate([tile] * (n // 16), axis=0)

    def step(g):
        left, right = [], []
        for j in range(per_step):
            slot = g * per_step + j
            hi = load(hi_ref, slot).astype(bf16)
            pieces = []
            for target, (rows, channels, count) in zip(targets, groups):
                n = 8 * len(rows)
                hot = target == tall(hi, n)
                for c in channels:
                    value = load(recv_ref, slot * CHANNELS + c)
                    lead = value.astype(bf16)
                    rest = (value - lead.astype(f32)).astype(bf16)
                    pieces.append(jnp.where(hot, tall(lead, n), zero))
                    pieces.append(jnp.where(hot, tall(rest, n), zero))
                if count:
                    pieces.append(jnp.where(hot, one, zero))
            left.append(jnp.concatenate(pieces, axis=0))
            right.append(jnp.where(lo_iota == tall(load(lo_ref, slot).astype(bf16), lo_n), one, zero))
        total = lax.dot_general(
            jnp.concatenate(left, axis=1),
            jnp.concatenate(right, axis=1),
            (((1,), (1,)), ((), ())),
            preferred_element_type=f32,
        )
        acc_ref[...] = total if g == 0 else acc_ref[...] + total

    for g in range(slots // per_step):
        step(g)
    sums, start = [], 0
    for rows, channels, count in groups:
        n = 8 * len(rows)
        found = []
        for _ in channels:
            found.append(acc_ref[start : start + n, :] + acc_ref[start + n : start + 2 * n, :])
            start += 2 * n
        if count:
            found.append(acc_ref[start : start + n, :])
            start += n
        sums.append(found)
    return sums


def keep_tiles(ref, k, value):
    for t in range(ref.shape[1]):
        ref[k, t] = value[:, t * 128 : (t + 1) * 128]


def load_rows(ref, k, t, row):
    return ref[k, t, pl.ds(row, ref.shape[2] // 8, stride=8), :]


def store_rows(ref, k, row, value):
    for t in range(ref.shape[1]):
        ref[k, t, pl.ds(row, ref.shape[2] // 8, stride=8), :] = value[:, t * 128 : (t + 1) * 128]


ALL = tuple(range(8))
EDGES = (0, 7)
INNER = (1, 2, 3, 4, 5, 6)
FIELDS = ((0, 1, 2), True)


def first_kernel(
    recv_ref, rhs_ref, perm_ref, r1_ref, edge_ref, pair_ref, other_ref, hi_ref, lo_ref, acc_ref, tile_ref
):
    split_cells(recv_ref, hi_ref, lo_ref)
    incident, fields = scatter_slots(recv_ref, hi_ref, lo_ref, acc_ref, ((ALL, (3, 4), False), (EDGES,) + FIELDS))
    planes = perm_ref.shape[0] // 8
    for k in range(2):
        for r in range(8):
            store_rows(tile_ref, k, r, incident[k][r * planes : (r + 1) * planes])
    for k in range(2):
        inc = jnp.concatenate([tile_ref[k, t] for t in range(tile_ref.shape[1])], axis=1)
        value = rhs_ref[k] - inc
        r1_ref[k] = value
        keep_tiles(tile_ref, k, value)
    keep_tiles(tile_ref, 2, perm_ref[...])
    fields = [TAU * fields[3]] + fields[:3]
    for k in range(4):
        edge_ref[k] = fields[k]
    place = lax.axis_index("gx")
    even = lax.rem(place, 2) == 0
    top, bottom = place == 0, place == lax.axis_size("gx") - 1
    for t in range(tile_ref.shape[1]):
        lanes = slice(t * 128, (t + 1) * 128)
        for c in range(7):
            for k in range(3 if c < 3 else 1):
                if c < 3:
                    item = 3 * c + k
                    first, last = load_rows(tile_ref, c, t, k), load_rows(tile_ref, c, t, 5 + k)
                else:
                    item = 6 + c
                    first, last = fields[c - 3][0:planes, lanes], fields[c - 3][planes : 2 * planes, lanes]
                if c == 2:
                    first, last = jnp.where(top, 0.0, first), jnp.where(bottom, 0.0, last)
                rows = slice(item * planes, (item + 1) * planes)
                pair_ref[rows, lanes] = jnp.where(even, last, first)
                other_ref[rows, lanes] = jnp.where(even, first, last)


def second_kernel(recv_ref, hi_ref, lo_ref, edge_ref, wn_ref, acc_ref):
    (fields,) = scatter_slots(recv_ref, hi_ref, lo_ref, acc_ref, ((INNER,) + FIELDS,))
    planes = edge_ref.shape[1] // 2
    for k, value in enumerate([TAU * fields[3]] + fields[:3]):
        for j, r in enumerate(EDGES):
            store_rows(wn_ref, k, r, edge_ref[k, j * planes : (j + 1) * planes])
        for j, r in enumerate(INNER):
            store_rows(wn_ref, k, r, value[j * planes : (j + 1) * planes])


COL_PLACE = ((0, 3), (3, 3), (6, 3), (9, 1), (10, 1), (11, 1), (12, 1))


def strip_kernel(r1_ref, perm_ref, wn_ref, pair_ref, other_ref, out_pair_ref, out_other_ref, halo_ref):
    planes = perm_ref.shape[0] // 8
    lo_n = perm_ref.shape[1]
    even = lax.rem(lax.axis_index("gx"), 2) == 0
    halo_ref[...] = jnp.zeros(halo_ref.shape, f32)
    for c in range(7):
        width = 3 if c < 3 else 1
        for k in range(width):
            item = 3 * c + k if c < 3 else 6 + c
            rows = slice(item * planes, (item + 1) * planes)
            pair, other = pair_ref[rows, :], other_ref[rows, :]
            store_rows(halo_ref, c, k, jnp.where(even, pair, other))
            store_rows(halo_ref, c, 8 - width + k, jnp.where(even, other, pair))
    lane = lax.broadcasted_iota(jnp.int32, (planes, 16, 128), 2)
    position = lax.axis_index("gy")
    even = lax.rem(position, 2) == 0
    last = lax.axis_size("gy") - 1
    nothing = jnp.zeros((planes, 8, 128), f32)
    strips = []
    for start, sign, edge in ((0, 1, 0), (lo_n - 128, -1, last)):
        place = lane if sign > 0 else 127 - lane
        strip = jnp.zeros((planes, 16, 128), f32)
        for c in range(7):
            if c < 3:
                own = perm_ref[:, pl.ds(start, 128)] if c == 2 else r1_ref[c, :, pl.ds(start, 128)]
                other = halo_ref[c, start // 128].reshape(planes, 8, 128)
            else:
                own, other = wn_ref[c - 3, start // 128], nothing
            full = jnp.concatenate([own.reshape(planes, 8, 128), other], axis=1)
            offset, width = COL_PLACE[c]
            moved = pltpu.roll(full, (sign * offset) % 128, axis=2)
            strip = jnp.where((place >= offset) & (place < offset + width), moved, strip)
        strips.append(jnp.where(position == edge, 0.0, strip))
    out_pair_ref[...] = jnp.where(even, strips[1], strips[0])
    out_other_ref[...] = jnp.where(even, strips[0], strips[1])


def iterate(re, im, perm, w, nz, nx, ny):
    rows, cols = perm.shape[1:]
    diag = 6.0 - K_SQUARED * perm
    shift = BETA * K_SQUARED * perm
    inside = perm > 0.5
    inverse = jnp.where(inside, OMEGA / (diag * diag + shift * shift), 0.0)
    inv_re = diag * inverse
    inv_im = -shift * inverse

    def damp(a, b):
        return a * inv_re - b * inv_im, a * inv_im + b * inv_re

    def sides(v):
        nothing = jnp.zeros((1,) + v.shape[1:], f32)
        after = jnp.concatenate([v[1:], nothing], axis=0)
        before = jnp.concatenate([nothing, v[:-1]], axis=0)
        return (
            (after, before),
            (pltpu.roll(v, rows - 1, axis=1), pltpu.roll(v, 1, axis=1)),
            (pltpu.roll(v, cols - 1, axis=2), pltpu.roll(v, 1, axis=2)),
        )

    def helm(v, pairs):
        total = pairs[0][0] + pairs[0][1]
        for a, b in pairs[1:]:
            total = total + a + b
        return diag * v - total

    def swept(a, b):
        za, zb = damp(a, b)
        ma = helm(za, sides(za)) - shift * zb
        mb = helm(zb, sides(zb)) + shift * za
        da, db = damp(a - ma, b - mb)
        return za + da, zb + db

    def surface(v, pairs):
        (a, b), (c, d), (e, f) = pairs
        return w * v + nz * (a - b) + nx * (c - d) + ny * (e - f)

    def remaining(r, v):
        pairs = sides(v)
        return r - helm(v, pairs) - surface(v, pairs)

    sa, sb = swept(re, im)
    ra, rb = remaining(re, sa), remaining(im, sb)
    ua, ub = swept(ra, rb)
    return sa + ua, sb + ub, ra, rb


def tile_of(c, t, r1_ref, perm_ref, wn_ref, halo_ref):
    planes = perm_ref.shape[0] // 8
    lanes = slice(t * 128, (t + 1) * 128)
    if c < 3:
        own = perm_ref[:, lanes] if c == 2 else r1_ref[c, :, lanes]
    else:
        own = wn_ref[c - 3, t]
    return jnp.concatenate([own.reshape(planes, 8, 128), halo_ref[c, t].reshape(planes, 8, 128)], axis=1)


def inner_kernel(r1_ref, perm_ref, wn_ref, halo_ref, sol_ref, res_ref):
    tiles = halo_ref.shape[1]
    fields = [
        jnp.concatenate([tile_of(c, t, r1_ref, perm_ref, wn_ref, halo_ref) for t in range(tiles)], axis=2)
        for c in range(7)
    ]
    sa, sb, ra, rb = iterate(*fields)
    for k, (sol, res) in enumerate(((sa, ra), (sb, rb))):
        sol_ref[k] = sol[:, 0:8, :]
        res_ref[k] = res[:, 0:8, :]


def final_kernel(
    r1_ref, perm_ref, wn_ref, halo_ref, sol_in_ref, res_in_ref, pair_ref, other_ref, sol_ref, res_ref
):
    planes = perm_ref.shape[0] // 8
    last = halo_ref.shape[1] - 1
    lane = lax.broadcasted_iota(jnp.int32, (planes, 16, 128), 2)
    even = lax.rem(lax.axis_index("gy"), 2) == 0
    pair, other = pair_ref[...], other_ref[...]
    from_right = jnp.where(even, pair, other)
    from_left = jnp.where(even, other, pair)
    fields = []
    for c in range(7):
        offset, width = COL_PLACE[c]
        args = (r1_ref, perm_ref, wn_ref, halo_ref)
        field = jnp.where(lane < 56, tile_of(c, 0, *args), 0.0)
        field = jnp.where((lane >= 60) & (lane < 116), pltpu.roll(tile_of(c, last, *args), 116, axis=2), field)
        field = jnp.where((lane >= 116) & (lane < 116 + width), pltpu.roll(from_right, 116 - offset, axis=2), field)
        field = jnp.where(lane >= 128 - width, pltpu.roll(from_left, offset, axis=2), field)
        fields.append(field)
    sa, sb, ra, rb = iterate(*fields)
    near = lane[:, 0:8, :]
    for k, (sol, res) in enumerate(((sa, ra), (sb, rb))):
        for out_ref, in_ref, value in ((sol_ref, sol_in_ref, sol), (res_ref, res_in_ref, res)):
            value = value[:, 0:8, :]
            for t in range(last + 1):
                lanes = slice(t * 128, (t + 1) * 128)
                tile = in_ref[k, :, :, lanes]
                if t == 0:
                    tile = jnp.where(near < 8, value, tile)
                if t == last:
                    tile = jnp.where(near >= 120, pltpu.roll(value, 12, axis=2), tile)
                out_ref[k, :, :, lanes] = tile


def in_vmem(n):
    return [pl.BlockSpec(memory_space=pltpu.VMEM)] * n


def shape(*dims):
    return jax.ShapeDtypeStruct(dims, f32)


def per_device(rhs_field, permittivity, surf_dist, surf_normal, surf_inc, surf_cell, surf_mask, surf_owner):
    planes, rows, cols = permittivity.shape
    blocks, points = surf_cell.shape
    gx, gy = lax.axis_size("gx"), lax.axis_size("gy")
    devices = gx * gy
    slots = devices * CAP
    params = pltpu.CompilerParams(vmem_limit_bytes=48 << 20)
    send = pl.pallas_call(
        pack_kernel,
        out_shape=shape(slots * CHANNELS, points),
        in_specs=[pl.BlockSpec(memory_space=pltpu.HBM)] * 6,
        out_specs=pl.BlockSpec(memory_space=pltpu.VMEM),
        scratch_shapes=[
            pltpu.SMEM((blocks,), jnp.int32),
            pltpu.SMEM((blocks,), jnp.int32),
            pltpu.SMEM((devices,), jnp.int32),
            pltpu.VMEM((blocks, points), f32),
            pltpu.VMEM((CHANNELS, blocks, points), f32),
            pltpu.VMEM((blocks, points), jnp.int32),
            pltpu.VMEM((blocks, points), jnp.int32),
            pltpu.SemaphoreType.DMA((6,)),
        ],
        compiler_params=params,
        name="pack",
    )(*[
        pltpu.with_memory_space_constraint(x, pltpu.HBM)
        for x in (surf_owner[:, 0], surf_dist, surf_normal, surf_inc, surf_cell, surf_mask)
    ])
    recv = lax.all_to_all(send.reshape(-1), ("gx", "gy"), split_axis=0, concat_axis=0, tiled=True)
    recv = recv.reshape(slots * CHANNELS, points)
    cells = planes * rows
    rhs_field = rhs_field.reshape(2, cells, cols)
    permittivity = permittivity.reshape(cells, cols)

    tiles = cols // 128

    def cost(parts):
        flops = 2 * parts * cols * slots * points
        return pl.CostEstimate(flops=flops, transcendentals=0, bytes_accessed=slots * CHANNELS * points * 4)

    strip = shape(13 * planes, cols)
    parts = 4 * cells + 14 * planes
    local = shape(slots, points)
    r1, edges, pair, other, hi, lo = pl.pallas_call(
        first_kernel,
        out_shape=(shape(2, cells, cols), shape(4, 2 * planes, cols), strip, strip, local, local),
        in_specs=in_vmem(3),
        out_specs=tuple(in_vmem(6)),
        scratch_shapes=[pltpu.VMEM((parts, cols), f32), pltpu.VMEM((3, tiles, cells, 128), f32)],
        compiler_params=params,
        cost_estimate=cost(parts),
        name="first",
    )(recv, rhs_field, permittivity)
    from_pair = lax.ppermute(pair, "gx", [(i, i ^ 1) for i in range(gx)])
    from_other = lax.ppermute(other, "gx", [(i, (((i + 1) ^ 1) - 1) % gx) for i in range(gx)])
    parts = 7 * 6 * planes
    wn = pl.pallas_call(
        second_kernel,
        out_shape=shape(4, tiles, cells, 128),
        in_specs=in_vmem(4),
        out_specs=in_vmem(1)[0],
        scratch_shapes=[pltpu.VMEM((parts, cols), f32)],
        compiler_params=params,
        cost_estimate=cost(parts),
        name="second",
    )(recv, hi, lo, edges)
    pair, other, halo = pl.pallas_call(
        strip_kernel,
        out_shape=(shape(planes, 16, 128), shape(planes, 16, 128), shape(7, tiles, cells, 128)),
        in_specs=in_vmem(5),
        out_specs=tuple(in_vmem(3)),
        compiler_params=params,
        name="strips",
    )(r1, permittivity, wn, from_pair, from_other)
    from_pair = lax.ppermute(pair, "gy", [(i, i ^ 1) for i in range(gy)])
    from_other = lax.ppermute(other, "gy", [(i, (((i + 1) ^ 1) - 1) % gy) for i in range(gy)])
    field = shape(2, planes, rows, cols)
    sol, res = pl.pallas_call(
        inner_kernel,
        out_shape=(field, field),
        in_specs=in_vmem(4),
        out_specs=tuple(in_vmem(2)),
        compiler_params=params,
        cost_estimate=cost(8 * planes),
        name="inner",
    )(r1, permittivity, wn, halo)
    return pl.pallas_call(
        final_kernel,
        out_shape=(field, field),
        in_specs=in_vmem(8),
        out_specs=tuple(in_vmem(2)),
        compiler_params=params,
        name="final",
    )(r1, permittivity, wn, halo, sol, res, from_pair, from_other)


def solution(mesh):
    split = ("gx", "gy")
    placed = (
        P(None, None, "gx", "gy"),
        P(None, "gx", "gy"),
        P(split, None),
        P(None, split, None),
        P(None, split, None),
        P(split, None),
        P(split, None),
        P(split, None),
    )
    return jax.shard_map(
        per_device,
        mesh=mesh,
        in_specs=placed,
        out_specs=(P(None, None, "gx", "gy"), P(None, None, "gx", "gy")),
        check_vma=False,
    )
```

```python
import functools

import jax
import jax.numpy as jnp
from jax import lax
from jax.experimental import pallas as pl
from jax.experimental.pallas import tpu as pltpu
from jax.sharding import PartitionSpec as P

CAP = 2
K_SQUARED = 0.25
BETA = 0.5
OMEGA = 0.8
TAU = 1.0

CHANNELS = 6
GROUP = 128

f32 = jnp.float32
bf16 = jnp.bfloat16


def pack_kernel(
    owner_hbm, dist_hbm, normal_hbm, inc_hbm, cell_hbm, mask_hbm, out_ref,
    owner_ref, base_ref, count_ref, dist_ref, raw_ref, coef_ref, cell_ref, mask_ref, sems,
):
    blocks = dist_ref.shape[0]
    devices = count_ref.shape[0]
    copies = [
        pltpu.make_async_copy(owner_hbm, owner_ref, sems.at[0]),
        pltpu.make_async_copy(dist_hbm, dist_ref, sems.at[1]),
        pltpu.make_async_copy(normal_hbm, raw_ref.at[pl.ds(0, 3)], sems.at[2]),
        pltpu.make_async_copy(inc_hbm, raw_ref.at[pl.ds(3, 2)], sems.at[3]),
        pltpu.make_async_copy(cell_hbm, cell_ref, sems.at[4]),
        pltpu.make_async_copy(mask_hbm, mask_ref, sems.at[5]),
    ]
    for copy in copies:
        copy.start()
    out_ref[...] = jnp.full(out_ref.shape, -1.0, f32)

    def clear(i, carry):
        count_ref[i] = 0
        return carry

    lax.fori_loop(0, devices, clear, 0, unroll=8)
    copies[0].wait()

    def rank(b, carry):
        owner = owner_ref[b]
        seen = count_ref[owner]
        count_ref[owner] = seen + 1
        base_ref[b] = (owner * CAP + seen) * CHANNELS
        return carry

    lax.fori_loop(0, blocks, rank, 0, unroll=8)
    for copy in copies[1:]:
        copy.wait()
    half = 0.5 * TAU * dist_ref[...]
    for k in range(3):
        rows = slice(k * blocks, (k + 1) * blocks)
        coef_ref[rows] = half * raw_ref[k]
    for k in range(3, 5):
        coef_ref[k * blocks : (k + 1) * blocks] = TAU * raw_ref[k]
    coef_ref[5 * blocks : 6 * blocks] = jnp.where(mask_ref[...] > 0, cell_ref[...], 1 << 14).astype(f32)

    def place(b, carry):
        out_ref[pl.ds(base_ref[b], CHANNELS), :] = coef_ref[pl.ds(b, CHANNELS, stride=blocks), :]
        return carry

    lax.fori_loop(0, blocks, place, 0, unroll=8)


def split_cells(recv_ref, hi_ref, lo_ref):
    slots = hi_ref.shape[0]
    chunk = min(64, slots)
    for i in range(0, slots, chunk):
        cell = recv_ref[pl.ds(i * CHANNELS + CHANNELS - 1, chunk, stride=CHANNELS), :].astype(jnp.int32)
        hi_ref[i : i + chunk] = (cell >> 8).astype(f32)
        lo_ref[i : i + chunk] = (cell & 255).astype(f32)


def scatter_slots(recv_ref, hi_ref, lo_ref, acc_ref, groups):
    slots = hi_ref.shape[0]
    lo_n = acc_ref.shape[1]
    per_step = min(GROUP, slots)
    acc_ref[...] = jnp.zeros(acc_ref.shape, f32)
    one = jnp.ones((), bf16)
    zero = jnp.zeros((), bf16)
    targets = []
    for rows, _, _ in groups:
        place = lax.broadcasted_iota(jnp.int32, (8 * len(rows), 128), 0)
        item = place >> 3
        row = jnp.zeros_like(place)
        for k, r in enumerate(rows):
            row = jnp.where(item == k, r, row)
        targets.append(((place & 7) * 8 + row).astype(f32).astype(bf16))
    lo_iota = lax.broadcasted_iota(jnp.int32, (lo_n, 128), 0).astype(f32).astype(bf16)

    def load(ref, index):
        return jnp.broadcast_to(ref[pl.ds(index, 1), :], (16, 128))

    def tall(tile, n):
        return jnp.concatenate([tile] * (n // 16), axis=0)

    def step(g, carry):
        left, right = [], []
        for j in range(per_step):
            slot = g * per_step + j
            hi = load(hi_ref, slot).astype(bf16)
            pieces = []
            for target, (rows, channels, count) in zip(targets, groups):
                n = 8 * len(rows)
                hot = target == tall(hi, n)
                for c in channels:
                    value = load(recv_ref, slot * CHANNELS + c)
                    lead = value.astype(bf16)
                    rest = (value - lead.astype(f32)).astype(bf16)
                    pieces.append(jnp.where(hot, tall(lead, n), zero))
                    pieces.append(jnp.where(hot, tall(rest, n), zero))
                if count:
                    pieces.append(jnp.where(hot, one, zero))
            left.append(jnp.concatenate(pieces, axis=0))
            right.append(jnp.where(lo_iota == tall(load(lo_ref, slot).astype(bf16), lo_n), one, zero))
        acc_ref[...] += lax.dot_general(
            jnp.concatenate(left, axis=1),
            jnp.concatenate(right, axis=1),
            (((1,), (1,)), ((), ())),
            preferred_element_type=f32,
        )
        return carry

    lax.fori_loop(0, slots // per_step, step, 0)
    sums, start = [], 0
    for rows, channels, count in groups:
        n = 8 * len(rows)
        found = []
        for _ in channels:
            found.append(acc_ref[start : start + n, :] + acc_ref[start + n : start + 2 * n, :])
            start += 2 * n
        if count:
            found.append(acc_ref[start : start + n, :])
            start += n
        sums.append(found)
    return sums


def keep_tiles(ref, k, value):
    for t in range(ref.shape[1]):
        ref[k, t] = value[:, t * 128 : (t + 1) * 128]


def load_rows(ref, k, t, row):
    return ref[k, t, pl.ds(row, ref.shape[2] // 8, stride=8), :]


def store_rows(ref, k, row, value):
    for t in range(ref.shape[1]):
        ref[k, t, pl.ds(row, ref.shape[2] // 8, stride=8), :] = value[:, t * 128 : (t + 1) * 128]


ALL = tuple(range(8))
EDGES = (0, 7)
INNER = (1, 2, 3, 4, 5, 6)
FIELDS = ((0, 1, 2), True)


def first_kernel(
    recv_ref, rhs_ref, perm_ref, r1_ref, edge_ref, pair_ref, other_ref, hi_ref, lo_ref, acc_ref, tile_ref
):
    split_cells(recv_ref, hi_ref, lo_ref)
    incident, fields = scatter_slots(recv_ref, hi_ref, lo_ref, acc_ref, ((ALL, (3, 4), False), (EDGES,) + FIELDS))
    planes = perm_ref.shape[0] // 8
    for k in range(2):
        for r in range(8):
            store_rows(tile_ref, k, r, incident[k][r * planes : (r + 1) * planes])
    for k in range(2):
        inc = jnp.concatenate([tile_ref[k, t] for t in range(tile_ref.shape[1])], axis=1)
        value = rhs_ref[k] - inc
        r1_ref[k] = value
        keep_tiles(tile_ref, k, value)
    keep_tiles(tile_ref, 2, perm_ref[...])
    fields = [TAU * fields[3]] + fields[:3]
    for k in range(4):
        edge_ref[k] = fields[k]
    place = lax.axis_index("gx")
    even = lax.rem(place, 2) == 0
    top, bottom = place == 0, place == lax.axis_size("gx") - 1
    for t in range(tile_ref.shape[1]):
        lanes = slice(t * 128, (t + 1) * 128)
        for c in range(7):
            for k in range(3 if c < 3 else 1):
                if c < 3:
                    item = 3 * c + k
                    first, last = load_rows(tile_ref, c, t, k), load_rows(tile_ref, c, t, 5 + k)
                else:
                    item = 6 + c
                    first, last = fields[c - 3][0:planes, lanes], fields[c - 3][planes : 2 * planes, lanes]
                if c == 2:
                    first, last = jnp.where(top, 0.0, first), jnp.where(bottom, 0.0, last)
                rows = slice(item * planes, (item + 1) * planes)
                pair_ref[rows, lanes] = jnp.where(even, last, first)
                other_ref[rows, lanes] = jnp.where(even, first, last)


def second_kernel(recv_ref, hi_ref, lo_ref, edge_ref, wn_ref, acc_ref):
    (fields,) = scatter_slots(recv_ref, hi_ref, lo_ref, acc_ref, ((INNER,) + FIELDS,))
    planes = edge_ref.shape[1] // 2
    for k, value in enumerate([TAU * fields[3]] + fields[:3]):
        for j, r in enumerate(EDGES):
            store_rows(wn_ref, k, r, edge_ref[k, j * planes : (j + 1) * planes])
        for j, r in enumerate(INNER):
            store_rows(wn_ref, k, r, value[j * planes : (j + 1) * planes])


COL_PLACE = ((0, 3), (3, 3), (6, 3), (9, 1), (10, 1), (11, 1), (12, 1))


def strip_kernel(r1_ref, perm_ref, wn_ref, pair_ref, other_ref, out_pair_ref, out_other_ref, halo_ref):
    planes = perm_ref.shape[0] // 8
    lo_n = perm_ref.shape[1]
    even = lax.rem(lax.axis_index("gx"), 2) == 0
    halo_ref[...] = jnp.zeros(halo_ref.shape, f32)
    for c in range(7):
        width = 3 if c < 3 else 1
        for k in range(width):
            item = 3 * c + k if c < 3 else 6 + c
            rows = slice(item * planes, (item + 1) * planes)
            pair, other = pair_ref[rows, :], other_ref[rows, :]
            store_rows(halo_ref, c, k, jnp.where(even, pair, other))
            store_rows(halo_ref, c, 8 - width + k, jnp.where(even, other, pair))
    lane = lax.broadcasted_iota(jnp.int32, (planes, 16, 128), 2)
    position = lax.axis_index("gy")
    even = lax.rem(position, 2) == 0
    last = lax.axis_size("gy") - 1
    nothing = jnp.zeros((planes, 8, 128), f32)
    strips = []
    for start, sign, edge in ((0, 1, 0), (lo_n - 128, -1, last)):
        place = lane if sign > 0 else 127 - lane
        strip = jnp.zeros((planes, 16, 128), f32)
        for c in range(7):
            if c < 3:
                own = perm_ref[:, pl.ds(start, 128)] if c == 2 else r1_ref[c, :, pl.ds(start, 128)]
                other = halo_ref[c, start // 128].reshape(planes, 8, 128)
            else:
                own, other = wn_ref[c - 3, start // 128], nothing
            full = jnp.concatenate([own.reshape(planes, 8, 128), other], axis=1)
            offset, width = COL_PLACE[c]
            moved = pltpu.roll(full, (sign * offset) % 128, axis=2)
            strip = jnp.where((place >= offset) & (place < offset + width), moved, strip)
        strips.append(jnp.where(position == edge, 0.0, strip))
    lane = lax.broadcasted_iota(jnp.int32, (16, 128), 1)
    packed = []
    for strip, base in zip(strips, (0, 112)):
        flat = jnp.zeros((16, 128), f32)
        for p in range(planes):
            flat = jnp.where(lane >> 4 == p, pltpu.roll(strip[p], (16 * p - base) % 128, axis=1), flat)
        packed.append(flat)
    out_pair_ref[...] = jnp.where(even, packed[1], packed[0])
    out_other_ref[...] = jnp.where(even, packed[0], packed[1])


def iterate(re, im, perm, w, nz, nx, ny):
    rows, cols = perm.shape[1:]
    diag = 6.0 - K_SQUARED * perm
    shift = BETA * K_SQUARED * perm
    inside = perm > 0.5
    inverse = jnp.where(inside, OMEGA / (diag * diag + shift * shift), 0.0)
    inv_re = diag * inverse
    inv_im = -shift * inverse

    def damp(a, b):
        return a * inv_re - b * inv_im, a * inv_im + b * inv_re

    def sides(v):
        nothing = jnp.zeros((1,) + v.shape[1:], f32)
        after = jnp.concatenate([v[1:], nothing], axis=0)
        before = jnp.concatenate([nothing, v[:-1]], axis=0)
        return (
            (after, before),
            (pltpu.roll(v, rows - 1, axis=1), pltpu.roll(v, 1, axis=1)),
            (pltpu.roll(v, cols - 1, axis=2), pltpu.roll(v, 1, axis=2)),
        )

    def helm(v, pairs):
        total = pairs[0][0] + pairs[0][1]
        for a, b in pairs[1:]:
            total = total + a + b
        return diag * v - total

    def swept(a, b):
        za, zb = damp(a, b)
        ma = helm(za, sides(za)) - shift * zb
        mb = helm(zb, sides(zb)) + shift * za
        da, db = damp(a - ma, b - mb)
        return za + da, zb + db

    def surface(v, pairs):
        (a, b), (c, d), (e, f) = pairs
        return w * v + nz * (a - b) + nx * (c - d) + ny * (e - f)

    def remaining(r, v):
        pairs = sides(v)
        return r - helm(v, pairs) - surface(v, pairs)

    sa, sb = swept(re, im)
    ra, rb = remaining(re, sa), remaining(im, sb)
    ua, ub = swept(ra, rb)
    return sa + ua, sb + ub, ra, rb


def tile_of(c, t, r1_ref, perm_ref, wn_ref, halo_ref):
    planes = perm_ref.shape[0] // 8
    lanes = slice(t * 128, (t + 1) * 128)
    if c < 3:
        own = perm_ref[:, lanes] if c == 2 else r1_ref[c, :, lanes]
    else:
        own = wn_ref[c - 3, t]
    return jnp.concatenate([own.reshape(planes, 8, 128), halo_ref[c, t].reshape(planes, 8, 128)], axis=1)


def inner_kernel(r1_ref, perm_ref, wn_ref, halo_ref, sol_ref, res_ref):
    tiles = halo_ref.shape[1]
    fields = [
        jnp.concatenate([tile_of(c, t, r1_ref, perm_ref, wn_ref, halo_ref) for t in range(tiles)], axis=2)
        for c in range(7)
    ]
    sa, sb, ra, rb = iterate(*fields)
    for k, (sol, res) in enumerate(((sa, ra), (sb, rb))):
        sol_ref[k] = sol[:, 0:8, :]
        res_ref[k] = res[:, 0:8, :]


def final_kernel(
    r1_ref, perm_ref, wn_ref, halo_ref, sol_in_ref, res_in_ref, pair_ref, other_ref, sol_ref, res_ref
):
    planes = perm_ref.shape[0] // 8
    last = halo_ref.shape[1] - 1
    lane = lax.broadcasted_iota(jnp.int32, (planes, 16, 128), 2)
    even = lax.rem(lax.axis_index("gy"), 2) == 0
    pair, other = pair_ref[...], other_ref[...]
    from_right = jnp.where(even, pair, other)
    from_left = jnp.where(even, other, pair)
    from_right = jnp.stack([pltpu.roll(from_right, (-16 * p) % 128, axis=1) for p in range(planes)])
    from_left = jnp.stack([pltpu.roll(from_left, (112 - 16 * p) % 128, axis=1) for p in range(planes)])
    fields = []
    for c in range(7):
        offset, width = COL_PLACE[c]
        args = (r1_ref, perm_ref, wn_ref, halo_ref)
        field = jnp.where(lane < 56, tile_of(c, 0, *args), 0.0)
        field = jnp.where((lane >= 60) & (lane < 116), pltpu.roll(tile_of(c, last, *args), 116, axis=2), field)
        field = jnp.where((lane >= 116) & (lane < 116 + width), pltpu.roll(from_right, 116 - offset, axis=2), field)
        field = jnp.where(lane >= 128 - width, pltpu.roll(from_left, offset, axis=2), field)
        fields.append(field)
    sa, sb, ra, rb = iterate(*fields)
    near = lane[:, 0:8, :]
    for k, (sol, res) in enumerate(((sa, ra), (sb, rb))):
        for out_ref, in_ref, value in ((sol_ref, sol_in_ref, sol), (res_ref, res_in_ref, res)):
            value = value[:, 0:8, :]
            for t in range(last + 1):
                lanes = slice(t * 128, (t + 1) * 128)
                tile = in_ref[k, :, :, lanes]
                if t == 0:
                    tile = jnp.where(near < 8, value, tile)
                if t == last:
                    tile = jnp.where(near >= 120, pltpu.roll(value, 12, axis=2), tile)
                out_ref[k, :, :, lanes] = tile


def in_vmem(n):
    return [pl.BlockSpec(memory_space=pltpu.VMEM)] * n


def shape(*dims):
    return jax.ShapeDtypeStruct(dims, f32)


def per_device(rhs_field, permittivity, surf_dist, surf_normal, surf_inc, surf_cell, surf_mask, surf_owner):
    planes, rows, cols = permittivity.shape
    blocks, points = surf_cell.shape
    gx, gy = lax.axis_size("gx"), lax.axis_size("gy")
    devices = gx * gy
    slots = devices * CAP
    params = pltpu.CompilerParams(vmem_limit_bytes=48 << 20)
    send = pl.pallas_call(
        pack_kernel,
        out_shape=shape(slots * CHANNELS, points),
        in_specs=[pl.BlockSpec(memory_space=pltpu.HBM)] * 6,
        out_specs=pl.BlockSpec(memory_space=pltpu.VMEM),
        scratch_shapes=[
            pltpu.SMEM((blocks,), jnp.int32),
            pltpu.SMEM((blocks,), jnp.int32),
            pltpu.SMEM((devices,), jnp.int32),
            pltpu.VMEM((blocks, points), f32),
            pltpu.VMEM((CHANNELS - 1, blocks, points), f32),
            pltpu.VMEM((8 * blocks, points), f32),
            pltpu.VMEM((blocks, points), jnp.int32),
            pltpu.VMEM((blocks, points), jnp.int32),
            pltpu.SemaphoreType.DMA((6,)),
        ],
        compiler_params=params,
        name="pack",
    )(*[
        pltpu.with_memory_space_constraint(x, pltpu.HBM)
        for x in (surf_owner[:, 0], surf_dist, surf_normal, surf_inc, surf_cell, surf_mask)
    ])
    recv = lax.all_to_all(send.reshape(-1), ("gx", "gy"), split_axis=0, concat_axis=0, tiled=True)
    recv = recv.reshape(slots * CHANNELS, points)
    cells = planes * rows
    rhs_field = rhs_field.reshape(2, cells, cols)
    permittivity = permittivity.reshape(cells, cols)

    tiles = cols // 128

    def cost(parts):
        flops = 2 * parts * cols * slots * points
        return pl.CostEstimate(flops=flops, transcendentals=0, bytes_accessed=slots * CHANNELS * points * 4)

    strip = shape(13 * planes, cols)
    parts = 4 * cells + 14 * planes
    local = shape(slots, points)
    r1, edges, pair, other, hi, lo = pl.pallas_call(
        first_kernel,
        out_shape=(shape(2, cells, cols), shape(4, 2 * planes, cols), strip, strip, local, local),
        in_specs=in_vmem(3),
        out_specs=tuple(in_vmem(6)),
        scratch_shapes=[pltpu.VMEM((parts, cols), f32), pltpu.VMEM((3, tiles, cells, 128), f32)],
        compiler_params=params,
        cost_estimate=cost(parts),
        name="first",
    )(recv, rhs_field, permittivity)
    from_other = lax.ppermute(other, "gx", [(i, (((i + 1) ^ 1) - 1) % gx) for i in range(gx)])
    from_pair = lax.ppermute(pair, "gx", [(i, i ^ 1) for i in range(gx)])
    parts = 7 * 6 * planes
    wn = pl.pallas_call(
        second_kernel,
        out_shape=shape(4, tiles, cells, 128),
        in_specs=in_vmem(4),
        out_specs=in_vmem(1)[0],
        scratch_shapes=[pltpu.VMEM((parts, cols), f32)],
        compiler_params=params,
        cost_estimate=cost(parts),
        name="second",
    )(recv, hi, lo, edges)
    pair, other, halo = pl.pallas_call(
        strip_kernel,
        out_shape=(shape(16, 128), shape(16, 128), shape(7, tiles, cells, 128)),
        in_specs=in_vmem(5),
        out_specs=tuple(in_vmem(3)),
        compiler_params=params,
        name="strips",
    )(r1, permittivity, wn, from_pair, from_other)
    from_other = lax.ppermute(other, "gy", [(i, (((i + 1) ^ 1) - 1) % gy) for i in range(gy)])
    from_pair = lax.ppermute(pair, "gy", [(i, i ^ 1) for i in range(gy)])
    field = shape(2, planes, rows, cols)
    sol, res = pl.pallas_call(
        inner_kernel,
        out_shape=(field, field),
        in_specs=in_vmem(4),
        out_specs=tuple(in_vmem(2)),
        compiler_params=params,
        cost_estimate=cost(8 * planes),
        name="inner",
    )(r1, permittivity, wn, halo)
    return pl.pallas_call(
        final_kernel,
        out_shape=(field, field),
        in_specs=in_vmem(8),
        out_specs=tuple(in_vmem(2)),
        compiler_params=params,
        name="final",
    )(r1, permittivity, wn, halo, sol, res, from_pair, from_other)


def solution(mesh):
    split = ("gx", "gy")
    placed = (
        P(None, None, "gx", "gy"),
        P(None, "gx", "gy"),
        P(split, None),
        P(None, split, None),
        P(None, split, None),
        P(split, None),
        P(split, None),
        P(split, None),
    )
    return jax.shard_map(
        per_device,
        mesh=mesh,
        in_specs=placed,
        out_specs=(P(None, None, "gx", "gy"), P(None, None, "gx", "gy")),
        check_vma=False,
    )
```

```python
import functools

import jax
import jax.numpy as jnp
from jax import lax
from jax.experimental import pallas as pl
from jax.experimental.pallas import tpu as pltpu
from jax.sharding import PartitionSpec as P

CAP = 2
K_SQUARED = 0.25
BETA = 0.5
OMEGA = 0.8
TAU = 1.0

CHANNELS = 6
GROUP = 128

f32 = jnp.float32
bf16 = jnp.bfloat16


def pack_kernel(
    owner_hbm, dist_hbm, normal_hbm, inc_hbm, cell_hbm, mask_hbm, out_ref,
    owner_ref, first_ref, dist_ref, raw_ref, coef_ref, cell_ref, mask_ref, sems,
):
    blocks = dist_ref.shape[0]
    copies = [
        pltpu.make_async_copy(owner_hbm, owner_ref, sems.at[0]),
        pltpu.make_async_copy(dist_hbm, dist_ref, sems.at[1]),
        pltpu.make_async_copy(normal_hbm, raw_ref.at[pl.ds(0, 3)], sems.at[2]),
        pltpu.make_async_copy(inc_hbm, raw_ref.at[pl.ds(3, 2)], sems.at[3]),
        pltpu.make_async_copy(cell_hbm, cell_ref, sems.at[4]),
        pltpu.make_async_copy(mask_hbm, mask_ref, sems.at[5]),
    ]
    for copy in copies:
        copy.start()
    out_ref[...] = jnp.full(out_ref.shape, -1.0, f32)

    copies[0].wait()

    def note(i, carry):
        b = blocks - 1 - i
        first_ref[owner_ref[b]] = b
        return carry

    lax.fori_loop(0, blocks, note, 0, unroll=16)
    for copy in copies[1:]:
        copy.wait()
    half = 0.5 * TAU * dist_ref[...]
    for k in range(3):
        rows = slice(k * blocks, (k + 1) * blocks)
        coef_ref[rows] = half * raw_ref[k]
    for k in range(3, 5):
        coef_ref[k * blocks : (k + 1) * blocks] = TAU * raw_ref[k]
    coef_ref[5 * blocks : 6 * blocks] = jnp.where(mask_ref[...] > 0, cell_ref[...], 1 << 14).astype(f32)

    def place(b, carry):
        owner = owner_ref[b]
        base = (owner * CAP + jnp.where(first_ref[owner] == b, 0, 1)) * CHANNELS
        out_ref[pl.ds(base, CHANNELS), :] = coef_ref[pl.ds(b, CHANNELS, stride=blocks), :]
        return carry

    lax.fori_loop(0, blocks, place, 0, unroll=8)


def split_cells(recv_ref, hi_ref, lo_ref):
    slots = hi_ref.shape[0]
    chunk = min(64, slots)
    for i in range(0, slots, chunk):
        cell = recv_ref[pl.ds(i * CHANNELS + CHANNELS - 1, chunk, stride=CHANNELS), :].astype(jnp.int32)
        hi_ref[i : i + chunk] = (cell >> 8).astype(f32)
        lo_ref[i : i + chunk] = (cell & 255).astype(f32)


def scatter_slots(recv_ref, hi_ref, lo_ref, acc_ref, groups):
    slots = hi_ref.shape[0]
    lo_n = acc_ref.shape[1]
    per_step = min(GROUP, slots)
    acc_ref[...] = jnp.zeros(acc_ref.shape, f32)
    one = jnp.ones((), bf16)
    zero = jnp.zeros((), bf16)
    targets = []
    for rows, _, _ in groups:
        place = lax.broadcasted_iota(jnp.int32, (8 * len(rows), 128), 0)
        item = place >> 3
        row = jnp.zeros_like(place)
        for k, r in enumerate(rows):
            row = jnp.where(item == k, r, row)
        targets.append(((place & 7) * 8 + row).astype(f32).astype(bf16))
    lo_iota = lax.broadcasted_iota(jnp.int32, (lo_n, 128), 0).astype(f32).astype(bf16)

    def load(ref, index):
        return jnp.broadcast_to(ref[pl.ds(index, 1), :], (16, 128))

    def tall(tile, n):
        return jnp.concatenate([tile] * (n // 16), axis=0)

    def step(g, carry):
        left, right = [], []
        for j in range(per_step):
            slot = g * per_step + j
            hi = load(hi_ref, slot).astype(bf16)
            pieces = []
            for target, (rows, channels, count) in zip(targets, groups):
                n = 8 * len(rows)
                hot = target == tall(hi, n)
                for c in channels:
                    value = load(recv_ref, slot * CHANNELS + c)
                    lead = value.astype(bf16)
                    rest = (value - lead.astype(f32)).astype(bf16)
                    pieces.append(jnp.where(hot, tall(lead, n), zero))
                    pieces.append(jnp.where(hot, tall(rest, n), zero))
                if count:
                    pieces.append(jnp.where(hot, one, zero))
            left.append(jnp.concatenate(pieces, axis=0))
            right.append(jnp.where(lo_iota == tall(load(lo_ref, slot).astype(bf16), lo_n), one, zero))
        acc_ref[...] += lax.dot_general(
            jnp.concatenate(left, axis=1),
            jnp.concatenate(right, axis=1),
            (((1,), (1,)), ((), ())),
            preferred_element_type=f32,
        )
        return carry

    lax.fori_loop(0, slots // per_step, step, 0)
    sums, start = [], 0
    for rows, channels, count in groups:
        n = 8 * len(rows)
        found = []
        for _ in channels:
            found.append(acc_ref[start : start + n, :] + acc_ref[start + n : start + 2 * n, :])
            start += 2 * n
        if count:
            found.append(acc_ref[start : start + n, :])
            start += n
        sums.append(found)
    return sums


def keep_tiles(ref, k, value):
    for t in range(ref.shape[1]):
        ref[k, t] = value[:, t * 128 : (t + 1) * 128]


def load_rows(ref, k, t, row):
    return ref[k, t, pl.ds(row, ref.shape[2] // 8, stride=8), :]


def store_rows(ref, k, row, value):
    for t in range(ref.shape[1]):
        ref[k, t, pl.ds(row, ref.shape[2] // 8, stride=8), :] = value[:, t * 128 : (t + 1) * 128]


ALL = tuple(range(8))
EDGES = (0, 7)
INNER = (1, 2, 3, 4, 5, 6)
FIELDS = ((0, 1, 2), True)


def first_kernel(
    recv_ref, rhs_ref, perm_ref, r1_ref, edge_ref, pair_ref, other_ref, hi_ref, lo_ref, acc_ref, tile_ref
):
    split_cells(recv_ref, hi_ref, lo_ref)
    incident, fields = scatter_slots(recv_ref, hi_ref, lo_ref, acc_ref, ((ALL, (3, 4), False), (EDGES,) + FIELDS))
    planes = perm_ref.shape[0] // 8
    for k in range(2):
        for r in range(8):
            store_rows(tile_ref, k, r, incident[k][r * planes : (r + 1) * planes])
    for k in range(2):
        inc = jnp.concatenate([tile_ref[k, t] for t in range(tile_ref.shape[1])], axis=1)
        value = rhs_ref[k] - inc
        r1_ref[k] = value
        keep_tiles(tile_ref, k, value)
    keep_tiles(tile_ref, 2, perm_ref[...])
    fields = [TAU * fields[3]] + fields[:3]
    for k in range(4):
        edge_ref[k] = fields[k]
    place = lax.axis_index("gx")
    even = lax.rem(place, 2) == 0
    top, bottom = place == 0, place == lax.axis_size("gx") - 1
    for t in range(tile_ref.shape[1]):
        lanes = slice(t * 128, (t + 1) * 128)
        for c in range(7):
            for k in range(3 if c < 3 else 1):
                if c < 3:
                    item = 3 * c + k
                    first, last = load_rows(tile_ref, c, t, k), load_rows(tile_ref, c, t, 5 + k)
                else:
                    item = 6 + c
                    first, last = fields[c - 3][0:planes, lanes], fields[c - 3][planes : 2 * planes, lanes]
                if c == 2:
                    first, last = jnp.where(top, 0.0, first), jnp.where(bottom, 0.0, last)
                rows = slice(item * planes, (item + 1) * planes)
                pair_ref[rows, lanes] = jnp.where(even, last, first)
                other_ref[rows, lanes] = jnp.where(even, first, last)


def second_kernel(recv_ref, hi_ref, lo_ref, edge_ref, wn_ref, acc_ref):
    (fields,) = scatter_slots(recv_ref, hi_ref, lo_ref, acc_ref, ((INNER,) + FIELDS,))
    planes = edge_ref.shape[1] // 2
    for k, value in enumerate([TAU * fields[3]] + fields[:3]):
        for j, r in enumerate(EDGES):
            store_rows(wn_ref, k, r, edge_ref[k, j * planes : (j + 1) * planes])
        for j, r in enumerate(INNER):
            store_rows(wn_ref, k, r, value[j * planes : (j + 1) * planes])


COL_PLACE = ((0, 3), (3, 3), (6, 3), (9, 1), (10, 1), (11, 1), (12, 1))


def strip_kernel(r1_ref, perm_ref, wn_ref, pair_ref, other_ref, out_pair_ref, out_other_ref, halo_ref):
    planes = perm_ref.shape[0] // 8
    lo_n = perm_ref.shape[1]
    even = lax.rem(lax.axis_index("gx"), 2) == 0
    halo_ref[...] = jnp.zeros(halo_ref.shape, f32)
    for c in range(7):
        width = 3 if c < 3 else 1
        for k in range(width):
            item = 3 * c + k if c < 3 else 6 + c
            rows = slice(item * planes, (item + 1) * planes)
            pair, other = pair_ref[rows, :], other_ref[rows, :]
            store_rows(halo_ref, c, k, jnp.where(even, pair, other))
            store_rows(halo_ref, c, 8 - width + k, jnp.where(even, other, pair))
    lane = lax.broadcasted_iota(jnp.int32, (planes, 16, 128), 2)
    position = lax.axis_index("gy")
    even = lax.rem(position, 2) == 0
    last = lax.axis_size("gy") - 1
    nothing = jnp.zeros((planes, 8, 128), f32)
    strips = []
    for start, sign, edge in ((0, 1, 0), (lo_n - 128, -1, last)):
        place = lane if sign > 0 else 127 - lane
        strip = jnp.zeros((planes, 16, 128), f32)
        for c in range(7):
            if c < 3:
                own = perm_ref[:, pl.ds(start, 128)] if c == 2 else r1_ref[c, :, pl.ds(start, 128)]
                other = halo_ref[c, start // 128].reshape(planes, 8, 128)
            else:
                own, other = wn_ref[c - 3, start // 128], nothing
            full = jnp.concatenate([own.reshape(planes, 8, 128), other], axis=1)
            offset, width = COL_PLACE[c]
            moved = pltpu.roll(full, (sign * offset) % 128, axis=2)
            strip = jnp.where((place >= offset) & (place < offset + width), moved, strip)
        strips.append(jnp.where(position == edge, 0.0, strip))
    lane = lax.broadcasted_iota(jnp.int32, (16, 128), 1)
    packed = []
    for strip, base in zip(strips, (0, 112)):
        flat = jnp.zeros((16, 128), f32)
        for p in range(planes):
            flat = jnp.where(lane >> 4 == p, pltpu.roll(strip[p], (16 * p - base) % 128, axis=1), flat)
        packed.append(flat)
    out_pair_ref[...] = jnp.where(even, packed[1], packed[0])
    out_other_ref[...] = jnp.where(even, packed[0], packed[1])


def iterate(re, im, perm, w, nz, nx, ny):
    rows, cols = perm.shape[1:]
    diag = 6.0 - K_SQUARED * perm
    shift = BETA * K_SQUARED * perm
    inside = perm > 0.5
    inverse = jnp.where(inside, OMEGA / (diag * diag + shift * shift), 0.0)
    inv_re = diag * inverse
    inv_im = -shift * inverse

    def damp(a, b):
        return a * inv_re - b * inv_im, a * inv_im + b * inv_re

    def sides(v):
        nothing = jnp.zeros((1,) + v.shape[1:], f32)
        after = jnp.concatenate([v[1:], nothing], axis=0)
        before = jnp.concatenate([nothing, v[:-1]], axis=0)
        return (
            (after, before),
            (pltpu.roll(v, rows - 1, axis=1), pltpu.roll(v, 1, axis=1)),
            (pltpu.roll(v, cols - 1, axis=2), pltpu.roll(v, 1, axis=2)),
        )

    def helm(v, pairs):
        total = pairs[0][0] + pairs[0][1]
        for a, b in pairs[1:]:
            total = total + a + b
        return diag * v - total

    def swept(a, b):
        za, zb = damp(a, b)
        ma = helm(za, sides(za)) - shift * zb
        mb = helm(zb, sides(zb)) + shift * za
        da, db = damp(a - ma, b - mb)
        return za + da, zb + db

    def surface(v, pairs):
        (a, b), (c, d), (e, f) = pairs
        return w * v + nz * (a - b) + nx * (c - d) + ny * (e - f)

    def remaining(r, v):
        pairs = sides(v)
        return r - helm(v, pairs) - surface(v, pairs)

    sa, sb = swept(re, im)
    ra, rb = remaining(re, sa), remaining(im, sb)
    ua, ub = swept(ra, rb)
    return sa + ua, sb + ub, ra, rb


def tile_of(c, t, r1_ref, perm_ref, wn_ref, halo_ref):
    planes = perm_ref.shape[0] // 8
    lanes = slice(t * 128, (t + 1) * 128)
    if c < 3:
        own = perm_ref[:, lanes] if c == 2 else r1_ref[c, :, lanes]
    else:
        own = wn_ref[c - 3, t]
    return jnp.concatenate([own.reshape(planes, 8, 128), halo_ref[c, t].reshape(planes, 8, 128)], axis=1)


def inner_kernel(r1_ref, perm_ref, wn_ref, halo_ref, pair_ref, sol_ref, res_ref, pair_out_ref):
    pair_out_ref[...] = pair_ref[...]
    tiles = halo_ref.shape[1]
    fields = [
        jnp.concatenate([tile_of(c, t, r1_ref, perm_ref, wn_ref, halo_ref) for t in range(tiles)], axis=2)
        for c in range(7)
    ]
    sa, sb, ra, rb = iterate(*fields)
    for k, (sol, res) in enumerate(((sa, ra), (sb, rb))):
        sol_ref[k] = sol[:, 0:8, :]
        res_ref[k] = res[:, 0:8, :]


def final_kernel(
    r1_ref, perm_ref, wn_ref, halo_ref, sol_in_ref, res_in_ref, pair_ref, other_ref, sol_ref, res_ref
):
    planes = perm_ref.shape[0] // 8
    last = halo_ref.shape[1] - 1
    lane = lax.broadcasted_iota(jnp.int32, (planes, 16, 128), 2)
    even = lax.rem(lax.axis_index("gy"), 2) == 0
    pair, other = pair_ref[...], other_ref[...]
    from_right = jnp.where(even, pair, other)
    from_left = jnp.where(even, other, pair)
    from_right = jnp.stack([pltpu.roll(from_right, (-16 * p) % 128, axis=1) for p in range(planes)])
    from_left = jnp.stack([pltpu.roll(from_left, (112 - 16 * p) % 128, axis=1) for p in range(planes)])
    fields = []
    for c in range(7):
        offset, width = COL_PLACE[c]
        args = (r1_ref, perm_ref, wn_ref, halo_ref)
        field = jnp.where(lane < 56, tile_of(c, 0, *args), 0.0)
        field = jnp.where((lane >= 60) & (lane < 116), pltpu.roll(tile_of(c, last, *args), 116, axis=2), field)
        field = jnp.where((lane >= 116) & (lane < 116 + width), pltpu.roll(from_right, 116 - offset, axis=2), field)
        field = jnp.where(lane >= 128 - width, pltpu.roll(from_left, offset, axis=2), field)
        fields.append(field)
    sa, sb, ra, rb = iterate(*fields)
    near = lane[:, 0:8, :]
    for k, (sol, res) in enumerate(((sa, ra), (sb, rb))):
        for out_ref, in_ref, value in ((sol_ref, sol_in_ref, sol), (res_ref, res_in_ref, res)):
            value = value[:, 0:8, :]
            for t in range(last + 1):
                lanes = slice(t * 128, (t + 1) * 128)
                tile = in_ref[k, :, :, lanes]
                if t == 0:
                    tile = jnp.where(near < 8, value, tile)
                if t == last:
                    tile = jnp.where(near >= 120, pltpu.roll(value, 12, axis=2), tile)
                out_ref[k, :, :, lanes] = tile


def in_vmem(n):
    return [pl.BlockSpec(memory_space=pltpu.VMEM)] * n


def shape(*dims):
    return jax.ShapeDtypeStruct(dims, f32)


def per_device(rhs_field, permittivity, surf_dist, surf_normal, surf_inc, surf_cell, surf_mask, surf_owner):
    planes, rows, cols = permittivity.shape
    blocks, points = surf_cell.shape
    gx, gy = lax.axis_size("gx"), lax.axis_size("gy")
    devices = gx * gy
    slots = devices * CAP
    params = pltpu.CompilerParams(vmem_limit_bytes=48 << 20)
    send = pl.pallas_call(
        pack_kernel,
        out_shape=shape(slots * CHANNELS, points),
        in_specs=[pl.BlockSpec(memory_space=pltpu.HBM)] * 6,
        out_specs=pl.BlockSpec(memory_space=pltpu.VMEM),
        scratch_shapes=[
            pltpu.SMEM((blocks,), jnp.int32),
            pltpu.SMEM((devices,), jnp.int32),
            pltpu.VMEM((blocks, points), f32),
            pltpu.VMEM((CHANNELS - 1, blocks, points), f32),
            pltpu.VMEM((8 * blocks, points), f32),
            pltpu.VMEM((blocks, points), jnp.int32),
            pltpu.VMEM((blocks, points), jnp.int32),
            pltpu.SemaphoreType.DMA((6,)),
        ],
        compiler_params=params,
        name="pack",
    )(*[
        pltpu.with_memory_space_constraint(x, pltpu.HBM)
        for x in (surf_owner[:, 0], surf_dist, surf_normal, surf_inc, surf_cell, surf_mask)
    ])
    recv = lax.all_to_all(send.reshape(-1), ("gx", "gy"), split_axis=0, concat_axis=0, tiled=True)
    recv = recv.reshape(slots * CHANNELS, points)
    cells = planes * rows
    rhs_field = rhs_field.reshape(2, cells, cols)
    permittivity = permittivity.reshape(cells, cols)

    tiles = cols // 128

    def cost(parts):
        flops = 2 * parts * cols * slots * points
        return pl.CostEstimate(flops=flops, transcendentals=0, bytes_accessed=slots * CHANNELS * points * 4)

    strip = shape(13 * planes, cols)
    parts = 4 * cells + 14 * planes
    local = shape(slots, points)
    r1, edges, pair, other, hi, lo = pl.pallas_call(
        first_kernel,
        out_shape=(shape(2, cells, cols), shape(4, 2 * planes, cols), strip, strip, local, local),
        in_specs=in_vmem(3),
        out_specs=tuple(in_vmem(6)),
        scratch_shapes=[pltpu.VMEM((parts, cols), f32), pltpu.VMEM((3, tiles, cells, 128), f32)],
        compiler_params=params,
        cost_estimate=cost(parts),
        name="first",
    )(recv, rhs_field, permittivity)
    from_other = lax.ppermute(other, "gx", [(i, (((i + 1) ^ 1) - 1) % gx) for i in range(gx)])
    from_pair = lax.ppermute(pair, "gx", [(i, i ^ 1) for i in range(gx)])
    parts = 7 * 6 * planes
    wn = pl.pallas_call(
        second_kernel,
        out_shape=shape(4, tiles, cells, 128),
        in_specs=in_vmem(4),
        out_specs=in_vmem(1)[0],
        scratch_shapes=[pltpu.VMEM((parts, cols), f32)],
        compiler_params=params,
        cost_estimate=cost(parts),
        name="second",
    )(recv, hi, lo, edges)
    pair, other, halo = pl.pallas_call(
        strip_kernel,
        out_shape=(shape(16, 128), shape(16, 128), shape(7, tiles, cells, 128)),
        in_specs=in_vmem(5),
        out_specs=tuple(in_vmem(3)),
        compiler_params=params,
        name="strips",
    )(r1, permittivity, wn, from_pair, from_other)
    from_other = lax.ppermute(other, "gy", [(i, (((i + 1) ^ 1) - 1) % gy) for i in range(gy)])
    field = shape(2, planes, rows, cols)
    sol, res, pair = pl.pallas_call(
        inner_kernel,
        out_shape=(field, field, shape(16, 128)),
        in_specs=in_vmem(5),
        out_specs=tuple(in_vmem(3)),
        compiler_params=params,
        cost_estimate=cost(8 * planes),
        name="inner",
    )(r1, permittivity, wn, halo, pair)
    from_pair = lax.ppermute(pair, "gy", [(i, i ^ 1) for i in range(gy)])
    return pl.pallas_call(
        final_kernel,
        out_shape=(field, field),
        in_specs=in_vmem(8),
        out_specs=tuple(in_vmem(2)),
        compiler_params=params,
        name="final",
    )(r1, permittivity, wn, halo, sol, res, from_pair, from_other)


def solution(mesh):
    split = ("gx", "gy")
    placed = (
        P(None, None, "gx", "gy"),
        P(None, "gx", "gy"),
        P(split, None),
        P(None, split, None),
        P(None, split, None),
        P(split, None),
        P(split, None),
        P(split, None),
    )
    return jax.shard_map(
        per_device,
        mesh=mesh,
        in_specs=placed,
        out_specs=(P(None, None, "gx", "gy"), P(None, None, "gx", "gy")),
        check_vma=False,
    )
```

```python
import functools

import jax
import jax.numpy as jnp
from jax import lax
from jax.experimental import pallas as pl
from jax.experimental.pallas import tpu as pltpu
from jax.sharding import PartitionSpec as P

CAP = 2
K_SQUARED = 0.25
BETA = 0.5
OMEGA = 0.8
TAU = 1.0

CHANNELS = 6
GROUP = 128

f32 = jnp.float32
bf16 = jnp.bfloat16


def pack_kernel(
    owner_hbm, dist_hbm, normal_hbm, inc_hbm, cell_hbm, mask_hbm, out_ref,
    owner_ref, first_ref, dist_ref, raw_ref, coef_ref, cell_ref, mask_ref, sems,
):
    blocks = dist_ref.shape[0]
    devices = first_ref.shape[0]
    copies = [
        pltpu.make_async_copy(owner_hbm, owner_ref, sems.at[0]),
        pltpu.make_async_copy(dist_hbm, dist_ref, sems.at[1]),
        pltpu.make_async_copy(normal_hbm, raw_ref.at[pl.ds(0, 3)], sems.at[2]),
        pltpu.make_async_copy(inc_hbm, raw_ref.at[pl.ds(3, 2)], sems.at[3]),
        pltpu.make_async_copy(cell_hbm, cell_ref, sems.at[4]),
        pltpu.make_async_copy(mask_hbm, mask_ref, sems.at[5]),
    ]
    for copy in copies:
        copy.start()
    out_ref[...] = jnp.full(out_ref.shape, -1.0, f32)

    copies[0].wait()

    def note(i, carry):
        b = blocks - 1 - i
        first_ref[owner_ref[b]] = b
        return carry

    lax.fori_loop(0, blocks, note, 0, unroll=16)
    for copy in copies[1:]:
        copy.wait()
    half = 0.5 * TAU * dist_ref[...]
    for k in range(3):
        rows = slice(k * blocks, (k + 1) * blocks)
        coef_ref[rows] = half * raw_ref[k]
    for k in range(3, 5):
        coef_ref[k * blocks : (k + 1) * blocks] = TAU * raw_ref[k]
    coef_ref[5 * blocks : 6 * blocks] = jnp.where(mask_ref[...] > 0, cell_ref[...], 1 << 14).astype(f32)

    def place(b, carry):
        owner = owner_ref[b]
        peer = (owner & 1) * (devices // 2) + (owner >> 1)
        base = (peer * CAP + jnp.where(first_ref[owner] == b, 0, 1)) * CHANNELS
        out_ref[pl.ds(base, CHANNELS), :] = coef_ref[pl.ds(b, CHANNELS, stride=blocks), :]
        return carry

    lax.fori_loop(0, blocks, place, 0, unroll=16)


def split_cells(recv_ref, hi_ref, lo_ref):
    slots = hi_ref.shape[0]
    chunk = min(64, slots)
    for i in range(0, slots, chunk):
        cell = recv_ref[pl.ds(i * CHANNELS + CHANNELS - 1, chunk, stride=CHANNELS), :].astype(jnp.int32)
        hi_ref[i : i + chunk] = (cell >> 8).astype(f32)
        lo_ref[i : i + chunk] = (cell & 255).astype(f32)


def scatter_slots(recv_ref, hi_ref, lo_ref, acc_ref, groups):
    slots = hi_ref.shape[0]
    lo_n = acc_ref.shape[1]
    per_step = min(GROUP, slots)
    acc_ref[...] = jnp.zeros(acc_ref.shape, f32)
    one = jnp.ones((), bf16)
    zero = jnp.zeros((), bf16)
    targets = []
    for rows, _, _ in groups:
        place = lax.broadcasted_iota(jnp.int32, (8 * len(rows), 128), 0)
        item = place >> 3
        row = jnp.zeros_like(place)
        for k, r in enumerate(rows):
            row = jnp.where(item == k, r, row)
        targets.append(((place & 7) * 8 + row).astype(f32).astype(bf16))
    lo_iota = lax.broadcasted_iota(jnp.int32, (lo_n, 128), 0).astype(f32).astype(bf16)

    def load(ref, index):
        return jnp.broadcast_to(ref[pl.ds(index, 1), :], (16, 128))

    def tall(tile, n):
        return jnp.concatenate([tile] * (n // 16), axis=0)

    def step(g, carry):
        left, right = [], []
        for j in range(per_step):
            slot = g * per_step + j
            hi = load(hi_ref, slot).astype(bf16)
            pieces = []
            for target, (rows, channels, count) in zip(targets, groups):
                n = 8 * len(rows)
                hot = target == tall(hi, n)
                for c in channels:
                    value = load(recv_ref, slot * CHANNELS + c)
                    lead = value.astype(bf16)
                    rest = (value - lead.astype(f32)).astype(bf16)
                    pieces.append(jnp.where(hot, tall(lead, n), zero))
                    pieces.append(jnp.where(hot, tall(rest, n), zero))
                if count:
                    pieces.append(jnp.where(hot, one, zero))
            left.append(jnp.concatenate(pieces, axis=0))
            right.append(jnp.where(lo_iota == tall(load(lo_ref, slot).astype(bf16), lo_n), one, zero))
        acc_ref[...] += lax.dot_general(
            jnp.concatenate(left, axis=1),
            jnp.concatenate(right, axis=1),
            (((1,), (1,)), ((), ())),
            preferred_element_type=f32,
        )
        return carry

    lax.fori_loop(0, slots // per_step, step, 0)
    sums, start = [], 0
    for rows, channels, count in groups:
        n = 8 * len(rows)
        found = []
        for _ in channels:
            found.append(acc_ref[start : start + n, :] + acc_ref[start + n : start + 2 * n, :])
            start += 2 * n
        if count:
            found.append(acc_ref[start : start + n, :])
            start += n
        sums.append(found)
    return sums


def keep_tiles(ref, k, value):
    for t in range(ref.shape[1]):
        ref[k, t] = value[:, t * 128 : (t + 1) * 128]


def load_rows(ref, k, t, row):
    return ref[k, t, pl.ds(row, ref.shape[2] // 8, stride=8), :]


def store_rows(ref, k, row, value):
    for t in range(ref.shape[1]):
        ref[k, t, pl.ds(row, ref.shape[2] // 8, stride=8), :] = value[:, t * 128 : (t + 1) * 128]


ALL = tuple(range(8))
EDGES = (0, 7)
INNER = (1, 2, 3, 4, 5, 6)
FIELDS = ((0, 1, 2), True)


def first_kernel(
    recv_ref, rhs_ref, perm_ref, r1_ref, edge_ref, pair_ref, other_ref, hi_ref, lo_ref, acc_ref, tile_ref
):
    split_cells(recv_ref, hi_ref, lo_ref)
    incident, fields = scatter_slots(recv_ref, hi_ref, lo_ref, acc_ref, ((ALL, (3, 4), False), (EDGES,) + FIELDS))
    planes = perm_ref.shape[0] // 8
    for k in range(2):
        for r in range(8):
            store_rows(tile_ref, k, r, incident[k][r * planes : (r + 1) * planes])
    for k in range(2):
        inc = jnp.concatenate([tile_ref[k, t] for t in range(tile_ref.shape[1])], axis=1)
        value = rhs_ref[k] - inc
        r1_ref[k] = value
        keep_tiles(tile_ref, k, value)
    keep_tiles(tile_ref, 2, perm_ref[...])
    fields = [TAU * fields[3]] + fields[:3]
    for k in range(4):
        edge_ref[k] = fields[k]
    place = lax.axis_index("gx")
    even = lax.rem(place, 2) == 0
    top, bottom = place == 0, place == lax.axis_size("gx") - 1
    for t in range(tile_ref.shape[1]):
        lanes = slice(t * 128, (t + 1) * 128)
        for c in range(7):
            for k in range(3 if c < 3 else 1):
                if c < 3:
                    item = 3 * c + k
                    first, last = load_rows(tile_ref, c, t, k), load_rows(tile_ref, c, t, 5 + k)
                else:
                    item = 6 + c
                    first, last = fields[c - 3][0:planes, lanes], fields[c - 3][planes : 2 * planes, lanes]
                if c == 2:
                    first, last = jnp.where(top, 0.0, first), jnp.where(bottom, 0.0, last)
                rows = slice(item * planes, (item + 1) * planes)
                pair_ref[rows, lanes] = jnp.where(even, last, first)
                other_ref[rows, lanes] = jnp.where(even, first, last)


def second_kernel(recv_ref, hi_ref, lo_ref, edge_ref, wn_ref, acc_ref):
    (fields,) = scatter_slots(recv_ref, hi_ref, lo_ref, acc_ref, ((INNER,) + FIELDS,))
    planes = edge_ref.shape[1] // 2
    for k, value in enumerate([TAU * fields[3]] + fields[:3]):
        for j, r in enumerate(EDGES):
            store_rows(wn_ref, k, r, edge_ref[k, j * planes : (j + 1) * planes])
        for j, r in enumerate(INNER):
            store_rows(wn_ref, k, r, value[j * planes : (j + 1) * planes])


COL_PLACE = ((0, 3), (3, 3), (6, 3), (9, 1), (10, 1), (11, 1), (12, 1))


def strip_kernel(r1_ref, perm_ref, wn_ref, pair_ref, other_ref, out_pair_ref, out_other_ref, halo_ref):
    planes = perm_ref.shape[0] // 8
    lo_n = perm_ref.shape[1]
    even = lax.rem(lax.axis_index("gx"), 2) == 0
    halo_ref[...] = jnp.zeros(halo_ref.shape, f32)
    for c in range(7):
        width = 3 if c < 3 else 1
        for k in range(width):
            item = 3 * c + k if c < 3 else 6 + c
            rows = slice(item * planes, (item + 1) * planes)
            pair, other = pair_ref[rows, :], other_ref[rows, :]
            store_rows(halo_ref, c, k, jnp.where(even, pair, other))
            store_rows(halo_ref, c, 8 - width + k, jnp.where(even, other, pair))
    lane = lax.broadcasted_iota(jnp.int32, (planes, 16, 128), 2)
    position = lax.axis_index("gy")
    even = lax.rem(position, 2) == 0
    last = lax.axis_size("gy") - 1
    nothing = jnp.zeros((planes, 8, 128), f32)
    strips = []
    for start, sign, edge in ((0, 1, 0), (lo_n - 128, -1, last)):
        place = lane if sign > 0 else 127 - lane
        strip = jnp.zeros((planes, 16, 128), f32)
        for c in range(7):
            if c < 3:
                own = perm_ref[:, pl.ds(start, 128)] if c == 2 else r1_ref[c, :, pl.ds(start, 128)]
                other = halo_ref[c, start // 128].reshape(planes, 8, 128)
            else:
                own, other = wn_ref[c - 3, start // 128], nothing
            full = jnp.concatenate([own.reshape(planes, 8, 128), other], axis=1)
            offset, width = COL_PLACE[c]
            moved = pltpu.roll(full, (sign * offset) % 128, axis=2)
            strip = jnp.where((place >= offset) & (place < offset + width), moved, strip)
        strips.append(jnp.where(position == edge, 0.0, strip))
    lane = lax.broadcasted_iota(jnp.int32, (16, 128), 1)
    packed = []
    for strip, base in zip(strips, (0, 112)):
        flat = jnp.zeros((16, 128), f32)
        for p in range(planes):
            flat = jnp.where(lane >> 4 == p, pltpu.roll(strip[p], (16 * p - base) % 128, axis=1), flat)
        packed.append(flat)
    out_pair_ref[...] = jnp.where(even, packed[1], packed[0])
    out_other_ref[...] = jnp.where(even, packed[0], packed[1])


def iterate(re, im, perm, w, nz, nx, ny):
    rows, cols = perm.shape[1:]
    diag = 6.0 - K_SQUARED * perm
    shift = BETA * K_SQUARED * perm
    inside = perm > 0.5
    inverse = jnp.where(inside, OMEGA / (diag * diag + shift * shift), 0.0)
    inv_re = diag * inverse
    inv_im = -shift * inverse

    def damp(a, b):
        return a * inv_re - b * inv_im, a * inv_im + b * inv_re

    def sides(v):
        nothing = jnp.zeros((1,) + v.shape[1:], f32)
        after = jnp.concatenate([v[1:], nothing], axis=0)
        before = jnp.concatenate([nothing, v[:-1]], axis=0)
        return (
            (after, before),
            (pltpu.roll(v, rows - 1, axis=1), pltpu.roll(v, 1, axis=1)),
            (pltpu.roll(v, cols - 1, axis=2), pltpu.roll(v, 1, axis=2)),
        )

    def helm(v, pairs):
        total = pairs[0][0] + pairs[0][1]
        for a, b in pairs[1:]:
            total = total + a + b
        return diag * v - total

    def swept(a, b):
        za, zb = damp(a, b)
        ma = helm(za, sides(za)) - shift * zb
        mb = helm(zb, sides(zb)) + shift * za
        da, db = damp(a - ma, b - mb)
        return za + da, zb + db

    def surface(v, pairs):
        (a, b), (c, d), (e, f) = pairs
        return w * v + nz * (a - b) + nx * (c - d) + ny * (e - f)

    def remaining(r, v):
        pairs = sides(v)
        return r - helm(v, pairs) - surface(v, pairs)

    sa, sb = swept(re, im)
    ra, rb = remaining(re, sa), remaining(im, sb)
    ua, ub = swept(ra, rb)
    return sa + ua, sb + ub, ra, rb


def tile_of(c, t, r1_ref, perm_ref, wn_ref, halo_ref):
    planes = perm_ref.shape[0] // 8
    lanes = slice(t * 128, (t + 1) * 128)
    if c < 3:
        own = perm_ref[:, lanes] if c == 2 else r1_ref[c, :, lanes]
    else:
        own = wn_ref[c - 3, t]
    return jnp.concatenate([own.reshape(planes, 8, 128), halo_ref[c, t].reshape(planes, 8, 128)], axis=1)


def inner_kernel(r1_ref, perm_ref, wn_ref, halo_ref, pair_ref, sol_ref, res_ref, pair_out_ref):
    pair_out_ref[...] = pair_ref[...]
    tiles = halo_ref.shape[1]
    fields = [
        jnp.concatenate([tile_of(c, t, r1_ref, perm_ref, wn_ref, halo_ref) for t in range(tiles)], axis=2)
        for c in range(7)
    ]
    sa, sb, ra, rb = iterate(*fields)
    for k, (sol, res) in enumerate(((sa, ra), (sb, rb))):
        sol_ref[k] = sol[:, 0:8, :]
        res_ref[k] = res[:, 0:8, :]


def final_kernel(
    r1_ref, perm_ref, wn_ref, halo_ref, sol_in_ref, res_in_ref, pair_ref, other_ref, sol_ref, res_ref
):
    planes = perm_ref.shape[0] // 8
    last = halo_ref.shape[1] - 1
    lane = lax.broadcasted_iota(jnp.int32, (planes, 16, 128), 2)
    even = lax.rem(lax.axis_index("gy"), 2) == 0
    pair, other = pair_ref[...], other_ref[...]
    from_right = jnp.where(even, pair, other)
    from_left = jnp.where(even, other, pair)
    from_right = jnp.stack([pltpu.roll(from_right, (-16 * p) % 128, axis=1) for p in range(planes)])
    from_left = jnp.stack([pltpu.roll(from_left, (112 - 16 * p) % 128, axis=1) for p in range(planes)])
    fields = []
    for c in range(7):
        offset, width = COL_PLACE[c]
        args = (r1_ref, perm_ref, wn_ref, halo_ref)
        field = jnp.where(lane < 56, tile_of(c, 0, *args), 0.0)
        field = jnp.where((lane >= 60) & (lane < 116), pltpu.roll(tile_of(c, last, *args), 116, axis=2), field)
        field = jnp.where((lane >= 116) & (lane < 116 + width), pltpu.roll(from_right, 116 - offset, axis=2), field)
        field = jnp.where(lane >= 128 - width, pltpu.roll(from_left, offset, axis=2), field)
        fields.append(field)
    sa, sb, ra, rb = iterate(*fields)
    near = lane[:, 0:8, :]
    for k, (sol, res) in enumerate(((sa, ra), (sb, rb))):
        for out_ref, in_ref, value in ((sol_ref, sol_in_ref, sol), (res_ref, res_in_ref, res)):
            value = value[:, 0:8, :]
            for t in range(last + 1):
                lanes = slice(t * 128, (t + 1) * 128)
                tile = in_ref[k, :, :, lanes]
                if t == 0:
                    tile = jnp.where(near < 8, value, tile)
                if t == last:
                    tile = jnp.where(near >= 120, pltpu.roll(value, 12, axis=2), tile)
                out_ref[k, :, :, lanes] = tile


def in_vmem(n):
    return [pl.BlockSpec(memory_space=pltpu.VMEM)] * n


def shape(*dims):
    return jax.ShapeDtypeStruct(dims, f32)


def per_device(rhs_field, permittivity, surf_dist, surf_normal, surf_inc, surf_cell, surf_mask, surf_owner):
    planes, rows, cols = permittivity.shape
    blocks, points = surf_cell.shape
    gx, gy = lax.axis_size("gx"), lax.axis_size("gy")
    devices = gx * gy
    slots = devices * CAP
    params = pltpu.CompilerParams(vmem_limit_bytes=48 << 20)
    send = pl.pallas_call(
        pack_kernel,
        out_shape=shape(slots * CHANNELS, points),
        in_specs=[pl.BlockSpec(memory_space=pltpu.HBM)] * 6,
        out_specs=pl.BlockSpec(memory_space=pltpu.VMEM),
        scratch_shapes=[
            pltpu.SMEM((blocks,), jnp.int32),
            pltpu.SMEM((devices,), jnp.int32),
            pltpu.VMEM((blocks, points), f32),
            pltpu.VMEM((CHANNELS - 1, blocks, points), f32),
            pltpu.VMEM((8 * blocks, points), f32),
            pltpu.VMEM((blocks, points), jnp.int32),
            pltpu.VMEM((blocks, points), jnp.int32),
            pltpu.SemaphoreType.DMA((6,)),
        ],
        compiler_params=params,
        name="pack",
    )(*[
        pltpu.with_memory_space_constraint(x, pltpu.HBM)
        for x in (surf_owner[:, 0], surf_dist, surf_normal, surf_inc, surf_cell, surf_mask)
    ])
    peers = list(range(0, devices, 2)) + list(range(1, devices, 2))
    recv = lax.all_to_all(
        send.reshape(-1), ("gx", "gy"), split_axis=0, concat_axis=0, tiled=True, axis_index_groups=[peers]
    )
    recv = recv.reshape(slots * CHANNELS, points)
    cells = planes * rows
    rhs_field = rhs_field.reshape(2, cells, cols)
    permittivity = permittivity.reshape(cells, cols)

    tiles = cols // 128

    def cost(parts):
        flops = 2 * parts * cols * slots * points
        return pl.CostEstimate(flops=flops, transcendentals=0, bytes_accessed=slots * CHANNELS * points * 4)

    strip = shape(13 * planes, cols)
    parts = 4 * cells + 14 * planes
    local = shape(slots, points)
    r1, edges, pair, other, hi, lo = pl.pallas_call(
        first_kernel,
        out_shape=(shape(2, cells, cols), shape(4, 2 * planes, cols), strip, strip, local, local),
        in_specs=in_vmem(3),
        out_specs=tuple(in_vmem(6)),
        scratch_shapes=[pltpu.VMEM((parts, cols), f32), pltpu.VMEM((3, tiles, cells, 128), f32)],
        compiler_params=params,
        cost_estimate=cost(parts),
        name="first",
    )(recv, rhs_field, permittivity)
    from_other = lax.ppermute(other, "gx", [(i, (((i + 1) ^ 1) - 1) % gx) for i in range(gx)])
    from_pair = lax.ppermute(pair, "gx", [(i, i ^ 1) for i in range(gx)])
    parts = 7 * 6 * planes
    wn = pl.pallas_call(
        second_kernel,
        out_shape=shape(4, tiles, cells, 128),
        in_specs=in_vmem(4),
        out_specs=in_vmem(1)[0],
        scratch_shapes=[pltpu.VMEM((parts, cols), f32)],
        compiler_params=params,
        cost_estimate=cost(parts),
        name="second",
    )(recv, hi, lo, edges)
    pair, other, halo = pl.pallas_call(
        strip_kernel,
        out_shape=(shape(16, 128), shape(16, 128), shape(7, tiles, cells, 128)),
        in_specs=in_vmem(5),
        out_specs=tuple(in_vmem(3)),
        compiler_params=params,
        name="strips",
    )(r1, permittivity, wn, from_pair, from_other)
    from_other = lax.ppermute(other, "gy", [(i, (((i + 1) ^ 1) - 1) % gy) for i in range(gy)])
    field = shape(2, planes, rows, cols)
    sol, res, pair = pl.pallas_call(
        inner_kernel,
        out_shape=(field, field, shape(16, 128)),
        in_specs=in_vmem(5),
        out_specs=tuple(in_vmem(3)),
        compiler_params=params,
        cost_estimate=cost(8 * planes),
        name="inner",
    )(r1, permittivity, wn, halo, pair)
    from_pair = lax.ppermute(pair, "gy", [(i, i ^ 1) for i in range(gy)])
    return pl.pallas_call(
        final_kernel,
        out_shape=(field, field),
        in_specs=in_vmem(8),
        out_specs=tuple(in_vmem(2)),
        compiler_params=params,
        name="final",
    )(r1, permittivity, wn, halo, sol, res, from_pair, from_other)


def solution(mesh):
    split = ("gx", "gy")
    placed = (
        P(None, None, "gx", "gy"),
        P(None, "gx", "gy"),
        P(split, None),
        P(None, split, None),
        P(None, split, None),
        P(split, None),
        P(split, None),
        P(split, None),
    )
    return jax.shard_map(
        per_device,
        mesh=mesh,
        in_specs=placed,
        out_specs=(P(None, None, "gx", "gy"), P(None, None, "gx", "gy")),
        check_vma=False,
    )
```

```python
import functools

import jax
import jax.numpy as jnp
from jax import lax
from jax.experimental import pallas as pl
from jax.experimental.pallas import tpu as pltpu
from jax.sharding import PartitionSpec as P

CAP = 2
K_SQUARED = 0.25
BETA = 0.5
OMEGA = 0.8
TAU = 1.0

CHANNELS = 6
GROUP = 128

f32 = jnp.float32
bf16 = jnp.bfloat16


def pack_kernel(
    owner_hbm, dist_hbm, normal_hbm, inc_hbm, cell_hbm, mask_hbm, out_ref,
    owner_ref, first_ref, dist_ref, raw_ref, coef_ref, cell_ref, mask_ref, sems,
):
    blocks = dist_ref.shape[0]
    copies = [
        pltpu.make_async_copy(owner_hbm, owner_ref, sems.at[0]),
        pltpu.make_async_copy(dist_hbm, dist_ref, sems.at[1]),
        pltpu.make_async_copy(normal_hbm, raw_ref.at[pl.ds(0, 3)], sems.at[2]),
        pltpu.make_async_copy(inc_hbm, raw_ref.at[pl.ds(3, 2)], sems.at[3]),
        pltpu.make_async_copy(cell_hbm, cell_ref, sems.at[4]),
        pltpu.make_async_copy(mask_hbm, mask_ref, sems.at[5]),
    ]
    for copy in copies:
        copy.start()
    out_ref[...] = jnp.full(out_ref.shape, -1.0, f32)

    copies[0].wait()

    def note(i, carry):
        b = blocks - 1 - i
        first_ref[owner_ref[b]] = b
        return carry

    lax.fori_loop(0, blocks, note, 0, unroll=16)
    for copy in copies[1:]:
        copy.wait()
    half = 0.5 * TAU * dist_ref[...]
    for k in range(3):
        rows = slice(k * blocks, (k + 1) * blocks)
        coef_ref[rows] = half * raw_ref[k]
    for k in range(3, 5):
        coef_ref[k * blocks : (k + 1) * blocks] = TAU * raw_ref[k]
    coef_ref[5 * blocks : 6 * blocks] = jnp.where(mask_ref[...] > 0, cell_ref[...], 1 << 14).astype(f32)

    def place(b, carry):
        owner = owner_ref[b]
        base = (owner * CAP + jnp.where(first_ref[owner] == b, 0, 1)) * CHANNELS
        out_ref[pl.ds(base, CHANNELS), :] = coef_ref[pl.ds(b, CHANNELS, stride=blocks), :]
        return carry

    lax.fori_loop(0, blocks, place, 0, unroll=8)


def split_cells(recv_ref, hi_ref, lo_ref):
    slots = hi_ref.shape[0]
    chunk = min(64, slots)
    for i in range(0, slots, chunk):
        cell = recv_ref[pl.ds(i * CHANNELS + CHANNELS - 1, chunk, stride=CHANNELS), :].astype(jnp.int32)
        hi_ref[i : i + chunk] = (cell >> 8).astype(f32)
        lo_ref[i : i + chunk] = (cell & 255).astype(f32)


def scatter_slots(recv_ref, hi_ref, lo_ref, acc_ref, groups):
    slots = hi_ref.shape[0]
    lo_n = acc_ref.shape[1]
    per_step = min(GROUP, slots)
    acc_ref[...] = jnp.zeros(acc_ref.shape, f32)
    one = jnp.ones((), bf16)
    zero = jnp.zeros((), bf16)
    targets = []
    for rows, _, _ in groups:
        place = lax.broadcasted_iota(jnp.int32, (8 * len(rows), 128), 0)
        item = place >> 3
        row = jnp.zeros_like(place)
        for k, r in enumerate(rows):
            row = jnp.where(item == k, r, row)
        targets.append(((place & 7) * 8 + row).astype(f32).astype(bf16))
    lo_iota = lax.broadcasted_iota(jnp.int32, (lo_n, 128), 0).astype(f32).astype(bf16)

    def load(ref, index):
        return jnp.broadcast_to(ref[pl.ds(index, 1), :], (16, 128))

    def tall(tile, n):
        return jnp.concatenate([tile] * (n // 16), axis=0)

    def step(g, carry):
        left, right = [], []
        for j in range(per_step):
            slot = g * per_step + j
            hi = load(hi_ref, slot).astype(bf16)
            pieces = []
            for target, (rows, channels, count) in zip(targets, groups):
                n = 8 * len(rows)
                hot = target == tall(hi, n)
                for c in channels:
                    value = load(recv_ref, slot * CHANNELS + c)
                    lead = value.astype(bf16)
                    rest = (value - lead.astype(f32)).astype(bf16)
                    pieces.append(jnp.where(hot, tall(lead, n), zero))
                    pieces.append(jnp.where(hot, tall(rest, n), zero))
                if count:
                    pieces.append(jnp.where(hot, one, zero))
            left.append(jnp.concatenate(pieces, axis=0))
            right.append(jnp.where(lo_iota == tall(load(lo_ref, slot).astype(bf16), lo_n), one, zero))
        acc_ref[...] += lax.dot_general(
            jnp.concatenate(left, axis=1),
            jnp.concatenate(right, axis=1),
            (((1,), (1,)), ((), ())),
            preferred_element_type=f32,
        )
        return carry

    lax.fori_loop(0, slots // per_step, step, 0)
    sums, start = [], 0
    for rows, channels, count in groups:
        n = 8 * len(rows)
        found = []
        for _ in channels:
            found.append(acc_ref[start : start + n, :] + acc_ref[start + n : start + 2 * n, :])
            start += 2 * n
        if count:
            found.append(acc_ref[start : start + n, :])
            start += n
        sums.append(found)
    return sums


def keep_tiles(ref, k, value):
    for t in range(ref.shape[1]):
        ref[k, t] = value[:, t * 128 : (t + 1) * 128]


def load_rows(ref, k, t, row):
    return ref[k, t, pl.ds(row, ref.shape[2] // 8, stride=8), :]


def store_rows(ref, k, row, value):
    for t in range(ref.shape[1]):
        ref[k, t, pl.ds(row, ref.shape[2] // 8, stride=8), :] = value[:, t * 128 : (t + 1) * 128]


OUTER = (0, 1, 2, 5, 6, 7)
MIDDLE = (3, 4)
EDGES = (0, 7)
INNER = (1, 2, 3, 4, 5, 6)
FIELDS = ((0, 1, 2), True)


def subtract_rows(tile_ref, k, rows, sums):
    planes = tile_ref.shape[2] // 8
    for j, r in enumerate(rows):
        before = jnp.concatenate([load_rows(tile_ref, k, t, r) for t in range(tile_ref.shape[1])], axis=1)
        store_rows(tile_ref, k, r, before - sums[j * planes : (j + 1) * planes])


def first_kernel(
    recv_ref, rhs_ref, perm_ref, kept_ref, edge_ref, pair_ref, other_ref, hi_ref, lo_ref, acc_ref, tile_ref
):
    split_cells(recv_ref, hi_ref, lo_ref)
    incident, fields = scatter_slots(recv_ref, hi_ref, lo_ref, acc_ref, ((OUTER, (3, 4), False), (EDGES,) + FIELDS))
    planes = perm_ref.shape[0] // 8
    for k in range(2):
        keep_tiles(tile_ref, k, rhs_ref[k])
        subtract_rows(tile_ref, k, OUTER, incident[k])
        kept_ref[k] = tile_ref[k]
    keep_tiles(tile_ref, 2, perm_ref[...])
    fields = [TAU * fields[3]] + fields[:3]
    for k in range(4):
        edge_ref[k] = fields[k]
    place = lax.axis_index("gx")
    even = lax.rem(place, 2) == 0
    top, bottom = place == 0, place == lax.axis_size("gx") - 1
    for t in range(tile_ref.shape[1]):
        lanes = slice(t * 128, (t + 1) * 128)
        for c in range(7):
            for k in range(3 if c < 3 else 1):
                if c < 3:
                    item = 3 * c + k
                    first, last = load_rows(tile_ref, c, t, k), load_rows(tile_ref, c, t, 5 + k)
                else:
                    item = 6 + c
                    first, last = fields[c - 3][0:planes, lanes], fields[c - 3][planes : 2 * planes, lanes]
                if c == 2:
                    first, last = jnp.where(top, 0.0, first), jnp.where(bottom, 0.0, last)
                rows = slice(item * planes, (item + 1) * planes)
                pair_ref[rows, lanes] = jnp.where(even, last, first)
                other_ref[rows, lanes] = jnp.where(even, first, last)


def second_kernel(recv_ref, hi_ref, lo_ref, kept_ref, edge_ref, r1_ref, wn_ref, acc_ref, tile_ref):
    incident, fields = scatter_slots(recv_ref, hi_ref, lo_ref, acc_ref, ((MIDDLE, (3, 4), False), (INNER,) + FIELDS))
    for k in range(2):
        tile_ref[k] = kept_ref[k]
        subtract_rows(tile_ref, k, MIDDLE, incident[k])
        r1_ref[k] = jnp.concatenate([tile_ref[k, t] for t in range(tile_ref.shape[1])], axis=1)
    planes = edge_ref.shape[1] // 2
    for k, value in enumerate([TAU * fields[3]] + fields[:3]):
        for j, r in enumerate(EDGES):
            store_rows(wn_ref, k, r, edge_ref[k, j * planes : (j + 1) * planes])
        for j, r in enumerate(INNER):
            store_rows(wn_ref, k, r, value[j * planes : (j + 1) * planes])


COL_PLACE = ((0, 3), (3, 3), (6, 3), (9, 1), (10, 1), (11, 1), (12, 1))


def strip_kernel(r1_ref, perm_ref, wn_ref, pair_ref, other_ref, out_pair_ref, out_other_ref, halo_ref):
    planes = perm_ref.shape[0] // 8
    lo_n = perm_ref.shape[1]
    even = lax.rem(lax.axis_index("gx"), 2) == 0
    halo_ref[...] = jnp.zeros(halo_ref.shape, f32)
    for c in range(7):
        width = 3 if c < 3 else 1
        for k in range(width):
            item = 3 * c + k if c < 3 else 6 + c
            rows = slice(item * planes, (item + 1) * planes)
            pair, other = pair_ref[rows, :], other_ref[rows, :]
            store_rows(halo_ref, c, k, jnp.where(even, pair, other))
            store_rows(halo_ref, c, 8 - width + k, jnp.where(even, other, pair))
    lane = lax.broadcasted_iota(jnp.int32, (planes, 16, 128), 2)
    position = lax.axis_index("gy")
    even = lax.rem(position, 2) == 0
    last = lax.axis_size("gy") - 1
    nothing = jnp.zeros((planes, 8, 128), f32)
    strips = []
    for start, sign, edge in ((0, 1, 0), (lo_n - 128, -1, last)):
        place = lane if sign > 0 else 127 - lane
        strip = jnp.zeros((planes, 16, 128), f32)
        for c in range(7):
            if c < 3:
                own = perm_ref[:, pl.ds(start, 128)] if c == 2 else r1_ref[c, :, pl.ds(start, 128)]
                other = halo_ref[c, start // 128].reshape(planes, 8, 128)
            else:
                own, other = wn_ref[c - 3, start // 128], nothing
            full = jnp.concatenate([own.reshape(planes, 8, 128), other], axis=1)
            offset, width = COL_PLACE[c]
            moved = pltpu.roll(full, (sign * offset) % 128, axis=2)
            strip = jnp.where((place >= offset) & (place < offset + width), moved, strip)
        strips.append(jnp.where(position == edge, 0.0, strip))
    lane = lax.broadcasted_iota(jnp.int32, (16, 128), 1)
    packed = []
    for strip, base in zip(strips, (0, 112)):
        flat = jnp.zeros((16, 128), f32)
        for p in range(planes):
            flat = jnp.where(lane >> 4 == p, pltpu.roll(strip[p], (16 * p - base) % 128, axis=1), flat)
        packed.append(flat)
    out_pair_ref[...] = jnp.where(even, packed[1], packed[0])
    out_other_ref[...] = jnp.where(even, packed[0], packed[1])


def iterate(re, im, perm, w, nz, nx, ny):
    rows, cols = perm.shape[1:]
    diag = 6.0 - K_SQUARED * perm
    shift = BETA * K_SQUARED * perm
    inside = perm > 0.5
    inverse = jnp.where(inside, OMEGA / (diag * diag + shift * shift), 0.0)
    inv_re = diag * inverse
    inv_im = -shift * inverse

    def damp(a, b):
        return a * inv_re - b * inv_im, a * inv_im + b * inv_re

    def sides(v):
        nothing = jnp.zeros((1,) + v.shape[1:], f32)
        after = jnp.concatenate([v[1:], nothing], axis=0)
        before = jnp.concatenate([nothing, v[:-1]], axis=0)
        return (
            (after, before),
            (pltpu.roll(v, rows - 1, axis=1), pltpu.roll(v, 1, axis=1)),
            (pltpu.roll(v, cols - 1, axis=2), pltpu.roll(v, 1, axis=2)),
        )

    def helm(v, pairs):
        total = pairs[0][0] + pairs[0][1]
        for a, b in pairs[1:]:
            total = total + a + b
        return diag * v - total

    def swept(a, b):
        za, zb = damp(a, b)
        ma = helm(za, sides(za)) - shift * zb
        mb = helm(zb, sides(zb)) + shift * za
        da, db = damp(a - ma, b - mb)
        return za + da, zb + db

    def surface(v, pairs):
        (a, b), (c, d), (e, f) = pairs
        return w * v + nz * (a - b) + nx * (c - d) + ny * (e - f)

    def remaining(r, v):
        pairs = sides(v)
        return r - helm(v, pairs) - surface(v, pairs)

    sa, sb = swept(re, im)
    ra, rb = remaining(re, sa), remaining(im, sb)
    ua, ub = swept(ra, rb)
    return sa + ua, sb + ub, ra, rb


def tile_of(c, t, r1_ref, perm_ref, wn_ref, halo_ref):
    planes = perm_ref.shape[0] // 8
    lanes = slice(t * 128, (t + 1) * 128)
    if c < 3:
        own = perm_ref[:, lanes] if c == 2 else r1_ref[c, :, lanes]
    else:
        own = wn_ref[c - 3, t]
    return jnp.concatenate([own.reshape(planes, 8, 128), halo_ref[c, t].reshape(planes, 8, 128)], axis=1)


def inner_kernel(r1_ref, perm_ref, wn_ref, halo_ref, pair_ref, sol_ref, res_ref, pair_out_ref):
    pair_out_ref[...] = pair_ref[...]
    tiles = halo_ref.shape[1]
    fields = [
        jnp.concatenate([tile_of(c, t, r1_ref, perm_ref, wn_ref, halo_ref) for t in range(tiles)], axis=2)
        for c in range(7)
    ]
    sa, sb, ra, rb = iterate(*fields)
    for k, (sol, res) in enumerate(((sa, ra), (sb, rb))):
        sol_ref[k] = sol[:, 0:8, :]
        res_ref[k] = res[:, 0:8, :]


def final_kernel(
    r1_ref, perm_ref, wn_ref, halo_ref, sol_in_ref, res_in_ref, pair_ref, other_ref, sol_ref, res_ref
):
    planes = perm_ref.shape[0] // 8
    last = halo_ref.shape[1] - 1
    lane = lax.broadcasted_iota(jnp.int32, (planes, 16, 128), 2)
    even = lax.rem(lax.axis_index("gy"), 2) == 0
    pair, other = pair_ref[...], other_ref[...]
    from_right = jnp.where(even, pair, other)
    from_left = jnp.where(even, other, pair)
    from_right = jnp.stack([pltpu.roll(from_right, (-16 * p) % 128, axis=1) for p in range(planes)])
    from_left = jnp.stack([pltpu.roll(from_left, (112 - 16 * p) % 128, axis=1) for p in range(planes)])
    fields = []
    for c in range(7):
        offset, width = COL_PLACE[c]
        args = (r1_ref, perm_ref, wn_ref, halo_ref)
        field = jnp.where(lane < 56, tile_of(c, 0, *args), 0.0)
        field = jnp.where((lane >= 60) & (lane < 116), pltpu.roll(tile_of(c, last, *args), 116, axis=2), field)
        field = jnp.where((lane >= 116) & (lane < 116 + width), pltpu.roll(from_right, 116 - offset, axis=2), field)
        field = jnp.where(lane >= 128 - width, pltpu.roll(from_left, offset, axis=2), field)
        fields.append(field)
    sa, sb, ra, rb = iterate(*fields)
    near = lane[:, 0:8, :]
    for k, (sol, res) in enumerate(((sa, ra), (sb, rb))):
        for out_ref, in_ref, value in ((sol_ref, sol_in_ref, sol), (res_ref, res_in_ref, res)):
            value = value[:, 0:8, :]
            for t in range(last + 1):
                lanes = slice(t * 128, (t + 1) * 128)
                tile = in_ref[k, :, :, lanes]
                if t == 0:
                    tile = jnp.where(near < 8, value, tile)
                if t == last:
                    tile = jnp.where(near >= 120, pltpu.roll(value, 12, axis=2), tile)
                out_ref[k, :, :, lanes] = tile


def in_vmem(n):
    return [pl.BlockSpec(memory_space=pltpu.VMEM)] * n


def shape(*dims):
    return jax.ShapeDtypeStruct(dims, f32)


def per_device(rhs_field, permittivity, surf_dist, surf_normal, surf_inc, surf_cell, surf_mask, surf_owner):
    planes, rows, cols = permittivity.shape
    blocks, points = surf_cell.shape
    gx, gy = lax.axis_size("gx"), lax.axis_size("gy")
    devices = gx * gy
    slots = devices * CAP
    params = pltpu.CompilerParams(vmem_limit_bytes=48 << 20)
    send = pl.pallas_call(
        pack_kernel,
        out_shape=shape(slots * CHANNELS, points),
        in_specs=[pl.BlockSpec(memory_space=pltpu.HBM)] * 6,
        out_specs=pl.BlockSpec(memory_space=pltpu.VMEM),
        scratch_shapes=[
            pltpu.SMEM((blocks,), jnp.int32),
            pltpu.SMEM((devices,), jnp.int32),
            pltpu.VMEM((blocks, points), f32),
            pltpu.VMEM((CHANNELS - 1, blocks, points), f32),
            pltpu.VMEM((8 * blocks, points), f32),
            pltpu.VMEM((blocks, points), jnp.int32),
            pltpu.VMEM((blocks, points), jnp.int32),
            pltpu.SemaphoreType.DMA((6,)),
        ],
        compiler_params=params,
        name="pack",
    )(*[
        pltpu.with_memory_space_constraint(x, pltpu.HBM)
        for x in (surf_owner[:, 0], surf_dist, surf_normal, surf_inc, surf_cell, surf_mask)
    ])
    recv = lax.all_to_all(send.reshape(-1), ("gx", "gy"), split_axis=0, concat_axis=0, tiled=True)
    recv = recv.reshape(slots * CHANNELS, points)
    cells = planes * rows
    rhs_field = rhs_field.reshape(2, cells, cols)
    permittivity = permittivity.reshape(cells, cols)

    tiles = cols // 128

    def cost(parts):
        flops = 2 * parts * cols * slots * points
        return pl.CostEstimate(flops=flops, transcendentals=0, bytes_accessed=slots * CHANNELS * points * 4)

    strip = shape(13 * planes, cols)
    parts = 24 * planes + 14 * planes
    local = shape(slots, points)
    kept, edges, pair, other, hi, lo = pl.pallas_call(
        first_kernel,
        out_shape=(shape(2, tiles, cells, 128), shape(4, 2 * planes, cols), strip, strip, local, local),
        in_specs=in_vmem(3),
        out_specs=tuple(in_vmem(6)),
        scratch_shapes=[pltpu.VMEM((parts, cols), f32), pltpu.VMEM((3, tiles, cells, 128), f32)],
        compiler_params=params,
        cost_estimate=cost(parts),
        name="first",
    )(recv, rhs_field, permittivity)
    from_other = lax.ppermute(other, "gx", [(i, (((i + 1) ^ 1) - 1) % gx) for i in range(gx)])
    from_pair = lax.ppermute(pair, "gx", [(i, i ^ 1) for i in range(gx)])
    parts = 7 * 6 * planes + 4 * 2 * planes
    r1, wn = pl.pallas_call(
        second_kernel,
        out_shape=(shape(2, cells, cols), shape(4, tiles, cells, 128)),
        in_specs=in_vmem(5),
        out_specs=tuple(in_vmem(2)),
        scratch_shapes=[pltpu.VMEM((parts, cols), f32), pltpu.VMEM((2, tiles, cells, 128), f32)],
        compiler_params=params,
        cost_estimate=cost(parts),
        name="second",
    )(recv, hi, lo, kept, edges)
    pair, other, halo = pl.pallas_call(
        strip_kernel,
        out_shape=(shape(16, 128), shape(16, 128), shape(7, tiles, cells, 128)),
        in_specs=in_vmem(5),
        out_specs=tuple(in_vmem(3)),
        compiler_params=params,
        name="strips",
    )(r1, permittivity, wn, from_pair, from_other)
    from_other = lax.ppermute(other, "gy", [(i, (((i + 1) ^ 1) - 1) % gy) for i in range(gy)])
    field = shape(2, planes, rows, cols)
    sol, res, pair = pl.pallas_call(
        inner_kernel,
        out_shape=(field, field, shape(16, 128)),
        in_specs=in_vmem(5),
        out_specs=tuple(in_vmem(3)),
        compiler_params=params,
        cost_estimate=cost(8 * planes),
        name="inner",
    )(r1, permittivity, wn, halo, pair)
    from_pair = lax.ppermute(pair, "gy", [(i, i ^ 1) for i in range(gy)])
    return pl.pallas_call(
        final_kernel,
        out_shape=(field, field),
        in_specs=in_vmem(8),
        out_specs=tuple(in_vmem(2)),
        compiler_params=params,
        name="final",
    )(r1, permittivity, wn, halo, sol, res, from_pair, from_other)


def solution(mesh):
    split = ("gx", "gy")
    placed = (
        P(None, None, "gx", "gy"),
        P(None, "gx", "gy"),
        P(split, None),
        P(None, split, None),
        P(None, split, None),
        P(split, None),
        P(split, None),
        P(split, None),
    )
    return jax.shard_map(
        per_device,
        mesh=mesh,
        in_specs=placed,
        out_specs=(P(None, None, "gx", "gy"), P(None, None, "gx", "gy")),
        check_vma=False,
    )
```

```python
import functools

import jax
import jax.numpy as jnp
from jax import lax
from jax.experimental import pallas as pl
from jax.experimental.pallas import tpu as pltpu
from jax.sharding import PartitionSpec as P

CAP = 2
K_SQUARED = 0.25
BETA = 0.5
OMEGA = 0.8
TAU = 1.0

CHANNELS = 6
GROUP = 128

f32 = jnp.float32
bf16 = jnp.bfloat16


def pack_kernel(
    owner_hbm, dist_hbm, normal_hbm, inc_hbm, cell_hbm, mask_hbm, out_ref,
    owner_ref, first_ref, dist_ref, raw_ref, coef_ref, cell_ref, mask_ref, sems,
):
    blocks = dist_ref.shape[0]
    copies = [
        pltpu.make_async_copy(owner_hbm, owner_ref, sems.at[0]),
        pltpu.make_async_copy(dist_hbm, dist_ref, sems.at[1]),
        pltpu.make_async_copy(normal_hbm, raw_ref.at[pl.ds(0, 3)], sems.at[2]),
        pltpu.make_async_copy(inc_hbm, raw_ref.at[pl.ds(3, 2)], sems.at[3]),
        pltpu.make_async_copy(cell_hbm, cell_ref, sems.at[4]),
        pltpu.make_async_copy(mask_hbm, mask_ref, sems.at[5]),
    ]
    for copy in copies:
        copy.start()
    out_ref[...] = jnp.full(out_ref.shape, -1.0, f32)

    copies[0].wait()

    def note(i, carry):
        b = blocks - 1 - i
        first_ref[owner_ref[b]] = b
        return carry

    lax.fori_loop(0, blocks, note, 0, unroll=16)
    for copy in copies[1:]:
        copy.wait()
    half = 0.5 * TAU * dist_ref[...]
    for k in range(3):
        rows = slice(k * blocks, (k + 1) * blocks)
        coef_ref[rows] = half * raw_ref[k]
    for k in range(3, 5):
        coef_ref[k * blocks : (k + 1) * blocks] = TAU * raw_ref[k]
    coef_ref[5 * blocks : 6 * blocks] = jnp.where(mask_ref[...] > 0, cell_ref[...], 1 << 14).astype(f32)

    def place(b, carry):
        owner = owner_ref[b]
        base = (owner * CAP + jnp.where(first_ref[owner] == b, 0, 1)) * CHANNELS
        out_ref[pl.ds(base, CHANNELS), :] = coef_ref[pl.ds(b, CHANNELS, stride=blocks), :]
        return carry

    lax.fori_loop(0, blocks, place, 0, unroll=8)


def split_cells(recv_ref, hi_ref, lo_ref):
    slots = hi_ref.shape[0]
    chunk = min(64, slots)
    for i in range(0, slots, chunk):
        cell = recv_ref[pl.ds(i * CHANNELS + CHANNELS - 1, chunk, stride=CHANNELS), :].astype(jnp.int32)
        hi_ref[i : i + chunk] = (cell >> 8).astype(f32)
        lo_ref[i : i + chunk] = (cell & 255).astype(f32)


def scatter_slots(recv_ref, hi_ref, lo_ref, acc_ref, groups):
    slots = hi_ref.shape[0]
    lo_n = acc_ref.shape[1]
    per_step = min(GROUP, slots)
    acc_ref[...] = jnp.zeros(acc_ref.shape, f32)
    one = jnp.ones((), bf16)
    zero = jnp.zeros((), bf16)
    targets = []
    for rows, _, _ in groups:
        place = lax.broadcasted_iota(jnp.int32, (8 * len(rows), 128), 0)
        item = place >> 3
        row = jnp.zeros_like(place)
        for k, r in enumerate(rows):
            row = jnp.where(item == k, r, row)
        targets.append(((place & 7) * 8 + row).astype(f32).astype(bf16))
    lo_iota = lax.broadcasted_iota(jnp.int32, (lo_n, 128), 0).astype(f32).astype(bf16)

    def load(ref, index):
        return jnp.broadcast_to(ref[pl.ds(index, 1), :], (16, 128))

    def tall(tile, n):
        return jnp.concatenate([tile] * (n // 16), axis=0)

    def step(g, carry):
        left, right = [], []
        for j in range(per_step):
            slot = g * per_step + j
            hi = load(hi_ref, slot).astype(bf16)
            pieces = []
            for target, (rows, channels, count) in zip(targets, groups):
                n = 8 * len(rows)
                hot = target == tall(hi, n)
                for c in channels:
                    value = load(recv_ref, slot * CHANNELS + c)
                    lead = value.astype(bf16)
                    rest = (value - lead.astype(f32)).astype(bf16)
                    pieces.append(jnp.where(hot, tall(lead, n), zero))
                    pieces.append(jnp.where(hot, tall(rest, n), zero))
                if count:
                    pieces.append(jnp.where(hot, one, zero))
            left.append(jnp.concatenate(pieces, axis=0))
            right.append(jnp.where(lo_iota == tall(load(lo_ref, slot).astype(bf16), lo_n), one, zero))
        acc_ref[...] += lax.dot_general(
            jnp.concatenate(left, axis=1),
            jnp.concatenate(right, axis=1),
            (((1,), (1,)), ((), ())),
            preferred_element_type=f32,
        )
        return carry

    lax.fori_loop(0, slots // per_step, step, 0)
    sums, start = [], 0
    for rows, channels, count in groups:
        n = 8 * len(rows)
        found = []
        for _ in channels:
            found.append(acc_ref[start : start + n, :] + acc_ref[start + n : start + 2 * n, :])
            start += 2 * n
        if count:
            found.append(acc_ref[start : start + n, :])
            start += n
        sums.append(found)
    return sums


def keep_tiles(ref, k, value):
    for t in range(ref.shape[1]):
        ref[k, t] = value[:, t * 128 : (t + 1) * 128]


def load_rows(ref, k, t, row):
    return ref[k, t, pl.ds(row, ref.shape[2] // 8, stride=8), :]


def store_rows(ref, k, row, value):
    for t in range(ref.shape[1]):
        ref[k, t, pl.ds(row, ref.shape[2] // 8, stride=8), :] = value[:, t * 128 : (t + 1) * 128]


OUTER = (0, 1, 2, 5, 6, 7)
MIDDLE = (3, 4)
EDGES = (0, 7)
INNER = (1, 2, 3, 4, 5, 6)
FIELDS = ((0, 1, 2), True)


def subtract_rows(tile_ref, k, rows, sums):
    planes = tile_ref.shape[2] // 8
    for j, r in enumerate(rows):
        before = jnp.concatenate([load_rows(tile_ref, k, t, r) for t in range(tile_ref.shape[1])], axis=1)
        store_rows(tile_ref, k, r, before - sums[j * planes : (j + 1) * planes])


def first_kernel(
    recv_ref, rhs_ref, perm_ref, kept_ref, edge_ref, pair_ref, other_ref, hi_ref, lo_ref, acc_ref, tile_ref
):
    split_cells(recv_ref, hi_ref, lo_ref)
    incident, fields = scatter_slots(recv_ref, hi_ref, lo_ref, acc_ref, ((OUTER, (3, 4), False), (EDGES,) + FIELDS))
    planes = perm_ref.shape[0] // 8
    for k in range(2):
        keep_tiles(tile_ref, k, rhs_ref[k])
        subtract_rows(tile_ref, k, OUTER, incident[k])
        kept_ref[k] = tile_ref[k]
    keep_tiles(tile_ref, 2, perm_ref[...])
    fields = [TAU * fields[3]] + fields[:3]
    for k in range(4):
        edge_ref[k] = fields[k]
    place = lax.axis_index("gx")
    even = lax.rem(place, 2) == 0
    top, bottom = place == 0, place == lax.axis_size("gx") - 1
    for t in range(tile_ref.shape[1]):
        lanes = slice(t * 128, (t + 1) * 128)
        for c in range(7):
            for k in range(3 if c < 3 else 1):
                if c < 3:
                    item = 3 * c + k
                    first, last = load_rows(tile_ref, c, t, k), load_rows(tile_ref, c, t, 5 + k)
                else:
                    item = 6 + c
                    first, last = fields[c - 3][0:planes, lanes], fields[c - 3][planes : 2 * planes, lanes]
                if c == 2:
                    first, last = jnp.where(top, 0.0, first), jnp.where(bottom, 0.0, last)
                rows = slice(item * planes, (item + 1) * planes)
                pair_ref[rows, lanes] = jnp.where(even, last, first)
                other_ref[rows, lanes] = jnp.where(even, first, last)


def second_kernel(recv_ref, hi_ref, lo_ref, kept_ref, edge_ref, r1_ref, wn_ref, acc_ref, tile_ref):
    incident, fields = scatter_slots(recv_ref, hi_ref, lo_ref, acc_ref, ((MIDDLE, (3, 4), False), (INNER,) + FIELDS))
    for k in range(2):
        tile_ref[k] = kept_ref[k]
        subtract_rows(tile_ref, k, MIDDLE, incident[k])
        r1_ref[k] = jnp.concatenate([tile_ref[k, t] for t in range(tile_ref.shape[1])], axis=1)
    planes = edge_ref.shape[1] // 2
    for k, value in enumerate([TAU * fields[3]] + fields[:3]):
        for j, r in enumerate(EDGES):
            store_rows(wn_ref, k, r, edge_ref[k, j * planes : (j + 1) * planes])
        for j, r in enumerate(INNER):
            store_rows(wn_ref, k, r, value[j * planes : (j + 1) * planes])


COL_PLACE = ((0, 3), (3, 3), (6, 3), (9, 1), (10, 1), (11, 1), (12, 1))


def strip_kernel(r1_ref, perm_ref, wn_ref, pair_ref, other_ref, out_pair_ref, out_other_ref, halo_ref):
    planes = perm_ref.shape[0] // 8
    lo_n = perm_ref.shape[1]
    even = lax.rem(lax.axis_index("gx"), 2) == 0
    halo_ref[...] = jnp.zeros(halo_ref.shape, f32)
    for c in range(7):
        width = 3 if c < 3 else 1
        for k in range(width):
            item = 3 * c + k if c < 3 else 6 + c
            rows = slice(item * planes, (item + 1) * planes)
            pair, other = pair_ref[rows, :], other_ref[rows, :]
            store_rows(halo_ref, c, k, jnp.where(even, pair, other))
            store_rows(halo_ref, c, 8 - width + k, jnp.where(even, other, pair))
    lane = lax.broadcasted_iota(jnp.int32, (planes, 16, 128), 2)
    position = lax.axis_index("gy")
    even = lax.rem(position, 2) == 0
    last = lax.axis_size("gy") - 1
    nothing = jnp.zeros((planes, 8, 128), f32)
    strips = []
    for start, sign, edge in ((0, 1, 0), (lo_n - 128, -1, last)):
        place = lane if sign > 0 else 127 - lane
        strip = jnp.zeros((planes, 16, 128), f32)
        for c in range(7):
            if c < 3:
                own = perm_ref[:, pl.ds(start, 128)] if c == 2 else r1_ref[c, :, pl.ds(start, 128)]
                other = halo_ref[c, start // 128].reshape(planes, 8, 128)
            else:
                own, other = wn_ref[c - 3, start // 128], nothing
            full = jnp.concatenate([own.reshape(planes, 8, 128), other], axis=1)
            offset, width = COL_PLACE[c]
            moved = pltpu.roll(full, (sign * offset) % 128, axis=2)
            strip = jnp.where((place >= offset) & (place < offset + width), moved, strip)
        strips.append(jnp.where(position == edge, 0.0, strip))
    lane = lax.broadcasted_iota(jnp.int32, (16, 128), 1)
    packed = []
    for strip, base in zip(strips, (0, 112)):
        flat = jnp.zeros((16, 128), f32)
        for p in range(planes):
            flat = jnp.where(lane >> 4 == p, pltpu.roll(strip[p], (16 * p - base) % 128, axis=1), flat)
        packed.append(flat)
    out_pair_ref[...] = jnp.where(even, packed[1], packed[0])
    out_other_ref[...] = jnp.where(even, packed[0], packed[1])


def iterate(re, im, perm, w, nz, nx, ny):
    rows, cols = perm.shape[1:]
    diag = 6.0 - K_SQUARED * perm
    shift = BETA * K_SQUARED * perm
    inside = perm > 0.5
    inverse = jnp.where(inside, OMEGA / (diag * diag + shift * shift), 0.0)
    inv_re = diag * inverse
    inv_im = -shift * inverse

    def damp(a, b):
        return a * inv_re - b * inv_im, a * inv_im + b * inv_re

    def sides(v):
        nothing = jnp.zeros((1,) + v.shape[1:], f32)
        after = jnp.concatenate([v[1:], nothing], axis=0)
        before = jnp.concatenate([nothing, v[:-1]], axis=0)
        return (
            (after, before),
            (pltpu.roll(v, rows - 1, axis=1), pltpu.roll(v, 1, axis=1)),
            (pltpu.roll(v, cols - 1, axis=2), pltpu.roll(v, 1, axis=2)),
        )

    def helm(v, pairs):
        total = pairs[0][0] + pairs[0][1]
        for a, b in pairs[1:]:
            total = total + a + b
        return diag * v - total

    def swept(a, b):
        za, zb = damp(a, b)
        ma = helm(za, sides(za)) - shift * zb
        mb = helm(zb, sides(zb)) + shift * za
        da, db = damp(a - ma, b - mb)
        return za + da, zb + db

    def surface(v, pairs):
        (a, b), (c, d), (e, f) = pairs
        return w * v + nz * (a - b) + nx * (c - d) + ny * (e - f)

    def remaining(r, v):
        pairs = sides(v)
        return r - helm(v, pairs) - surface(v, pairs)

    sa, sb = swept(re, im)
    ra, rb = remaining(re, sa), remaining(im, sb)
    ua, ub = swept(ra, rb)
    return sa + ua, sb + ub, ra, rb


def tile_of(c, t, r1_ref, perm_ref, wn_ref, halo_ref):
    planes = perm_ref.shape[0] // 8
    lanes = slice(t * 128, (t + 1) * 128)
    if c < 3:
        own = perm_ref[:, lanes] if c == 2 else r1_ref[c, :, lanes]
    else:
        own = wn_ref[c - 3, t]
    return jnp.concatenate([own.reshape(planes, 8, 128), halo_ref[c, t].reshape(planes, 8, 128)], axis=1)


def inner_kernel(r1_ref, perm_ref, wn_ref, halo_ref, pair_ref, sol_ref, res_ref, pair_out_ref):
    pair_out_ref[...] = pair_ref[...]
    tiles = halo_ref.shape[1]
    fields = [
        jnp.concatenate([tile_of(c, t, r1_ref, perm_ref, wn_ref, halo_ref) for t in range(tiles)], axis=2)
        for c in range(7)
    ]
    sa, sb, ra, rb = iterate(*fields)
    for k, (sol, res) in enumerate(((sa, ra), (sb, rb))):
        sol_ref[k] = sol[:, 0:8, :]
        res_ref[k] = res[:, 0:8, :]


def near_kernel(r1_ref, perm_ref, wn_ref, halo_ref, near_ref):
    lane = lax.broadcasted_iota(jnp.int32, near_ref.shape[1:], 2)
    last = halo_ref.shape[1] - 1
    for c in range(7):
        head = tile_of(c, 0, r1_ref, perm_ref, wn_ref, halo_ref)
        tail = pltpu.roll(tile_of(c, last, r1_ref, perm_ref, wn_ref, halo_ref), 116, axis=2)
        near_ref[c] = jnp.where(lane < 56, head, jnp.where((lane >= 60) & (lane < 116), tail, 0.0))


def final_kernel(near_ref, sol_in_ref, res_in_ref, pair_ref, other_ref, sol_ref, res_ref):
    planes = near_ref.shape[1]
    last = sol_ref.shape[3] // 128 - 1
    lane = lax.broadcasted_iota(jnp.int32, (planes, 16, 128), 2)
    even = lax.rem(lax.axis_index("gy"), 2) == 0
    pair, other = pair_ref[...], other_ref[...]
    from_right = jnp.where(even, pair, other)
    from_left = jnp.where(even, other, pair)
    from_right = jnp.stack([pltpu.roll(from_right, (-16 * p) % 128, axis=1) for p in range(planes)])
    from_left = jnp.stack([pltpu.roll(from_left, (112 - 16 * p) % 128, axis=1) for p in range(planes)])
    fields = []
    for c in range(7):
        offset, width = COL_PLACE[c]
        right = (lane >= 116) & (lane < 116 + width)
        field = jnp.where(right, pltpu.roll(from_right, 116 - offset, axis=2), near_ref[c])
        field = jnp.where(lane >= 128 - width, pltpu.roll(from_left, offset, axis=2), field)
        fields.append(field)
    sa, sb, ra, rb = iterate(*fields)
    near = lane[:, 0:8, :]
    for k, (sol, res) in enumerate(((sa, ra), (sb, rb))):
        for out_ref, in_ref, value in ((sol_ref, sol_in_ref, sol), (res_ref, res_in_ref, res)):
            value = value[:, 0:8, :]
            for t in range(last + 1):
                lanes = slice(t * 128, (t + 1) * 128)
                tile = in_ref[k, :, :, lanes]
                if t == 0:
                    tile = jnp.where(near < 8, value, tile)
                if t == last:
                    tile = jnp.where(near >= 120, pltpu.roll(value, 12, axis=2), tile)
                out_ref[k, :, :, lanes] = tile


def in_vmem(n):
    return [pl.BlockSpec(memory_space=pltpu.VMEM)] * n


def shape(*dims):
    return jax.ShapeDtypeStruct(dims, f32)


def per_device(rhs_field, permittivity, surf_dist, surf_normal, surf_inc, surf_cell, surf_mask, surf_owner):
    planes, rows, cols = permittivity.shape
    blocks, points = surf_cell.shape
    gx, gy = lax.axis_size("gx"), lax.axis_size("gy")
    devices = gx * gy
    slots = devices * CAP
    params = pltpu.CompilerParams(vmem_limit_bytes=48 << 20)
    send = pl.pallas_call(
        pack_kernel,
        out_shape=shape(slots * CHANNELS, points),
        in_specs=[pl.BlockSpec(memory_space=pltpu.HBM)] * 6,
        out_specs=pl.BlockSpec(memory_space=pltpu.VMEM),
        scratch_shapes=[
            pltpu.SMEM((blocks,), jnp.int32),
            pltpu.SMEM((devices,), jnp.int32),
            pltpu.VMEM((blocks, points), f32),
            pltpu.VMEM((CHANNELS - 1, blocks, points), f32),
            pltpu.VMEM((8 * blocks, points), f32),
            pltpu.VMEM((blocks, points), jnp.int32),
            pltpu.VMEM((blocks, points), jnp.int32),
            pltpu.SemaphoreType.DMA((6,)),
        ],
        compiler_params=params,
        name="pack",
    )(*[
        pltpu.with_memory_space_constraint(x, pltpu.HBM)
        for x in (surf_owner[:, 0], surf_dist, surf_normal, surf_inc, surf_cell, surf_mask)
    ])
    recv = lax.all_to_all(send.reshape(-1), ("gx", "gy"), split_axis=0, concat_axis=0, tiled=True)
    recv = recv.reshape(slots * CHANNELS, points)
    cells = planes * rows
    rhs_field = rhs_field.reshape(2, cells, cols)
    permittivity = permittivity.reshape(cells, cols)

    tiles = cols // 128

    def cost(parts):
        flops = 2 * parts * cols * slots * points
        return pl.CostEstimate(flops=flops, transcendentals=0, bytes_accessed=slots * CHANNELS * points * 4)

    strip = shape(13 * planes, cols)
    parts = 24 * planes + 14 * planes
    local = shape(slots, points)
    kept, edges, pair, other, hi, lo = pl.pallas_call(
        first_kernel,
        out_shape=(shape(2, tiles, cells, 128), shape(4, 2 * planes, cols), strip, strip, local, local),
        in_specs=in_vmem(3),
        out_specs=tuple(in_vmem(6)),
        scratch_shapes=[pltpu.VMEM((parts, cols), f32), pltpu.VMEM((3, tiles, cells, 128), f32)],
        compiler_params=params,
        cost_estimate=cost(parts),
        name="first",
    )(recv, rhs_field, permittivity)
    from_other = lax.ppermute(other, "gx", [(i, (((i + 1) ^ 1) - 1) % gx) for i in range(gx)])
    from_pair = lax.ppermute(pair, "gx", [(i, i ^ 1) for i in range(gx)])
    parts = 7 * 6 * planes + 4 * 2 * planes
    r1, wn = pl.pallas_call(
        second_kernel,
        out_shape=(shape(2, cells, cols), shape(4, tiles, cells, 128)),
        in_specs=in_vmem(5),
        out_specs=tuple(in_vmem(2)),
        scratch_shapes=[pltpu.VMEM((parts, cols), f32), pltpu.VMEM((2, tiles, cells, 128), f32)],
        compiler_params=params,
        cost_estimate=cost(parts),
        name="second",
    )(recv, hi, lo, kept, edges)
    pair, other, halo = pl.pallas_call(
        strip_kernel,
        out_shape=(shape(16, 128), shape(16, 128), shape(7, tiles, cells, 128)),
        in_specs=in_vmem(5),
        out_specs=tuple(in_vmem(3)),
        compiler_params=params,
        name="strips",
    )(r1, permittivity, wn, from_pair, from_other)
    from_other = lax.ppermute(other, "gy", [(i, (((i + 1) ^ 1) - 1) % gy) for i in range(gy)])
    field = shape(2, planes, rows, cols)
    sol, res, pair = pl.pallas_call(
        inner_kernel,
        out_shape=(field, field, shape(16, 128)),
        in_specs=in_vmem(5),
        out_specs=tuple(in_vmem(3)),
        compiler_params=params,
        cost_estimate=cost(8 * planes),
        name="inner",
    )(r1, permittivity, wn, halo, pair)
    near = pl.pallas_call(
        near_kernel,
        out_shape=shape(7, planes, 16, 128),
        in_specs=in_vmem(4),
        out_specs=in_vmem(1)[0],
        compiler_params=params,
        cost_estimate=cost(8 * planes),
        name="near",
    )(r1, permittivity, wn, halo)
    from_pair = lax.ppermute(pair, "gy", [(i, i ^ 1) for i in range(gy)])
    return pl.pallas_call(
        final_kernel,
        out_shape=(field, field),
        in_specs=in_vmem(5),
        out_specs=tuple(in_vmem(2)),
        compiler_params=params,
        name="final",
    )(near, sol, res, from_pair, from_other)


def solution(mesh):
    split = ("gx", "gy")
    placed = (
        P(None, None, "gx", "gy"),
        P(None, "gx", "gy"),
        P(split, None),
        P(None, split, None),
        P(None, split, None),
        P(split, None),
        P(split, None),
        P(split, None),
    )
    return jax.shard_map(
        per_device,
        mesh=mesh,
        in_specs=placed,
        out_specs=(P(None, None, "gx", "gy"), P(None, None, "gx", "gy")),
        check_vma=False,
    )
```

```python
import functools

import jax
import jax.numpy as jnp
from jax import lax
from jax.experimental import pallas as pl
from jax.experimental.pallas import tpu as pltpu
from jax.sharding import PartitionSpec as P

CAP = 2
K_SQUARED = 0.25
BETA = 0.5
OMEGA = 0.8
TAU = 1.0

CHANNELS = 6
GROUP = 128

f32 = jnp.float32
bf16 = jnp.bfloat16


def pack_kernel(
    owner_hbm, dist_hbm, normal_hbm, inc_hbm, cell_hbm, mask_hbm, out_ref,
    owner_ref, first_ref, dist_ref, raw_ref, coef_ref, cell_ref, mask_ref, sems,
):
    blocks = dist_ref.shape[0]
    copies = [
        pltpu.make_async_copy(owner_hbm, owner_ref, sems.at[0]),
        pltpu.make_async_copy(dist_hbm, dist_ref, sems.at[1]),
        pltpu.make_async_copy(normal_hbm, raw_ref.at[pl.ds(0, 3)], sems.at[2]),
        pltpu.make_async_copy(inc_hbm, raw_ref.at[pl.ds(3, 2)], sems.at[3]),
        pltpu.make_async_copy(cell_hbm, cell_ref, sems.at[4]),
        pltpu.make_async_copy(mask_hbm, mask_ref, sems.at[5]),
    ]
    for copy in copies:
        copy.start()
    out_ref[...] = jnp.full(out_ref.shape, -1.0, f32)

    copies[0].wait()

    def note(i, carry):
        b = blocks - 1 - i
        first_ref[owner_ref[b]] = b
        return carry

    lax.fori_loop(0, blocks, note, 0, unroll=16)
    for copy in copies[1:]:
        copy.wait()
    half = 0.5 * TAU * dist_ref[...]
    for k in range(3):
        rows = slice(k * blocks, (k + 1) * blocks)
        coef_ref[rows] = half * raw_ref[k]
    for k in range(3, 5):
        coef_ref[k * blocks : (k + 1) * blocks] = TAU * raw_ref[k]
    coef_ref[5 * blocks : 6 * blocks] = jnp.where(mask_ref[...] > 0, cell_ref[...], 1 << 14).astype(f32)

    def place(b, carry):
        owner = owner_ref[b]
        base = (owner * CAP + jnp.where(first_ref[owner] == b, 0, 1)) * CHANNELS
        out_ref[pl.ds(base, CHANNELS), :] = coef_ref[pl.ds(b, CHANNELS, stride=blocks), :]
        return carry

    lax.fori_loop(0, blocks, place, 0, unroll=4)


def split_cells(recv_ref, hi_ref, lo_ref):
    slots = hi_ref.shape[0]
    chunk = min(64, slots)
    for i in range(0, slots, chunk):
        cell = recv_ref[pl.ds(i * CHANNELS + CHANNELS - 1, chunk, stride=CHANNELS), :].astype(jnp.int32)
        hi_ref[i : i + chunk] = (cell >> 8).astype(f32)
        lo_ref[i : i + chunk] = (cell & 255).astype(f32)


def scatter_slots(recv_ref, hi_ref, lo_ref, acc_ref, groups):
    slots = hi_ref.shape[0]
    lo_n = acc_ref.shape[1]
    per_step = min(GROUP, slots)
    acc_ref[...] = jnp.zeros(acc_ref.shape, f32)
    one = jnp.ones((), bf16)
    zero = jnp.zeros((), bf16)
    targets = []
    for rows, _, _ in groups:
        place = lax.broadcasted_iota(jnp.int32, (8 * len(rows), 128), 0)
        item = place >> 3
        row = jnp.zeros_like(place)
        for k, r in enumerate(rows):
            row = jnp.where(item == k, r, row)
        targets.append(((place & 7) * 8 + row).astype(f32).astype(bf16))
    lo_iota = lax.broadcasted_iota(jnp.int32, (lo_n, 128), 0).astype(f32).astype(bf16)

    def load(ref, index):
        return jnp.broadcast_to(ref[pl.ds(index, 1), :], (16, 128))

    def tall(tile, n):
        return jnp.concatenate([tile] * (n // 16), axis=0)

    def step(g, carry):
        left, right = [], []
        for j in range(per_step):
            slot = g * per_step + j
            hi = load(hi_ref, slot).astype(bf16)
            pieces = []
            for target, (rows, channels, count) in zip(targets, groups):
                n = 8 * len(rows)
                hot = target == tall(hi, n)
                for c in channels:
                    value = load(recv_ref, slot * CHANNELS + c)
                    lead = value.astype(bf16)
                    rest = (value - lead.astype(f32)).astype(bf16)
                    pieces.append(jnp.where(hot, tall(lead, n), zero))
                    pieces.append(jnp.where(hot, tall(rest, n), zero))
                if count:
                    pieces.append(jnp.where(hot, one, zero))
            left.append(jnp.concatenate(pieces, axis=0))
            right.append(jnp.where(lo_iota == tall(load(lo_ref, slot).astype(bf16), lo_n), one, zero))
        acc_ref[...] += lax.dot_general(
            jnp.concatenate(left, axis=1),
            jnp.concatenate(right, axis=1),
            (((1,), (1,)), ((), ())),
            preferred_element_type=f32,
        )
        return carry

    lax.fori_loop(0, slots // per_step, step, 0)
    sums, start = [], 0
    for rows, channels, count in groups:
        n = 8 * len(rows)
        found = []
        for _ in channels:
            found.append(acc_ref[start : start + n, :] + acc_ref[start + n : start + 2 * n, :])
            start += 2 * n
        if count:
            found.append(acc_ref[start : start + n, :])
            start += n
        sums.append(found)
    return sums


def keep_tiles(ref, k, value):
    for t in range(ref.shape[1]):
        ref[k, t] = value[:, t * 128 : (t + 1) * 128]


def load_rows(ref, k, t, row):
    return ref[k, t, pl.ds(row, ref.shape[2] // 8, stride=8), :]


def store_rows(ref, k, row, value):
    for t in range(ref.shape[1]):
        ref[k, t, pl.ds(row, ref.shape[2] // 8, stride=8), :] = value[:, t * 128 : (t + 1) * 128]


OUTER = (0, 1, 2, 5, 6, 7)
MIDDLE = (3, 4)
EDGES = (0, 7)
INNER = (1, 2, 3, 4, 5, 6)
FIELDS = ((0, 1, 2), True)


def subtract_rows(tile_ref, k, rows, sums):
    planes = tile_ref.shape[2] // 8
    for j, r in enumerate(rows):
        before = jnp.concatenate([load_rows(tile_ref, k, t, r) for t in range(tile_ref.shape[1])], axis=1)
        store_rows(tile_ref, k, r, before - sums[j * planes : (j + 1) * planes])


def first_kernel(
    recv_ref, rhs_ref, perm_ref, kept_ref, edge_ref, pair_ref, other_ref, hi_ref, lo_ref, acc_ref, tile_ref
):
    split_cells(recv_ref, hi_ref, lo_ref)
    incident, fields = scatter_slots(recv_ref, hi_ref, lo_ref, acc_ref, ((OUTER, (3, 4), False), (EDGES,) + FIELDS))
    planes = perm_ref.shape[0] // 8
    for k in range(2):
        keep_tiles(tile_ref, k, rhs_ref[k])
        subtract_rows(tile_ref, k, OUTER, incident[k])
        kept_ref[k] = tile_ref[k]
    keep_tiles(tile_ref, 2, perm_ref[...])
    fields = [TAU * fields[3]] + fields[:3]
    for k in range(4):
        edge_ref[k] = fields[k]
    place = lax.axis_index("gx")
    even = lax.rem(place, 2) == 0
    top, bottom = place == 0, place == lax.axis_size("gx") - 1
    for t in range(tile_ref.shape[1]):
        lanes = slice(t * 128, (t + 1) * 128)
        for c in range(7):
            for k in range(3 if c < 3 else 1):
                if c < 3:
                    item = 3 * c + k
                    first, last = load_rows(tile_ref, c, t, k), load_rows(tile_ref, c, t, 5 + k)
                else:
                    item = 6 + c
                    first, last = fields[c - 3][0:planes, lanes], fields[c - 3][planes : 2 * planes, lanes]
                if c == 2:
                    first, last = jnp.where(top, 0.0, first), jnp.where(bottom, 0.0, last)
                rows = slice(item * planes, (item + 1) * planes)
                pair_ref[rows, lanes] = jnp.where(even, last, first)
                other_ref[rows, lanes] = jnp.where(even, first, last)


def second_kernel(recv_ref, hi_ref, lo_ref, kept_ref, edge_ref, r1_ref, wn_ref, acc_ref, tile_ref):
    incident, fields = scatter_slots(recv_ref, hi_ref, lo_ref, acc_ref, ((MIDDLE, (3, 4), False), (INNER,) + FIELDS))
    for k in range(2):
        tile_ref[k] = kept_ref[k]
        subtract_rows(tile_ref, k, MIDDLE, incident[k])
        r1_ref[k] = jnp.concatenate([tile_ref[k, t] for t in range(tile_ref.shape[1])], axis=1)
    planes = edge_ref.shape[1] // 2
    for k, value in enumerate([TAU * fields[3]] + fields[:3]):
        for j, r in enumerate(EDGES):
            store_rows(wn_ref, k, r, edge_ref[k, j * planes : (j + 1) * planes])
        for j, r in enumerate(INNER):
            store_rows(wn_ref, k, r, value[j * planes : (j + 1) * planes])


COL_PLACE = ((0, 3), (3, 3), (6, 3), (9, 1), (10, 1), (11, 1), (12, 1))


def strip_kernel(r1_ref, perm_ref, wn_ref, pair_ref, other_ref, out_pair_ref, out_other_ref, halo_ref):
    planes = perm_ref.shape[0] // 8
    lo_n = perm_ref.shape[1]
    even = lax.rem(lax.axis_index("gx"), 2) == 0
    halo_ref[...] = jnp.zeros(halo_ref.shape, f32)
    for c in range(7):
        width = 3 if c < 3 else 1
        for k in range(width):
            item = 3 * c + k if c < 3 else 6 + c
            rows = slice(item * planes, (item + 1) * planes)
            pair, other = pair_ref[rows, :], other_ref[rows, :]
            store_rows(halo_ref, c, k, jnp.where(even, pair, other))
            store_rows(halo_ref, c, 8 - width + k, jnp.where(even, other, pair))
    lane = lax.broadcasted_iota(jnp.int32, (planes, 16, 128), 2)
    position = lax.axis_index("gy")
    even = lax.rem(position, 2) == 0
    last = lax.axis_size("gy") - 1
    nothing = jnp.zeros((planes, 8, 128), f32)
    strips = []
    for start, sign, edge in ((0, 1, 0), (lo_n - 128, -1, last)):
        place = lane if sign > 0 else 127 - lane
        strip = jnp.zeros((planes, 16, 128), f32)
        for c in range(7):
            if c < 3:
                own = perm_ref[:, pl.ds(start, 128)] if c == 2 else r1_ref[c, :, pl.ds(start, 128)]
                other = halo_ref[c, start // 128].reshape(planes, 8, 128)
            else:
                own, other = wn_ref[c - 3, start // 128], nothing
            full = jnp.concatenate([own.reshape(planes, 8, 128), other], axis=1)
            offset, width = COL_PLACE[c]
            moved = pltpu.roll(full, (sign * offset) % 128, axis=2)
            strip = jnp.where((place >= offset) & (place < offset + width), moved, strip)
        strips.append(jnp.where(position == edge, 0.0, strip))
    lane = lax.broadcasted_iota(jnp.int32, (16, 128), 1)
    packed = []
    for strip, base in zip(strips, (0, 112)):
        flat = jnp.zeros((16, 128), f32)
        for p in range(planes):
            flat = jnp.where(lane >> 4 == p, pltpu.roll(strip[p], (16 * p - base) % 128, axis=1), flat)
        packed.append(flat)
    out_pair_ref[...] = jnp.where(even, packed[1], packed[0])
    out_other_ref[...] = jnp.where(even, packed[0], packed[1])


def iterate(re, im, perm, w, nz, nx, ny):
    rows, cols = perm.shape[1:]
    diag = 6.0 - K_SQUARED * perm
    shift = BETA * K_SQUARED * perm
    inside = perm > 0.5
    inverse = jnp.where(inside, OMEGA / (diag * diag + shift * shift), 0.0)
    inv_re = diag * inverse
    inv_im = -shift * inverse

    def damp(a, b):
        return a * inv_re - b * inv_im, a * inv_im + b * inv_re

    def sides(v):
        nothing = jnp.zeros((1,) + v.shape[1:], f32)
        after = jnp.concatenate([v[1:], nothing], axis=0)
        before = jnp.concatenate([nothing, v[:-1]], axis=0)
        return (
            (after, before),
            (pltpu.roll(v, rows - 1, axis=1), pltpu.roll(v, 1, axis=1)),
            (pltpu.roll(v, cols - 1, axis=2), pltpu.roll(v, 1, axis=2)),
        )

    def helm(v, pairs):
        total = pairs[0][0] + pairs[0][1]
        for a, b in pairs[1:]:
            total = total + a + b
        return diag * v - total

    def swept(a, b):
        za, zb = damp(a, b)
        ma = helm(za, sides(za)) - shift * zb
        mb = helm(zb, sides(zb)) + shift * za
        da, db = damp(a - ma, b - mb)
        return za + da, zb + db

    def surface(v, pairs):
        (a, b), (c, d), (e, f) = pairs
        return w * v + nz * (a - b) + nx * (c - d) + ny * (e - f)

    def remaining(r, v):
        pairs = sides(v)
        return r - helm(v, pairs) - surface(v, pairs)

    sa, sb = swept(re, im)
    ra, rb = remaining(re, sa), remaining(im, sb)
    ua, ub = swept(ra, rb)
    return sa + ua, sb + ub, ra, rb


def tile_of(c, t, r1_ref, perm_ref, wn_ref, halo_ref):
    planes = perm_ref.shape[0] // 8
    lanes = slice(t * 128, (t + 1) * 128)
    if c < 3:
        own = perm_ref[:, lanes] if c == 2 else r1_ref[c, :, lanes]
    else:
        own = wn_ref[c - 3, t]
    return jnp.concatenate([own.reshape(planes, 8, 128), halo_ref[c, t].reshape(planes, 8, 128)], axis=1)


def inner_kernel(r1_ref, perm_ref, wn_ref, halo_ref, pair_ref, sol_ref, res_ref, pair_out_ref):
    pair_out_ref[...] = pair_ref[...]
    tiles = halo_ref.shape[1]
    fields = [
        jnp.concatenate([tile_of(c, t, r1_ref, perm_ref, wn_ref, halo_ref) for t in range(tiles)], axis=2)
        for c in range(7)
    ]
    sa, sb, ra, rb = iterate(*fields)
    for k, (sol, res) in enumerate(((sa, ra), (sb, rb))):
        sol_ref[k] = sol[:, 0:8, :]
        res_ref[k] = res[:, 0:8, :]


def near_kernel(r1_ref, perm_ref, wn_ref, halo_ref, near_ref):
    lane = lax.broadcasted_iota(jnp.int32, near_ref.shape[1:], 2)
    last = halo_ref.shape[1] - 1
    for c in range(7):
        head = tile_of(c, 0, r1_ref, perm_ref, wn_ref, halo_ref)
        tail = pltpu.roll(tile_of(c, last, r1_ref, perm_ref, wn_ref, halo_ref), 116, axis=2)
        near_ref[c] = jnp.where(lane < 56, head, jnp.where((lane >= 60) & (lane < 116), tail, 0.0))


def final_kernel(near_ref, sol_in_ref, res_in_ref, pair_ref, other_ref, sol_ref, res_ref):
    planes = near_ref.shape[1]
    last = sol_ref.shape[3] // 128 - 1
    lane = lax.broadcasted_iota(jnp.int32, (planes, 16, 128), 2)
    even = lax.rem(lax.axis_index("gy"), 2) == 0
    pair, other = pair_ref[...], other_ref[...]
    from_right = jnp.where(even, pair, other)
    from_left = jnp.where(even, other, pair)
    from_right = jnp.stack([pltpu.roll(from_right, (-16 * p) % 128, axis=1) for p in range(planes)])
    from_left = jnp.stack([pltpu.roll(from_left, (112 - 16 * p) % 128, axis=1) for p in range(planes)])
    fields = []
    for c in range(7):
        offset, width = COL_PLACE[c]
        right = (lane >= 116) & (lane < 116 + width)
        field = jnp.where(right, pltpu.roll(from_right, 116 - offset, axis=2), near_ref[c])
        field = jnp.where(lane >= 128 - width, pltpu.roll(from_left, offset, axis=2), field)
        fields.append(field)
    sa, sb, ra, rb = iterate(*fields)
    near = lane[:, 0:8, :]
    for k, (sol, res) in enumerate(((sa, ra), (sb, rb))):
        for out_ref, in_ref, value in ((sol_ref, sol_in_ref, sol), (res_ref, res_in_ref, res)):
            value = value[:, 0:8, :]
            for t in range(last + 1):
                lanes = slice(t * 128, (t + 1) * 128)
                tile = in_ref[k, :, :, lanes]
                if t == 0:
                    tile = jnp.where(near < 8, value, tile)
                if t == last:
                    tile = jnp.where(near >= 120, pltpu.roll(value, 12, axis=2), tile)
                out_ref[k, :, :, lanes] = tile


def in_vmem(n):
    return [pl.BlockSpec(memory_space=pltpu.VMEM)] * n


def shape(*dims):
    return jax.ShapeDtypeStruct(dims, f32)


def per_device(rhs_field, permittivity, surf_dist, surf_normal, surf_inc, surf_cell, surf_mask, surf_owner):
    planes, rows, cols = permittivity.shape
    blocks, points = surf_cell.shape
    gx, gy = lax.axis_size("gx"), lax.axis_size("gy")
    devices = gx * gy
    slots = devices * CAP
    params = pltpu.CompilerParams(vmem_limit_bytes=48 << 20)
    send = pl.pallas_call(
        pack_kernel,
        out_shape=shape(slots * CHANNELS, points),
        in_specs=[pl.BlockSpec(memory_space=pltpu.HBM)] * 6,
        out_specs=pl.BlockSpec(memory_space=pltpu.VMEM),
        scratch_shapes=[
            pltpu.SMEM((blocks,), jnp.int32),
            pltpu.SMEM((devices,), jnp.int32),
            pltpu.VMEM((blocks, points), f32),
            pltpu.VMEM((CHANNELS - 1, blocks, points), f32),
            pltpu.VMEM((8 * blocks, points), f32),
            pltpu.VMEM((blocks, points), jnp.int32),
            pltpu.VMEM((blocks, points), jnp.int32),
            pltpu.SemaphoreType.DMA((6,)),
        ],
        compiler_params=params,
        name="pack",
    )(*[
        pltpu.with_memory_space_constraint(x, pltpu.HBM)
        for x in (surf_owner[:, 0], surf_dist, surf_normal, surf_inc, surf_cell, surf_mask)
    ])
    recv = lax.all_to_all(send.reshape(-1), ("gx", "gy"), split_axis=0, concat_axis=0, tiled=True)
    recv = recv.reshape(slots * CHANNELS, points)
    cells = planes * rows
    rhs_field = rhs_field.reshape(2, cells, cols)
    permittivity = permittivity.reshape(cells, cols)

    tiles = cols // 128

    def cost(parts):
        flops = 2 * parts * cols * slots * points
        return pl.CostEstimate(flops=flops, transcendentals=0, bytes_accessed=slots * CHANNELS * points * 4)

    strip = shape(13 * planes, cols)
    parts = 24 * planes + 14 * planes
    local = shape(slots, points)
    kept, edges, pair, other, hi, lo = pl.pallas_call(
        first_kernel,
        out_shape=(shape(2, tiles, cells, 128), shape(4, 2 * planes, cols), strip, strip, local, local),
        in_specs=in_vmem(3),
        out_specs=tuple(in_vmem(6)),
        scratch_shapes=[pltpu.VMEM((parts, cols), f32), pltpu.VMEM((3, tiles, cells, 128), f32)],
        compiler_params=params,
        cost_estimate=cost(parts),
        name="first",
    )(recv, rhs_field, permittivity)
    from_other = lax.ppermute(other, "gx", [(i, (((i + 1) ^ 1) - 1) % gx) for i in range(gx)])
    from_pair = lax.ppermute(pair, "gx", [(i, i ^ 1) for i in range(gx)])
    parts = 7 * 6 * planes + 4 * 2 * planes
    r1, wn = pl.pallas_call(
        second_kernel,
        out_shape=(shape(2, cells, cols), shape(4, tiles, cells, 128)),
        in_specs=in_vmem(5),
        out_specs=tuple(in_vmem(2)),
        scratch_shapes=[pltpu.VMEM((parts, cols), f32), pltpu.VMEM((2, tiles, cells, 128), f32)],
        compiler_params=params,
        cost_estimate=cost(parts),
        name="second",
    )(recv, hi, lo, kept, edges)
    pair, other, halo = pl.pallas_call(
        strip_kernel,
        out_shape=(shape(16, 128), shape(16, 128), shape(7, tiles, cells, 128)),
        in_specs=in_vmem(5),
        out_specs=tuple(in_vmem(3)),
        compiler_params=params,
        name="strips",
    )(r1, permittivity, wn, from_pair, from_other)
    from_other = lax.ppermute(other, "gy", [(i, (((i + 1) ^ 1) - 1) % gy) for i in range(gy)])
    field = shape(2, planes, rows, cols)
    sol, res, pair = pl.pallas_call(
        inner_kernel,
        out_shape=(field, field, shape(16, 128)),
        in_specs=in_vmem(5),
        out_specs=tuple(in_vmem(3)),
        compiler_params=params,
        cost_estimate=cost(8 * planes),
        name="inner",
    )(r1, permittivity, wn, halo, pair)
    near = pl.pallas_call(
        near_kernel,
        out_shape=shape(7, planes, 16, 128),
        in_specs=in_vmem(4),
        out_specs=in_vmem(1)[0],
        compiler_params=params,
        cost_estimate=cost(8 * planes),
        name="near",
    )(r1, permittivity, wn, halo)
    from_pair = lax.ppermute(pair, "gy", [(i, i ^ 1) for i in range(gy)])
    return pl.pallas_call(
        final_kernel,
        out_shape=(field, field),
        in_specs=in_vmem(5),
        out_specs=tuple(in_vmem(2)),
        compiler_params=params,
        name="final",
    )(near, sol, res, from_pair, from_other)


def solution(mesh):
    split = ("gx", "gy")
    placed = (
        P(None, None, "gx", "gy"),
        P(None, "gx", "gy"),
        P(split, None),
        P(None, split, None),
        P(None, split, None),
        P(split, None),
        P(split, None),
        P(split, None),
    )
    return jax.shard_map(
        per_device,
        mesh=mesh,
        in_specs=placed,
        out_specs=(P(None, None, "gx", "gy"), P(None, None, "gx", "gy")),
        check_vma=False,
    )
```
